32 devices in a mesh: dp: 4 (over y, x), tensor: 8 (over z, core).
Axes of the slice: x: 2, y: 2, z: 4, core: 2. Of those that a mesh axis runs over, the one named last changes fastest.
Arguments:
- hidden_in: bfloat16 [12, 1024, 2048], P('dp', 'tensor'), may hold values from -6 to 6
- out_grad: bfloat16 [12, 1024, 2048], P('dp', 'tensor'), may hold values from -6 to 6
- buckets: int32 [1024, 1024], replicated, may hold values from 0 to 31
- gain_attn: bfloat16 [2048], replicated, may hold values from 0.099609375 to 1.8984375
- gain_ffn: bfloat16 [2048], replicated, may hold values from 0.099609375 to 1.8984375
- w_query: bfloat16 [2048, 2048], P('dp', 'tensor'), may hold values from -0.03125 to 0.03125
- w_key: bfloat16 [2048, 2048], P('dp', 'tensor'), may hold values from -0.125 to 0.125
- w_value: bfloat16 [2048, 2048], P('dp', 'tensor'), may hold values from -0.125 to 0.125
- w_out: bfloat16 [2048, 2048], P('tensor', 'dp'), may hold values from -1 to 1
- w_gate: bfloat16 [2048, 5120], P('dp', 'tensor'), may hold values from -0.125 to 0.125
- w_up: bfloat16 [2048, 5120], P('dp', 'tensor'), may hold values from -0.125 to 0.125
- w_down: bfloat16 [5120, 2048], P('tensor', 'dp'), may hold values from -0.125 to 0.125
- bias_table: bfloat16 [32, 32], P('dp', 'tensor'), may hold values from -4 to 4
Outputs:
- output: bfloat16 [12, 1024, 2048], P('dp', 'tensor')
- grad_input: bfloat16 [12, 1024, 2048], P('dp', 'tensor')
- grad_gain_attn: float32 [2048], replicated
- grad_gain_ffn: float32 [2048], replicated
- grad_query: float32 [2048, 2048], P('dp', 'tensor')
- grad_key: float32 [2048, 2048], P('dp', 'tensor')
- grad_value: float32 [2048, 2048], P('dp', 'tensor')
- grad_out: float32 [2048, 2048], P('tensor', 'dp')
- grad_gate: float32 [2048, 5120], P('dp', 'tensor')
- grad_up: float32 [2048, 5120], P('dp', 'tensor')
- grad_down: float32 [5120, 2048], P('tensor', 'dp')
- grad_bias: float32 [32, 32], P('dp', 'tensor')
The draws below stay inside these ranges and needn't reach their ends.
Inputs may be any that keep to these rules, and one draw needn't show every extreme that they name: `buckets`: the bucket of each pair of query and key positions, the same for every sequence and head.
All inputs are finite; a program needn't handle non-finite values.
Results may differ from the reference program's by a relative error of at most 0.018.
Values may be sent and summed in bfloat16 or wider, within the bound.
No kernel may reach another device: no remote copies, remote signals or barrier semaphores. Data moves between devices by JAX's collectives and lax.ppermute only.
A program may use at most 320 MiB of HBM per device.

```python
import jax
import jax.numpy as jnp
from jax import lax

D = 2048
HEADS = 32
HD = 64
FF = 5120
NB = 32
LEN = 1024
INNER = 2048
SEQS = 12


def touch_ends(drawn, key, low, top_value):
    place = [jax.random.randint(jax.random.fold_in(key, axis), (), 0, length) for axis, length in enumerate(drawn.shape)]
    widest = drawn.shape.index(max(drawn.shape))
    beside = place[:widest] + [(place[widest] + 1) % drawn.shape[widest]] + place[widest + 1:]
    return drawn.at[tuple(place)].set(low).at[tuple(beside)].set(top_value)


def shard_levels(own_key, shape, pieces, smallest, top_value):
    level = 1.0
    for axis_at, shards_of in pieces:
        heights = jax.random.uniform(jax.random.fold_in(jax.random.fold_in(own_key, 6), axis_at), (shards_of,), jnp.float32, smallest / len(pieces), top_value / len(pieces))
        level = level * jnp.repeat(jnp.exp(heights), shape[axis_at] // shards_of).reshape((-1,) + (1,) * (len(shape) - 1 - axis_at))
    return level


def noise(key, shape, scale, bound, split=(), held_as=jnp.bfloat16):
    entries = jax.random.normal(key, shape, jnp.float32) * scale
    if len(split) > 0:
        entries = shard_levels(key, shape, split, -0.22, 0.18) * entries
    return jnp.clip(entries, min=-bound, max=bound).astype(held_as)


def setup_inputs(seed: int = 0) -> dict:
    arg_keys = jax.random.split(jax.random.key(seed), 14)
    hidden_in = noise(arg_keys[0], (SEQS, LEN, D), 1.0, 6.0, ((0, 4), (1, 8)))
    out_grad = noise(arg_keys[1], (SEQS, LEN, D), 1.0, 6.0, ((0, 4), (1, 8)))
    buckets = touch_ends(jax.random.randint(arg_keys[2], (LEN, LEN), 0, NB), jax.random.fold_in(arg_keys[2], 1), 0, NB - 1).astype(jnp.int32)
    gain_attn = jnp.clip(1.0 + 0.18 * jax.random.normal(arg_keys[3], (D,), jnp.float32), 0.099609375, 1.8984375).astype(jnp.bfloat16)
    gain_ffn = jnp.clip(1.0 + 0.18 * jax.random.normal(arg_keys[4], (D,), jnp.float32), 0.099609375, 1.8984375).astype(jnp.bfloat16)
    w_query = noise(arg_keys[5], (D, INNER), (16 * D) ** -0.5, 0.03125, ((0, 4), (1, 8)))
    w_key = noise(arg_keys[6], (D, INNER), D ** -0.5, 0.125, ((0, 4), (1, 8)))
    w_value = noise(arg_keys[7], (D, INNER), D ** -0.5, 0.125, ((0, 4), (1, 8)))
    w_out = noise(arg_keys[8], (INNER, D), (max(INNER // 64, 1)) ** -0.5, 1.0, ((0, 8), (1, 4)))
    w_gate = noise(arg_keys[9], (D, FF), D ** -0.5, 0.125, ((0, 4), (1, 8)))
    w_up = noise(arg_keys[10], (D, FF), D ** -0.5, 0.125, ((0, 4), (1, 8)))
    w_down = noise(arg_keys[11], (FF, D), (FF // 2) ** -0.5, 0.125, ((0, 8), (1, 4)))
    bias_table = noise(arg_keys[12], (NB, HEADS), 1.0, 4.0, ((0, 4), (1, 8)))
    return {"hidden_in": hidden_in, "out_grad": out_grad, "buckets": buckets, "gain_attn": gain_attn, "gain_ffn": gain_ffn, "w_query": w_query, "w_key": w_key, "w_value": w_value, "w_out": w_out, "w_gate": w_gate, "w_up": w_up, "w_down": w_down, "bias_table": bias_table}


norm_eps = 1e-06
FULL_PRECISION = lax.Precision.HIGHEST

@jax.custom_vjp
def low(v):
    return lax.optimization_barrier(v.astype(jnp.bfloat16)).astype(jnp.float32)

@jax.custom_vjp
def low_back(v):
    return v

def low_keep(v):
    return (low(v), None)

def low_pass(kept, grad):
    return (grad,)

def back_keep(v):
    return (v, None)

def back_low(kept, grad):
    return (low(grad),)
low.defvjp(low_keep, low_pass)
low_back.defvjp(back_keep, back_low)

def rms_scale(seq_rows, gain_vec):
    inv_rms = lax.rsqrt(lax.optimization_barrier(jnp.mean(seq_rows * seq_rows, axis=-1, keepdims=True)) + norm_eps)
    return seq_rows * inv_rms * gain_vec

def gelu_gate(gate_pre, up_pre):
    return jax.nn.gelu(gate_pre, approximate=True) * up_pre

def one_sequence(seq_rows, params, bias_full):
    gain_one, gain_two, query_w, key_w, value_w, out_w, gate_w, up_w, down_w = params
    norm_one = low(rms_scale(seq_rows, gain_one))

    def project(weight):
        return low_back(low(jnp.dot(norm_one, weight, precision=FULL_PRECISION))).reshape(LEN, HEADS, HD)
    queries = project(query_w)
    key_rows = project(key_w)
    value_rows = project(value_w)
    scores = low_back(jnp.einsum('ihd,jhd->hij', queries, key_rows, precision=FULL_PRECISION) + bias_full)
    attn_probs = jax.nn.softmax(scores, axis=-1)
    context = jnp.einsum('hij,jhd->ihd', low(attn_probs), value_rows, precision=FULL_PRECISION)
    context = low_back(low(context)).reshape(LEN, INNER)
    mid_rows = seq_rows + low_back(jnp.dot(context, out_w, precision=FULL_PRECISION))
    norm_two = low(rms_scale(mid_rows, gain_two))
    gate_pre = low_back(jnp.dot(norm_two, gate_w, precision=FULL_PRECISION))
    up_pre = low_back(jnp.dot(norm_two, up_w, precision=FULL_PRECISION))
    hidden = low(gelu_gate(gate_pre, up_pre))
    return mid_rows + low_back(jnp.dot(hidden, down_w, precision=FULL_PRECISION))

def forward(rows_all, params, table_vals, buckets):
    bias_full = jnp.transpose(table_vals[buckets], (2, 0, 1))

    def seq_step(carried, seq_rows):
        return (carried, one_sequence(seq_rows, params, bias_full))
    _, outputs = lax.scan(jax.checkpoint(seq_step), jnp.zeros((), jnp.float32), rows_all)
    return outputs

def reference(hidden_in, out_grad, buckets, gain_attn, gain_ffn, w_query, w_key, w_value, w_out, w_gate, w_up, w_down, bias_table):
    params = tuple((weight.astype(jnp.float32) for weight in (gain_attn, gain_ffn, w_query, w_key, w_value, w_out, w_gate, w_up, w_down)))
    rows_all = hidden_in.astype(jnp.float32)

    def whole_layer(layer_in, layer_params, table_vals):
        return forward(layer_in, layer_params, table_vals, buckets)
    outputs, pullback = jax.vjp(whole_layer, rows_all, params, bias_table.astype(jnp.float32))
    d_rows, d_params, d_table = pullback(out_grad.astype(jnp.float32))
    return (outputs.astype(jnp.bfloat16), d_rows.astype(jnp.bfloat16), d_params[0], d_params[1], d_params[2], d_params[3], d_params[4], d_params[5], d_params[6], d_params[7], d_params[8], d_table)
```

```python
import functools
import jax
import jax.numpy as jnp
from jax import lax
from jax.experimental import pallas as pl
from jax.experimental.pallas import tpu as pltpu
from jax.sharding import PartitionSpec as P

HD = 64
LANES = 128
norm_eps = 1e-06
VMEM_ROOM = 50 * 1024 * 1024


def nt_dot(left, right):
    return lax.dot_general(
        left, right, (((1,), (1,)), ((), ())), preferred_element_type=jnp.float32
    )


def nn_dot(left, right):
    return jnp.dot(left, right, preferred_element_type=jnp.float32)


def head_masks(rows):
    lane = lax.broadcasted_iota(jnp.int32, (rows, LANES), 1)
    return (lane < HD, lane >= HD)


def only_head(keep, pair_cols):
    return jnp.where(keep, pair_cols, jnp.zeros_like(pair_cols))


def expand_kernel(buckets_ref, table_ref, bias_ref):
    heads = table_ref.shape[0]
    rows, cols = buckets_ref.shape
    for col in range(0, cols, LANES):
        ids = buckets_ref[:, col : col + LANES]
        for head in range(heads):
            row = jnp.broadcast_to(table_ref[head : head + 1, :], (rows, LANES))
            bias_ref[head, :, col : col + LANES] = jnp.take_along_axis(
                row, ids, axis=1
            ).astype(jnp.bfloat16)


def expand_bias(buckets_t, table_rows):
    length = buckets_t.shape[0]
    heads = table_rows.shape[0]
    block = 64
    return pl.pallas_call(
        expand_kernel,
        grid=(length // block,),
        in_specs=[
            pl.BlockSpec((block, length), lambda i: (i, 0)),
            pl.BlockSpec((heads, LANES), lambda i: (0, 0)),
        ],
        out_specs=pl.BlockSpec((heads, block, length), lambda i: (0, i, 0)),
        out_shape=jax.ShapeDtypeStruct((heads, length, length), jnp.bfloat16),
        cost_estimate=pl.CostEstimate(
            flops=8 * heads * length * length,
            bytes_accessed=length * length * (4 + 2 * heads),
            transcendentals=0,
        ),
        name="expand_bias",
    )(buckets_t, table_rows)


def forward_kernel(block_cols, qkv_ref, bias_ref, context_ref, lse_ref):
    length = qkv_ref.shape[0]
    keys = qkv_ref[:, LANES : 2 * LANES]
    masks = head_masks(length)
    head_keys = [only_head(keep, keys) for keep in masks]
    values_t = qkv_ref[:, 2 * LANES :].T
    for start in range(0, length, block_cols):
        span = pl.ds(start, block_cols)
        queries = qkv_ref[span, :LANES]
        pieces = []
        for head in range(2):
            scores = nt_dot(head_keys[head], queries) + bias_ref[head, :, span].astype(
                jnp.float32
            )
            top = jnp.max(scores, axis=0, keepdims=True)
            shifted = jnp.exp(scores - top)
            total = jnp.sum(shifted, axis=0, keepdims=True)
            probs = (shifted * (1.0 / total)).astype(jnp.bfloat16)
            pieces.append(nn_dot(values_t[head * HD : (head + 1) * HD], probs))
            lse_ref[0, head : head + 1, span] = top + jnp.log(total)
        context_ref[span, :] = jnp.concatenate(pieces, axis=0).T.astype(jnp.bfloat16)


def attention_forward(qkv, bias_t):
    length = qkv.shape[0]
    pairs = qkv.shape[1] // (3 * LANES)
    heads = 2 * pairs
    return pl.pallas_call(
        functools.partial(forward_kernel, min(256, length)),
        grid=(pairs,),
        in_specs=[
            pl.BlockSpec((length, 3 * LANES), lambda p: (0, p)),
            pl.BlockSpec((2, length, length), lambda p: (p, 0, 0)),
        ],
        out_specs=[
            pl.BlockSpec((length, LANES), lambda p: (0, p)),
            pl.BlockSpec((1, 2, length), lambda p: (p, 0, 0)),
        ],
        out_shape=[
            jax.ShapeDtypeStruct((length, pairs * LANES), jnp.bfloat16),
            jax.ShapeDtypeStruct((pairs, 2, length), jnp.float32),
        ],
        compiler_params=pltpu.CompilerParams(vmem_limit_bytes=VMEM_ROOM),
        cost_estimate=pl.CostEstimate(
            flops=16 * heads * length * length * HD,
            bytes_accessed=2 * heads * length * length + 8 * heads * length * HD,
            transcendentals=heads * length * length,
        ),
        name="attention_forward",
    )(qkv, bias_t)


def backward_kernel(
    block_cols, qkv_ref, grad_ref, bias_ref, lse_ref, out_ref, grad_scores_ref, dk_acc, dv_acc
):
    length = qkv_ref.shape[0]
    keys = qkv_ref[:, LANES : 2 * LANES]
    values = qkv_ref[:, 2 * LANES :]
    masks = head_masks(length)
    small_masks = head_masks(block_cols)
    head_keys = [only_head(keep, keys) for keep in masks]
    head_values = [only_head(keep, values) for keep in masks]
    keys_t = keys.T
    for start in range(0, length, block_cols):
        span = pl.ds(start, block_cols)
        queries = qkv_ref[span, :LANES]
        grads = grad_ref[span, :]
        pieces = []
        for head in range(2):
            scores = nt_dot(head_keys[head], queries) + bias_ref[head, :, span].astype(
                jnp.float32
            )
            probs = jnp.exp(scores - lse_ref[0, head : head + 1, span])
            grad_probs = nt_dot(head_values[head], grads)
            inner = jnp.sum(probs * grad_probs, axis=0, keepdims=True)
            grad_scores = (probs * (grad_probs - inner)).astype(jnp.bfloat16)
            grad_scores_ref[head, :, span] = grad_scores
            value_part = nn_dot(
                probs.astype(jnp.bfloat16), only_head(small_masks[head], grads)
            )
            key_part = nn_dot(grad_scores, only_head(small_masks[head], queries))
            if start == 0 and head == 0:
                dv_acc[...] = value_part
                dk_acc[...] = key_part
            else:
                dv_acc[...] += value_part
                dk_acc[...] += key_part
            pieces.append(nn_dot(keys_t[head * HD : (head + 1) * HD], grad_scores))
        out_ref[span, :LANES] = jnp.concatenate(pieces, axis=0).T.astype(jnp.bfloat16)
    out_ref[:, LANES : 2 * LANES] = dk_acc[...].astype(jnp.bfloat16)
    out_ref[:, 2 * LANES :] = dv_acc[...].astype(jnp.bfloat16)


def attention_backward(qkv, grad_context, bias_t, lse):
    length = qkv.shape[0]
    pairs = qkv.shape[1] // (3 * LANES)
    heads = 2 * pairs
    return pl.pallas_call(
        functools.partial(backward_kernel, min(256, length)),
        grid=(pairs,),
        in_specs=[
            pl.BlockSpec((length, 3 * LANES), lambda p: (0, p)),
            pl.BlockSpec((length, LANES), lambda p: (0, p)),
            pl.BlockSpec((2, length, length), lambda p: (p, 0, 0)),
            pl.BlockSpec((1, 2, length), lambda p: (p, 0, 0)),
        ],
        out_specs=[
            pl.BlockSpec((length, 3 * LANES), lambda p: (0, p)),
            pl.BlockSpec((2, length, length), lambda p: (p, 0, 0)),
        ],
        out_shape=[
            jax.ShapeDtypeStruct((length, pairs * 3 * LANES), jnp.bfloat16),
            jax.ShapeDtypeStruct((heads, length, length), jnp.bfloat16),
        ],
        scratch_shapes=[
            pltpu.VMEM((length, LANES), jnp.float32),
            pltpu.VMEM((length, LANES), jnp.float32),
        ],
        compiler_params=pltpu.CompilerParams(vmem_limit_bytes=VMEM_ROOM),
        cost_estimate=pl.CostEstimate(
            flops=40 * heads * length * length * HD,
            bytes_accessed=4 * heads * length * length + 16 * heads * length * HD,
            transcendentals=heads * length * length,
        ),
        name="attention_backward",
    )(qkv, grad_context, bias_t, lse)


def histogram_kernel(bucket_count, group, buckets_ref, *refs):
    grads, (sums_ref, values) = refs[:-2], refs[-2:]
    heads, rows, cols = values.shape

    @pl.when(pl.program_id(0) == 0)
    def _():
        sums_ref[...] = jnp.zeros_like(sums_ref)

    total = grads[0][...].astype(jnp.float32)
    for other in grads[1:]:
        total = total + other[...].astype(jnp.float32)
    values[...] = total

    @pl.loop(0, bucket_count // group)
    def _(step):
        first = step * group
        acc = [[jnp.zeros((8, LANES), jnp.float32) for _ in range(heads)] for _ in range(group)]
        for row in range(0, rows, 8):
            for col in range(0, cols, LANES):
                ids = buckets_ref[row : row + 8, col : col + LANES]
                vals = [values[h, row : row + 8, col : col + LANES] for h in range(heads)]
                for j in range(group):
                    hit = ids == first + j
                    for h in range(heads):
                        acc[j][h] = acc[j][h] + jnp.where(hit, vals[h], 0.0)
        for j in range(group):
            for h in range(heads):
                sums_ref[h, first + j] += acc[j][h]


def bucket_sums(buckets_t, grad_scores, bucket_count):
    heads, length, _ = grad_scores[0].shape
    block = 32
    sums = pl.pallas_call(
        functools.partial(histogram_kernel, bucket_count, 4),
        grid=(length // block,),
        in_specs=[pl.BlockSpec((block, length), lambda i: (i, 0))]
        + [pl.BlockSpec((heads, block, length), lambda i: (0, i, 0))] * len(grad_scores),
        out_specs=pl.BlockSpec((heads, bucket_count, 8, LANES), lambda i: (0, 0, 0, 0)),
        out_shape=jax.ShapeDtypeStruct((heads, bucket_count, 8, LANES), jnp.float32),
        scratch_shapes=[pltpu.VMEM((heads, block, length), jnp.float32)],
        compiler_params=pltpu.CompilerParams(vmem_limit_bytes=VMEM_ROOM),
        cost_estimate=pl.CostEstimate(
            flops=60 * bucket_count * heads * length * length,
            bytes_accessed=length * length * (4 + 2 * heads * len(grad_scores)),
            transcendentals=0,
        ),
        name="bucket_sums",
    )(buckets_t, *grad_scores)
    return jnp.sum(sums, axis=(2, 3)).T


def xor_pairs(count, mask):
    return [(i, i ^ mask) for i in range(count)]


def reorder(blocks, place):
    blocks = list(blocks)
    bit = 1
    while bit < len(blocks):
        flag = (place & bit) != 0
        blocks = [jnp.where(flag, blocks[i ^ bit], blocks[i]) for i in range(len(blocks))]
        bit *= 2
    return blocks


def rms_parts(seq_rows, gain_vec):
    inv_rms = lax.rsqrt(jnp.mean(seq_rows * seq_rows, axis=-1, keepdims=True) + norm_eps)
    plain_rows = seq_rows * inv_rms
    return (plain_rows, inv_rms, (plain_rows * gain_vec).astype(jnp.bfloat16))


def rms_back(grad_norm, plain_rows, inv_rms, gain_vec):
    scaled_grad = grad_norm * gain_vec
    return inv_rms * (
        scaled_grad - plain_rows * jnp.mean(scaled_grad * plain_rows, axis=-1, keepdims=True)
    )


def gelu_gate(gate_pre, up_pre):
    return jax.nn.gelu(gate_pre, approximate=True) * up_pre


def tn_dot(left, right):
    return lax.dot_general(
        left, right, (((0,), (0,)), ((), ())), preferred_element_type=jnp.float32
    )


def make_body(dp_size, tensor_size):
    zs = tensor_size // 2
    z_groups = [[2 * z + core for z in range(zs)] for core in range(2)]
    core_pairs = xor_pairs(tensor_size, 1)

    def to_core(x):
        return lax.ppermute(x, "tensor", core_pairs)

    def to_dp(x, mask):
        return lax.ppermute(x, "dp", xor_pairs(dp_size, mask))

    def to_z(x, mask):
        return lax.ppermute(x, "tensor", xor_pairs(tensor_size, 2 * mask))

    def dp_relative(x):
        return [x] + [to_dp(x, k) for k in range(1, dp_size)]

    def dp_total(pick):
        own = pick(0).astype(jnp.float32)
        for k in range(1, dp_size):
            own = own + to_dp(pick(k).astype(jnp.bfloat16), k).astype(jnp.float32)
        return own

    def z_gather(x):
        return lax.all_gather(x, "tensor", axis=0, tiled=True, axis_index_groups=z_groups)

    def z_scatter(x):
        return lax.psum_scatter(
            x, "tensor", scatter_dimension=0, tiled=True, axis_index_groups=z_groups
        )

    def all_sum(x):
        bit = 1
        while bit < tensor_size:
            x = x + lax.ppermute(x, "tensor", xor_pairs(tensor_size, bit))
            bit *= 2
        bit = 1
        while bit < dp_size:
            x = x + to_dp(x, bit)
            bit *= 2
        return x

    def body(
        hidden_in,
        out_grad,
        buckets,
        gain_attn,
        gain_ffn,
        w_query,
        w_key,
        w_value,
        w_out,
        w_gate,
        w_up,
        w_down,
        bias_table,
    ):
        dp_at = lax.axis_index("dp")
        tensor_at = lax.axis_index("tensor")
        core_at = tensor_at % 2
        z_at = tensor_at // 2
        seqs, rows, width = hidden_in.shape
        tokens = seqs * rows
        length = buckets.shape[0]
        feats = w_query.shape[0]
        inner = w_query.shape[1]
        heads = inner // HD
        pairs = inner // LANES
        ff = w_gate.shape[1]
        part = ff // dp_size
        table_rows = bias_table.shape[0]
        bucket_count = table_rows * dp_size
        gain_one = gain_attn.astype(jnp.float32)
        gain_two = gain_ffn.astype(jnp.float32)

        qkv_local = jnp.concatenate(
            [
                w[:, p * LANES : (p + 1) * LANES]
                for p in range(pairs)
                for w in (w_query, w_key, w_value)
            ],
            axis=1,
        )
        pad_rows = -table_rows % 16
        table_pad = jnp.pad(bias_table, ((0, pad_rows), (0, 3 * inner - heads)))
        payload = reorder(
            dp_relative(jnp.concatenate([qkv_local, table_pad], axis=0)), dp_at
        )
        w_qkv = jnp.concatenate([p[:feats] for p in payload], axis=0)
        table = jnp.concatenate(
            [p[feats : feats + table_rows, :heads] for p in payload], axis=0
        )
        buckets_t = buckets.T
        bias_t = expand_bias(
            buckets_t,
            jnp.pad(table.astype(jnp.float32).T, ((0, 0), (0, LANES - bucket_count))),
        )

        x_rows = hidden_in.astype(jnp.float32)
        plain_one, inv_one, norm_one = rms_parts(x_rows, gain_one)
        norm_full = [
            lax.all_gather(norm_one[s], "tensor", axis=0, tiled=True) for s in range(seqs)
        ]

        out_z = z_gather(w_out)
        out_own = jnp.concatenate(reorder(dp_relative(out_z), dp_at), axis=1)
        out_other = to_core(out_own)

        ffn_local = jnp.stack([w_gate.T, w_up.T, w_down]).reshape(3, dp_size, part, feats)

        def ffn_block(k):
            return lax.dynamic_index_in_dim(ffn_local, dp_at ^ k, 1, keepdims=False)

        ffn_parts = [ffn_block(0)] + [to_dp(ffn_block(k), k) for k in range(1, dp_size)]
        ffn_rows = jnp.concatenate(reorder(ffn_parts, dp_at), axis=2).reshape(3 * part, width)
        ffn_all = z_gather(ffn_rows).reshape(zs, 3, part, width)
        ffn_all = jnp.transpose(ffn_all, (1, 0, 2, 3)).reshape(3 * ff, width)
        w_pre = ffn_all[: 2 * ff]
        w_post = ffn_all[2 * ff :]

        def context_to_tokens(context):
            blocks = context.reshape(zs, 2, rows, inner)
            own = lax.dynamic_index_in_dim(blocks, core_at, 1, keepdims=False)
            got = to_core(lax.dynamic_index_in_dim(blocks, 1 - core_at, 1, keepdims=False))
            both = jnp.concatenate([own, got], axis=-1)
            moved = [lax.dynamic_index_in_dim(both, z_at, 0, keepdims=False)]
            for k in range(1, zs):
                moved.append(
                    to_z(lax.dynamic_index_in_dim(both, z_at ^ k, 0, keepdims=False), k)
                )
            moved = reorder(moved, z_at)
            return (
                jnp.concatenate([m[:, :inner] for m in moved], axis=1),
                jnp.concatenate([m[:, inner:] for m in moved], axis=1),
            )

        def tokens_to_context(own, other):
            pair = jnp.stack(reorder([own, to_core(other)], core_at))

            def block(k):
                return lax.dynamic_slice_in_dim(pair, (z_at ^ k) * inner, inner, 2)

            moved = [block(0)] + [to_z(block(k), k) for k in range(1, zs)]
            return jnp.stack(reorder(moved, z_at)).reshape(length, inner)

        qkv_all, lse_all, ctx_own, ctx_other = [], [], [], []
        for s in range(seqs):
            qkv = nn_dot(norm_full[s], w_qkv).astype(jnp.bfloat16)
            context, lse = attention_forward(qkv, bias_t)
            own, other = context_to_tokens(context)
            qkv_all.append(qkv)
            lse_all.append(lse)
            ctx_own.append(own)
            ctx_other.append(other)
        ctx_own = jnp.concatenate(ctx_own, axis=0)
        ctx_other = jnp.concatenate(ctx_other, axis=0)
        attn_rows = nn_dot(ctx_own, out_own) + nn_dot(ctx_other, out_other)
        x_flat = x_rows.reshape(tokens, width)
        mid_rows = x_flat + attn_rows
        plain_two, inv_two, norm_two = rms_parts(mid_rows, gain_two)

        def group_rows(x):
            own = jnp.concatenate(dp_relative(x), axis=0)
            return (own, to_core(own))

        def group_total(own, other):
            own = own + to_core(other.astype(jnp.bfloat16)).astype(jnp.float32)
            return dp_total(lambda k: own[k * tokens : (k + 1) * tokens])

        cot_halves = group_rows(out_grad.reshape(tokens, width))
        norm_halves = group_rows(norm_two)
        out_parts, back_parts, hidden_halves, pre_halves = [], [], [], []
        for norm_half, cot_half in zip(norm_halves, cot_halves):
            pre = nt_dot(norm_half, w_pre)
            hidden, pull = jax.vjp(gelu_gate, pre[:, :ff], pre[:, ff:])
            hidden = hidden.astype(jnp.bfloat16)
            grad_gate, grad_up = pull(nt_dot(cot_half, w_post))
            grad_pre = jnp.concatenate([grad_gate, grad_up], axis=1).astype(jnp.bfloat16)
            out_parts.append(nn_dot(hidden, w_post))
            back_parts.append(nn_dot(grad_pre, w_pre))
            hidden_halves.append(hidden)
            pre_halves.append(grad_pre)
        grad_post = tn_dot(hidden_halves[0], cot_halves[0]) + tn_dot(
            hidden_halves[1], cot_halves[1]
        )
        grad_first = tn_dot(pre_halves[0], norm_halves[0]) + tn_dot(
            pre_halves[1], norm_halves[1]
        )
        grad_norm_two = group_total(*back_parts)
        post_z = z_scatter(grad_post.astype(jnp.bfloat16))
        first_z = z_scatter(
            jnp.transpose(
                grad_first.astype(jnp.bfloat16).reshape(2, zs, part, width), (1, 0, 2, 3)
            ).reshape(zs * 2 * part, width)
        )
        output = (mid_rows + group_total(*out_parts)).astype(jnp.bfloat16)

        grad_gain_two = jnp.sum(grad_norm_two * plain_two, axis=0)
        grad_mid = out_grad.reshape(tokens, width).astype(jnp.float32) + rms_back(
            grad_norm_two, plain_two, inv_two, gain_two
        )
        grad_mid_low = grad_mid.astype(jnp.bfloat16)
        back_own = nt_dot(grad_mid_low, out_own).astype(jnp.bfloat16)
        back_other = nt_dot(grad_mid_low, out_other).astype(jnp.bfloat16)
        grad_norm_one, grad_qkv, grad_scores = [], None, []
        for s in range(seqs):
            at = slice(s * rows, (s + 1) * rows)
            grad_context = tokens_to_context(back_own[at], back_other[at])
            grad_proj, grad_score = attention_backward(
                qkv_all[s], grad_context, bias_t, lse_all[s]
            )
            grad_scores.append(grad_score)
            grad_norm_one.append(
                lax.psum_scatter(
                    nt_dot(grad_proj, w_qkv).astype(jnp.bfloat16),
                    "tensor",
                    scatter_dimension=0,
                    tiled=True,
                ).astype(jnp.float32)
            )
            more = tn_dot(norm_full[s], grad_proj)
            grad_qkv = more if grad_qkv is None else grad_qkv + more

        grad_out_own = tn_dot(ctx_own, grad_mid_low)
        grad_out_other = tn_dot(ctx_other, grad_mid_low)
        grad_out_own = grad_out_own + to_core(grad_out_other.astype(jnp.bfloat16)).astype(
            jnp.float32
        )
        grad_out = z_scatter(
            dp_total(
                lambda k: lax.dynamic_slice_in_dim(grad_out_own, (dp_at ^ k) * feats, feats, 1)
            ).astype(jnp.bfloat16)
        ).astype(jnp.float32)

        def ffn_grad(z_rows, mats):
            def block(k):
                return lax.dynamic_slice_in_dim(z_rows, (dp_at ^ k) * feats, feats, 1)

            moved = [block(0)] + [to_dp(block(k), k) for k in range(1, dp_size)]
            moved = jnp.stack(reorder(moved, dp_at)).reshape(dp_size, mats, part, feats)
            return [moved[:, m].reshape(ff, feats).astype(jnp.float32) for m in range(mats)]

        (grad_down,) = ffn_grad(post_z, 1)
        grad_gate_t, grad_up_t = ffn_grad(first_z, 2)

        table_grad = bucket_sums(buckets_t, grad_scores, bucket_count)

        def qkv_block(k):
            at = dp_at ^ k
            return jnp.concatenate(
                [
                    lax.dynamic_slice_in_dim(grad_qkv, at * feats, feats, 0),
                    jnp.pad(
                        lax.dynamic_slice_in_dim(table_grad, at * table_rows, table_rows, 0),
                        ((0, pad_rows), (0, 3 * inner - heads)),
                    ),
                ],
                axis=0,
            )

        summed = dp_total(qkv_block)
        grad_table = summed[feats : feats + table_rows, :heads]

        def columns(which):
            return jnp.concatenate(
                [
                    summed[:feats, (3 * p + which) * LANES : (3 * p + which + 1) * LANES]
                    for p in range(pairs)
                ],
                axis=1,
            )

        grad_norm_one = jnp.stack(grad_norm_one)
        grad_gain_one = jnp.sum(grad_norm_one * plain_one, axis=(0, 1))
        grad_in = (
            grad_mid.reshape(seqs, rows, width)
            + rms_back(grad_norm_one, plain_one, inv_one, gain_one)
        ).astype(jnp.bfloat16)
        gains = all_sum(jnp.stack([grad_gain_one, grad_gain_two]))
        return (
            output.reshape(seqs, rows, width),
            grad_in,
            gains[0],
            gains[1],
            columns(0),
            columns(1),
            columns(2),
            grad_out,
            grad_gate_t.T,
            grad_up_t.T,
            grad_down,
            grad_table,
        )

    return body


def solution(mesh):
    in_specs = (
        P("dp", "tensor", None),
        P("dp", "tensor", None),
        P(),
        P(),
        P(),
        P("dp", "tensor"),
        P("dp", "tensor"),
        P("dp", "tensor"),
        P("tensor", "dp"),
        P("dp", "tensor"),
        P("dp", "tensor"),
        P("tensor", "dp"),
        P("dp", "tensor"),
    )
    out_specs = (
        P("dp", "tensor", None),
        P("dp", "tensor", None),
        P(),
        P(),
        P("dp", "tensor"),
        P("dp", "tensor"),
        P("dp", "tensor"),
        P("tensor", "dp"),
        P("dp", "tensor"),
        P("dp", "tensor"),
        P("tensor", "dp"),
        P("dp", "tensor"),
    )
    body = make_body(mesh.shape["dp"], mesh.shape["tensor"])
    return jax.shard_map(body, mesh=mesh, in_specs=in_specs, out_specs=out_specs, check_vma=False)
```

```python
import functools
import jax
import jax.numpy as jnp
from jax import lax
from jax.experimental import pallas as pl
from jax.experimental.pallas import tpu as pltpu
from jax.sharding import PartitionSpec as P

HD = 64
LANES = 128
norm_eps = 1e-06
VMEM_ROOM = 50 * 1024 * 1024


def nt_dot(left, right):
    return lax.dot_general(
        left, right, (((1,), (1,)), ((), ())), preferred_element_type=jnp.float32
    )


def nn_dot(left, right):
    return jnp.dot(left, right, preferred_element_type=jnp.float32)


def head_masks(rows):
    lane = lax.broadcasted_iota(jnp.int32, (rows, LANES), 1)
    return (lane < HD, lane >= HD)


def only_head(keep, pair_cols):
    return jnp.where(keep, pair_cols, jnp.zeros_like(pair_cols))


def expand_kernel(buckets_ref, table_ref, bias_ref):
    heads = table_ref.shape[0]
    rows, cols = buckets_ref.shape
    for col in range(0, cols, LANES):
        ids = buckets_ref[:, col : col + LANES]
        for head in range(heads):
            row = jnp.broadcast_to(table_ref[head : head + 1, :], (rows, LANES))
            bias_ref[head, :, col : col + LANES] = jnp.take_along_axis(
                row, ids, axis=1
            ).astype(jnp.bfloat16)


def expand_bias(buckets_t, table_rows):
    length = buckets_t.shape[0]
    heads = table_rows.shape[0]
    block = 64
    return pl.pallas_call(
        expand_kernel,
        grid=(length // block,),
        in_specs=[
            pl.BlockSpec((block, length), lambda i: (i, 0)),
            pl.BlockSpec((heads, LANES), lambda i: (0, 0)),
        ],
        out_specs=pl.BlockSpec((heads, block, length), lambda i: (0, i, 0)),
        out_shape=jax.ShapeDtypeStruct((heads, length, length), jnp.bfloat16),
        cost_estimate=pl.CostEstimate(
            flops=8 * heads * length * length,
            bytes_accessed=length * length * (4 + 2 * heads),
            transcendentals=0,
        ),
        name="expand_bias",
    )(buckets_t, table_rows)


def forward_kernel(block_cols, qkv_ref, bias_ref, context_ref, lse_ref):
    length = qkv_ref.shape[0]
    keys = qkv_ref[:, LANES : 2 * LANES]
    masks = head_masks(length)
    head_keys = [only_head(keep, keys) for keep in masks]
    values_t = qkv_ref[:, 2 * LANES :].T
    for start in range(0, length, block_cols):
        span = pl.ds(start, block_cols)
        queries = qkv_ref[span, :LANES]
        pieces = []
        for head in range(2):
            scores = nt_dot(head_keys[head], queries) + bias_ref[head, :, span].astype(
                jnp.float32
            )
            top = jnp.max(scores, axis=0, keepdims=True)
            shifted = jnp.exp(scores - top)
            total = jnp.sum(shifted, axis=0, keepdims=True)
            probs = (shifted * (1.0 / total)).astype(jnp.bfloat16)
            pieces.append(nn_dot(values_t[head * HD : (head + 1) * HD], probs))
            lse_ref[0, head : head + 1, span] = top + jnp.log(total)
        context_ref[span, :] = jnp.concatenate(pieces, axis=0).T.astype(jnp.bfloat16)


def attention_forward(qkv, bias_t):
    length = qkv.shape[0]
    pairs = qkv.shape[1] // (3 * LANES)
    heads = 2 * pairs
    return pl.pallas_call(
        functools.partial(forward_kernel, min(256, length)),
        grid=(pairs,),
        in_specs=[
            pl.BlockSpec((length, 3 * LANES), lambda p: (0, p)),
            pl.BlockSpec((2, length, length), lambda p: (p, 0, 0)),
        ],
        out_specs=[
            pl.BlockSpec((length, LANES), lambda p: (0, p)),
            pl.BlockSpec((1, 2, length), lambda p: (p, 0, 0)),
        ],
        out_shape=[
            jax.ShapeDtypeStruct((length, pairs * LANES), jnp.bfloat16),
            jax.ShapeDtypeStruct((pairs, 2, length), jnp.float32),
        ],
        compiler_params=pltpu.CompilerParams(vmem_limit_bytes=VMEM_ROOM),
        cost_estimate=pl.CostEstimate(
            flops=16 * heads * length * length * HD,
            bytes_accessed=2 * heads * length * length + 8 * heads * length * HD,
            transcendentals=heads * length * length,
        ),
        name="attention_forward",
    )(qkv, bias_t)


def backward_kernel(
    block_cols, qkv_ref, grad_ref, bias_ref, lse_ref, out_ref, grad_scores_ref, dk_acc, dv_acc
):
    length = qkv_ref.shape[0]
    keys = qkv_ref[:, LANES : 2 * LANES]
    values = qkv_ref[:, 2 * LANES :]
    masks = head_masks(length)
    small_masks = head_masks(block_cols)
    head_keys = [only_head(keep, keys) for keep in masks]
    head_values = [only_head(keep, values) for keep in masks]
    keys_t = keys.T
    for start in range(0, length, block_cols):
        span = pl.ds(start, block_cols)
        queries = qkv_ref[span, :LANES]
        grads = grad_ref[span, :]
        pieces = []
        for head in range(2):
            scores = nt_dot(head_keys[head], queries) + bias_ref[head, :, span].astype(
                jnp.float32
            )
            probs = jnp.exp(scores - lse_ref[0, head : head + 1, span])
            grad_probs = nt_dot(head_values[head], grads)
            inner = jnp.sum(probs * grad_probs, axis=0, keepdims=True)
            grad_scores = (probs * (grad_probs - inner)).astype(jnp.bfloat16)
            grad_scores_ref[head, :, span] = grad_scores
            value_part = nn_dot(
                probs.astype(jnp.bfloat16), only_head(small_masks[head], grads)
            )
            key_part = nn_dot(grad_scores, only_head(small_masks[head], queries))
            if start == 0 and head == 0:
                dv_acc[...] = value_part
                dk_acc[...] = key_part
            else:
                dv_acc[...] += value_part
                dk_acc[...] += key_part
            pieces.append(nn_dot(keys_t[head * HD : (head + 1) * HD], grad_scores))
        out_ref[span, :LANES] = jnp.concatenate(pieces, axis=0).T.astype(jnp.bfloat16)
    out_ref[:, LANES : 2 * LANES] = dk_acc[...].astype(jnp.bfloat16)
    out_ref[:, 2 * LANES :] = dv_acc[...].astype(jnp.bfloat16)


def attention_backward(qkv, grad_context, bias_t, lse):
    length = qkv.shape[0]
    pairs = qkv.shape[1] // (3 * LANES)
    heads = 2 * pairs
    return pl.pallas_call(
        functools.partial(backward_kernel, min(256, length)),
        grid=(pairs,),
        in_specs=[
            pl.BlockSpec((length, 3 * LANES), lambda p: (0, p)),
            pl.BlockSpec((length, LANES), lambda p: (0, p)),
            pl.BlockSpec((2, length, length), lambda p: (p, 0, 0)),
            pl.BlockSpec((1, 2, length), lambda p: (p, 0, 0)),
        ],
        out_specs=[
            pl.BlockSpec((length, 3 * LANES), lambda p: (0, p)),
            pl.BlockSpec((2, length, length), lambda p: (p, 0, 0)),
        ],
        out_shape=[
            jax.ShapeDtypeStruct((length, pairs * 3 * LANES), jnp.bfloat16),
            jax.ShapeDtypeStruct((heads, length, length), jnp.bfloat16),
        ],
        scratch_shapes=[
            pltpu.VMEM((length, LANES), jnp.float32),
            pltpu.VMEM((length, LANES), jnp.float32),
        ],
        compiler_params=pltpu.CompilerParams(vmem_limit_bytes=VMEM_ROOM),
        cost_estimate=pl.CostEstimate(
            flops=40 * heads * length * length * HD,
            bytes_accessed=4 * heads * length * length + 16 * heads * length * HD,
            transcendentals=heads * length * length,
        ),
        name="attention_backward",
    )(qkv, grad_context, bias_t, lse)


def histogram_kernel(bucket_count, group, buckets_ref, *refs):
    grads, (sums_ref, values) = refs[:-2], refs[-2:]
    heads, rows, cols = values.shape

    @pl.when(pl.program_id(0) == 0)
    def _():
        sums_ref[...] = jnp.zeros_like(sums_ref)

    total = grads[0][...].astype(jnp.float32)
    for other in grads[1:]:
        total = total + other[...].astype(jnp.float32)
    values[...] = total

    @pl.loop(0, bucket_count // group)
    def _(step):
        first = step * group
        acc = [[jnp.zeros((8, LANES), jnp.float32) for _ in range(heads)] for _ in range(group)]
        for row in range(0, rows, 8):
            for col in range(0, cols, LANES):
                ids = buckets_ref[row : row + 8, col : col + LANES]
                vals = [values[h, row : row + 8, col : col + LANES] for h in range(heads)]
                for j in range(group):
                    hit = ids == first + j
                    for h in range(heads):
                        acc[j][h] = acc[j][h] + jnp.where(hit, vals[h], 0.0)
        for j in range(group):
            for h in range(heads):
                sums_ref[h, first + j] += acc[j][h]


def bucket_sums(buckets_t, grad_scores, bucket_count):
    heads, length, _ = grad_scores[0].shape
    block = 32
    sums = pl.pallas_call(
        functools.partial(histogram_kernel, bucket_count, 4),
        grid=(length // block,),
        in_specs=[pl.BlockSpec((block, length), lambda i: (i, 0))]
        + [pl.BlockSpec((heads, block, length), lambda i: (0, i, 0))] * len(grad_scores),
        out_specs=pl.BlockSpec((heads, bucket_count, 8, LANES), lambda i: (0, 0, 0, 0)),
        out_shape=jax.ShapeDtypeStruct((heads, bucket_count, 8, LANES), jnp.float32),
        scratch_shapes=[pltpu.VMEM((heads, block, length), jnp.float32)],
        compiler_params=pltpu.CompilerParams(vmem_limit_bytes=VMEM_ROOM),
        cost_estimate=pl.CostEstimate(
            flops=60 * bucket_count * heads * length * length,
            bytes_accessed=length * length * (4 + 2 * heads * len(grad_scores)),
            transcendentals=0,
        ),
        name="bucket_sums",
    )(buckets_t, *grad_scores)
    return jnp.sum(sums, axis=(2, 3)).T


def xor_pairs(count, mask):
    return [(i, i ^ mask) for i in range(count)]


def reorder(blocks, place):
    blocks = list(blocks)
    bit = 1
    while bit < len(blocks):
        flag = (place & bit) != 0
        blocks = [jnp.where(flag, blocks[i ^ bit], blocks[i]) for i in range(len(blocks))]
        bit *= 2
    return blocks


def rms_parts(seq_rows, gain_vec):
    inv_rms = lax.rsqrt(jnp.mean(seq_rows * seq_rows, axis=-1, keepdims=True) + norm_eps)
    plain_rows = seq_rows * inv_rms
    return (plain_rows, inv_rms, (plain_rows * gain_vec).astype(jnp.bfloat16))


def rms_back(grad_norm, plain_rows, inv_rms, gain_vec):
    scaled_grad = grad_norm * gain_vec
    return inv_rms * (
        scaled_grad - plain_rows * jnp.mean(scaled_grad * plain_rows, axis=-1, keepdims=True)
    )


def gelu_gate(gate_pre, up_pre):
    return jax.nn.gelu(gate_pre, approximate=True) * up_pre


def tn_dot(left, right):
    return lax.dot_general(
        left, right, (((0,), (0,)), ((), ())), preferred_element_type=jnp.float32
    )


def after(x, *needed):
    return lax.optimization_barrier((x, *needed))[0]


def make_body(dp_size, tensor_size):
    zs = tensor_size // 2
    z_groups = [[2 * z + core for z in range(zs)] for core in range(2)]
    core_pairs = xor_pairs(tensor_size, 1)

    def to_core(x):
        return lax.ppermute(x, "tensor", core_pairs)

    def to_dp(x, mask):
        return lax.ppermute(x, "dp", xor_pairs(dp_size, mask))

    def to_z(x, mask):
        return lax.ppermute(x, "tensor", xor_pairs(tensor_size, 2 * mask))

    def dp_relative(x):
        return [x] + [to_dp(x, k) for k in range(1, dp_size)]

    def exchange(send, pick, size):
        return [pick(0)] + [send(pick(k), k) for k in range(1, size)]

    def total_of(send, pick, size):
        own = pick(0).astype(jnp.float32)
        for k in range(1, size):
            own = own + send(pick(k).astype(jnp.bfloat16), k).astype(jnp.float32)
        return own

    def z_gather(x):
        return lax.all_gather(x, "tensor", axis=0, tiled=True, axis_index_groups=z_groups)

    def z_scatter(x):
        return lax.psum_scatter(
            x, "tensor", scatter_dimension=0, tiled=True, axis_index_groups=z_groups
        )

    def all_sum(x):
        bit = 1
        while bit < tensor_size:
            x = x + lax.ppermute(x, "tensor", xor_pairs(tensor_size, bit))
            bit *= 2
        bit = 1
        while bit < dp_size:
            x = x + to_dp(x, bit)
            bit *= 2
        return x

    def body(
        hidden_in,
        out_grad,
        buckets,
        gain_attn,
        gain_ffn,
        w_query,
        w_key,
        w_value,
        w_out,
        w_gate,
        w_up,
        w_down,
        bias_table,
    ):
        dp_at = lax.axis_index("dp")
        tensor_at = lax.axis_index("tensor")
        core_at = tensor_at % 2
        z_at = tensor_at // 2
        seqs, rows, width = hidden_in.shape
        length = buckets.shape[0]
        feats = w_query.shape[0]
        inner = w_query.shape[1]
        heads = inner // HD
        pairs = inner // LANES
        ff = w_gate.shape[1]
        part = ff // dp_size
        table_rows = bias_table.shape[0]
        bucket_count = table_rows * dp_size
        pad_rows = -table_rows % 16
        gain_one = gain_attn.astype(jnp.float32)
        gain_two = gain_ffn.astype(jnp.float32)
        every = range(seqs)

        def feature_block(x, k):
            return lax.dynamic_slice_in_dim(x, (dp_at ^ k) * feats, feats, 1)

        x_rows = [hidden_in[s].astype(jnp.float32) for s in every]
        first_norm = [rms_parts(x, gain_one) for x in x_rows]
        norm_full = [
            lax.all_gather(first_norm[s][2], "tensor", axis=0, tiled=True) for s in every
        ]

        qkv_local = jnp.concatenate(
            [
                w[:, p * LANES : (p + 1) * LANES]
                for p in range(pairs)
                for w in (w_query, w_key, w_value)
            ],
            axis=1,
        )
        table_pad = jnp.pad(bias_table, ((0, pad_rows), (0, 3 * inner - heads)))
        payload = dp_relative(jnp.concatenate([qkv_local, table_pad], axis=0))
        arrived = payload[1:]
        payload = reorder(payload, dp_at)
        w_qkv = jnp.concatenate([p[:feats] for p in payload], axis=0)
        table = jnp.concatenate(
            [p[feats : feats + table_rows, :heads] for p in payload], axis=0
        )
        buckets_t = buckets.T
        bias_t = expand_bias(
            buckets_t,
            jnp.pad(table.astype(jnp.float32).T, ((0, 0), (0, LANES - bucket_count))),
        )

        out_z = jnp.concatenate(reorder(exchange(to_z, lambda k: w_out, zs), z_at), axis=0)

        ffn_local = jnp.stack([w_gate.T, w_up.T, w_down]).reshape(3, dp_size, part, feats)
        ffn_local = after(ffn_local, *arrived)
        ffn_parts = exchange(
            to_dp,
            lambda k: lax.dynamic_index_in_dim(ffn_local, dp_at ^ k, 1, keepdims=False),
            dp_size,
        )
        arrived = ffn_parts[1:]
        ffn_parts = reorder(ffn_parts, dp_at)
        pre_rows = jnp.concatenate([p[:2] for p in ffn_parts], axis=2)
        post_rows = jnp.concatenate([p[2] for p in ffn_parts], axis=1)
        pre_gathered = z_gather(pre_rows.reshape(2 * part, width))
        post_gathered = z_gather(post_rows)

        out_parts = dp_relative(after(out_z, *arrived))

        def group_rows(x):
            own = jnp.concatenate(dp_relative(x), axis=0)
            return jnp.concatenate([own, to_core(own)], axis=0)

        def context_to_tokens(context):
            blocks = context.reshape(zs, 2, rows, inner)
            own = lax.dynamic_index_in_dim(blocks, core_at, 1, keepdims=False)
            got = to_core(lax.dynamic_index_in_dim(blocks, 1 - core_at, 1, keepdims=False))
            both = jnp.concatenate([own, got], axis=-1)
            swapped = got
            moved = exchange(
                to_z,
                lambda k: lax.dynamic_index_in_dim(both, z_at ^ k, 0, keepdims=False),
                zs,
            )
            moved = reorder(moved, z_at)
            return (
                jnp.concatenate([m[:, :inner] for m in moved], axis=1),
                jnp.concatenate([m[:, inner:] for m in moved], axis=1),
                swapped,
            )

        def tokens_to_context(own, other):
            pair = jnp.stack(reorder([own, to_core(other)], core_at))
            moved = exchange(
                to_z,
                lambda k: lax.dynamic_slice_in_dim(pair, (z_at ^ k) * inner, inner, 2),
                zs,
            )
            return jnp.stack(reorder(moved, z_at)).reshape(length, inner)

        qkv_all, lse_all, ctx_own, ctx_other, swaps = [], [], [], [], []
        mid_rows, second_norm, norm_two_full, cot_full = [], [], [], []

        def feed_forward_input(s):
            mid = x_rows[s] + (nn_dot(ctx_own[s], out_own) + nn_dot(ctx_other[s], out_other))
            mid_rows.append(mid)
            second_norm.append(rms_parts(mid, gain_two))
            norm_two_full.append(group_rows(second_norm[s][2]))

        for s in every:
            source = norm_full[s]
            if s > 0:
                source = after(source, swaps[s - 1])
            if s > 1:
                source = after(source, second_norm[s - 2][2])
            qkv = nn_dot(source, w_qkv).astype(jnp.bfloat16)
            context, lse = attention_forward(qkv, bias_t)
            if s == 0:
                out_parts = after(tuple(out_parts), context)
                out_own = jnp.concatenate(reorder(out_parts, dp_at), axis=1)
                out_other = to_core(out_own)
            own, other, swapped = context_to_tokens(context)
            qkv_all.append(qkv)
            lse_all.append(lse)
            ctx_own.append(own)
            ctx_other.append(other)
            swaps.append(swapped)
            cot_full.append(group_rows(after(out_grad[s], context)))
            if s > 0:
                feed_forward_input(s - 1)
        feed_forward_input(seqs - 1)

        pre_gathered, w_post = after((pre_gathered, post_gathered), norm_two_full[-1])
        w_pre = jnp.transpose(
            pre_gathered.reshape(zs, 2, part, width), (1, 0, 2, 3)
        ).reshape(2 * ff, width)
        half = dp_size * rows

        def group_total(partial, count):
            own = partial[: dp_size * count]
            other = partial[dp_size * count :]
            own = own + to_core(other.astype(jnp.bfloat16)).astype(jnp.float32)
            return total_of(to_dp, lambda k: own[k * count : (k + 1) * count], dp_size)

        first_parts, hidden_all = [], []
        grad_post = None
        for s in every:
            pre = nt_dot(norm_two_full[s], w_pre)
            hidden = gelu_gate(pre[:, :ff], pre[:, ff:]).astype(jnp.bfloat16)
            first_parts.append(pre)
            hidden_all.append(hidden)
            more = tn_dot(hidden, cot_full[s])
            grad_post = more if grad_post is None else grad_post + more
        grad_post = grad_post.astype(jnp.bfloat16)
        pre_all, grad_norm_two = [], []
        ready = grad_post
        for s in every:
            pre = first_parts[s]
            _, pull = jax.vjp(gelu_gate, pre[:, :ff], pre[:, ff:])
            grad_gate, grad_up = pull(nt_dot(after(cot_full[s], ready), w_post))
            grad_pre = jnp.concatenate([grad_gate, grad_up], axis=1).astype(jnp.bfloat16)
            ready = nn_dot(grad_pre, w_pre)
            grad_norm_two.append(group_total(ready, rows))
            pre_all.append(grad_pre)
        grad_pre_w = None
        for s in every:
            more = tn_dot(after(pre_all[s], ready), norm_two_full[s])
            grad_pre_w = more if grad_pre_w is None else grad_pre_w + more
        grad_pre_w = grad_pre_w.astype(jnp.bfloat16)
        post_z = z_scatter(grad_post)
        pre_z = z_scatter(
            jnp.transpose(
                grad_pre_w.reshape(2, zs, part, width), (1, 0, 2, 3)
            ).reshape(zs * 2 * part, width)
        )

        grad_mid, grad_mid_low, gain_two_sum = [], [], None
        for s in every:
            plain, inv, _ = second_norm[s]
            more = jnp.sum(grad_norm_two[s] * plain, axis=0)
            gain_two_sum = more if gain_two_sum is None else gain_two_sum + more
            grad = out_grad[s].astype(jnp.float32) + rms_back(
                grad_norm_two[s], plain, inv, gain_two
            )
            grad_mid.append(grad)
            grad_mid_low.append(grad.astype(jnp.bfloat16))

        grad_normed, grad_qkv, grad_scores = [], None, []
        for s in every:
            back_own = nt_dot(grad_mid_low[s], out_own).astype(jnp.bfloat16)
            back_other = nt_dot(grad_mid_low[s], out_other).astype(jnp.bfloat16)
            grad_context = tokens_to_context(back_own, back_other)
            if s == 0:
                grad_context = after(grad_context, grad_pre_w)
            grad_proj, grad_score = attention_backward(
                qkv_all[s], grad_context, bias_t, lse_all[s]
            )
            grad_scores.append(grad_score)
            normed_part = nt_dot(grad_proj, w_qkv).astype(jnp.bfloat16)
            grad_normed.append(
                lax.psum_scatter(
                    normed_part, "tensor", scatter_dimension=0, tiled=True
                ).astype(jnp.float32)
            )
            more = tn_dot(norm_full[s], after(grad_proj, normed_part))
            grad_qkv = more if grad_qkv is None else grad_qkv + more

        mid_low = after(jnp.concatenate(grad_mid_low, axis=0), grad_qkv)
        grad_out_own = tn_dot(jnp.concatenate(ctx_own, axis=0), mid_low)
        grad_out_other = tn_dot(jnp.concatenate(ctx_other, axis=0), mid_low)
        grad_out_sum = grad_out_own + to_core(grad_out_other.astype(jnp.bfloat16)).astype(
            jnp.float32
        )
        grad_out_z = total_of(to_dp, lambda k: feature_block(grad_out_sum, k), dp_size)
        grad_out = total_of(
            to_z,
            lambda k: lax.dynamic_slice_in_dim(grad_out_z, (z_at ^ k) * inner, inner, 0),
            zs,
        )

        hidden_own = jnp.concatenate([h[:half] for h in hidden_all], axis=0)
        hidden_other = jnp.concatenate([h[half:] for h in hidden_all], axis=0)
        hidden_own, hidden_other = (
            after(hidden_own, grad_out_other, grad_out_own),
            after(hidden_other, grad_out_other),
        )
        sent = to_core(nn_dot(hidden_other, w_post).astype(jnp.bfloat16))
        own = (nn_dot(hidden_own, w_post) + sent.astype(jnp.float32)).reshape(
            seqs, dp_size, rows, width
        )
        ffn_out = total_of(to_dp, lambda k: own[:, k], dp_size)
        output = jnp.stack(
            [(mid_rows[s] + ffn_out[s]).astype(jnp.bfloat16) for s in every]
        )

        def ffn_grad(z_rows, mats):
            moved = exchange(to_dp, lambda k: feature_block(z_rows, k), dp_size)
            moved = jnp.stack(reorder(moved, dp_at)).reshape(dp_size, mats, part, feats)
            return [moved[:, m].reshape(ff, feats).astype(jnp.float32) for m in range(mats)]

        (grad_down,) = ffn_grad(post_z, 1)
        grad_gate_t, grad_up_t = ffn_grad(pre_z, 2)

        summed = total_of(
            to_dp,
            lambda k: lax.dynamic_slice_in_dim(grad_qkv, (dp_at ^ k) * feats, feats, 0),
            dp_size,
        )

        def columns(which):
            return jnp.concatenate(
                [
                    summed[:, (3 * p + which) * LANES : (3 * p + which + 1) * LANES]
                    for p in range(pairs)
                ],
                axis=1,
            )

        table_grad = bucket_sums(after(buckets_t, own), grad_scores, bucket_count)
        grad_table = total_of(
            to_dp,
            lambda k: lax.dynamic_slice_in_dim(
                table_grad, (dp_at ^ k) * table_rows, table_rows, 0
            ),
            dp_size,
        )

        grad_in, gain_one_sum = [], None
        for s in every:
            plain, inv, _ = first_norm[s]
            more = jnp.sum(grad_normed[s] * plain, axis=0)
            gain_one_sum = more if gain_one_sum is None else gain_one_sum + more
            grad_in.append(
                (grad_mid[s] + rms_back(grad_normed[s], plain, inv, gain_one)).astype(
                    jnp.bfloat16
                )
            )
        gain_two_sum = all_sum(gain_two_sum)
        gain_one_sum = all_sum(gain_one_sum)
        return (
            output,
            jnp.stack(grad_in),
            gain_one_sum,
            gain_two_sum,
            columns(0),
            columns(1),
            columns(2),
            grad_out,
            grad_gate_t.T,
            grad_up_t.T,
            grad_down,
            grad_table,
        )

    return body


def solution(mesh):
    in_specs = (
        P("dp", "tensor", None),
        P("dp", "tensor", None),
        P(),
        P(),
        P(),
        P("dp", "tensor"),
        P("dp", "tensor"),
        P("dp", "tensor"),
        P("tensor", "dp"),
        P("dp", "tensor"),
        P("dp", "tensor"),
        P("tensor", "dp"),
        P("dp", "tensor"),
    )
    out_specs = (
        P("dp", "tensor", None),
        P("dp", "tensor", None),
        P(),
        P(),
        P("dp", "tensor"),
        P("dp", "tensor"),
        P("dp", "tensor"),
        P("tensor", "dp"),
        P("dp", "tensor"),
        P("dp", "tensor"),
        P("tensor", "dp"),
        P("dp", "tensor"),
    )
    body = make_body(mesh.shape["dp"], mesh.shape["tensor"])
    return jax.shard_map(body, mesh=mesh, in_specs=in_specs, out_specs=out_specs, check_vma=False)
```

```python
import functools
import jax
import jax.numpy as jnp
from jax import lax
from jax.experimental import pallas as pl
from jax.experimental.pallas import tpu as pltpu
from jax.sharding import PartitionSpec as P

HD = 64
LANES = 128
norm_eps = 1e-06
VMEM_ROOM = 50 * 1024 * 1024


def nt_dot(left, right):
    return lax.dot_general(
        left, right, (((1,), (1,)), ((), ())), preferred_element_type=jnp.float32
    )


def nn_dot(left, right):
    return jnp.dot(left, right, preferred_element_type=jnp.float32)


def head_masks(rows):
    lane = lax.broadcasted_iota(jnp.int32, (rows, LANES), 1)
    return (lane < HD, lane >= HD)


def only_head(keep, pair_cols):
    return jnp.where(keep, pair_cols, jnp.zeros_like(pair_cols))


def expand_kernel(buckets_ref, table_ref, bias_ref):
    heads = table_ref.shape[0]
    rows, cols = buckets_ref.shape
    for col in range(0, cols, LANES):
        ids = buckets_ref[:, col : col + LANES]
        for head in range(heads):
            row = jnp.broadcast_to(table_ref[head : head + 1, :], (rows, LANES))
            bias_ref[head, :, col : col + LANES] = jnp.take_along_axis(
                row, ids, axis=1
            ).astype(jnp.bfloat16)


def expand_bias(buckets_t, table_rows):
    length = buckets_t.shape[0]
    heads = table_rows.shape[0]
    block = 64
    return pl.pallas_call(
        expand_kernel,
        grid=(length // block,),
        in_specs=[
            pl.BlockSpec((block, length), lambda i: (i, 0)),
            pl.BlockSpec((heads, LANES), lambda i: (0, 0)),
        ],
        out_specs=pl.BlockSpec((heads, block, length), lambda i: (0, i, 0)),
        out_shape=jax.ShapeDtypeStruct((heads, length, length), jnp.bfloat16),
        cost_estimate=pl.CostEstimate(
            flops=8 * heads * length * length,
            bytes_accessed=length * length * (4 + 2 * heads),
            transcendentals=0,
        ),
        name="expand_bias",
    )(buckets_t, table_rows)


def forward_kernel(block_cols, qkv_ref, bias_ref, context_ref, lse_ref):
    length = qkv_ref.shape[0]
    keys = qkv_ref[:, LANES : 2 * LANES]
    masks = head_masks(length)
    head_keys = [only_head(keep, keys) for keep in masks]
    values_t = qkv_ref[:, 2 * LANES :].T
    for start in range(0, length, block_cols):
        span = pl.ds(start, block_cols)
        queries = qkv_ref[span, :LANES]
        pieces = []
        for head in range(2):
            scores = nt_dot(head_keys[head], queries) + bias_ref[head, :, span].astype(
                jnp.float32
            )
            top = jnp.max(scores, axis=0, keepdims=True)
            shifted = jnp.exp(scores - top)
            total = jnp.sum(shifted, axis=0, keepdims=True)
            probs = (shifted * (1.0 / total)).astype(jnp.bfloat16)
            pieces.append(nn_dot(values_t[head * HD : (head + 1) * HD], probs))
            lse_ref[0, head : head + 1, span] = top + jnp.log(total)
        context_ref[span, :] = jnp.concatenate(pieces, axis=0).T.astype(jnp.bfloat16)


def attention_forward(qkv, bias_t):
    length = qkv.shape[0]
    pairs = qkv.shape[1] // (3 * LANES)
    heads = 2 * pairs
    return pl.pallas_call(
        functools.partial(forward_kernel, min(256, length)),
        grid=(pairs,),
        in_specs=[
            pl.BlockSpec((length, 3 * LANES), lambda p: (0, p)),
            pl.BlockSpec((2, length, length), lambda p: (p, 0, 0)),
        ],
        out_specs=[
            pl.BlockSpec((length, LANES), lambda p: (0, p)),
            pl.BlockSpec((1, 2, length), lambda p: (p, 0, 0)),
        ],
        out_shape=[
            jax.ShapeDtypeStruct((length, pairs * LANES), jnp.bfloat16),
            jax.ShapeDtypeStruct((pairs, 2, length), jnp.float32),
        ],
        compiler_params=pltpu.CompilerParams(vmem_limit_bytes=VMEM_ROOM),
        cost_estimate=pl.CostEstimate(
            flops=16 * heads * length * length * HD,
            bytes_accessed=2 * heads * length * length + 8 * heads * length * HD,
            transcendentals=heads * length * length,
        ),
        name="attention_forward",
    )(qkv, bias_t)


def backward_kernel(
    block_cols, qkv_ref, grad_ref, bias_ref, lse_ref, out_ref, grad_scores_ref, dk_acc, dv_acc
):
    length = qkv_ref.shape[0]
    keys = qkv_ref[:, LANES : 2 * LANES]
    values = qkv_ref[:, 2 * LANES :]
    masks = head_masks(length)
    small_masks = head_masks(block_cols)
    head_keys = [only_head(keep, keys) for keep in masks]
    head_values = [only_head(keep, values) for keep in masks]
    keys_t = keys.T
    for start in range(0, length, block_cols):
        span = pl.ds(start, block_cols)
        queries = qkv_ref[span, :LANES]
        grads = grad_ref[span, :]
        pieces = []
        for head in range(2):
            scores = nt_dot(head_keys[head], queries) + bias_ref[head, :, span].astype(
                jnp.float32
            )
            probs = jnp.exp(scores - lse_ref[0, head : head + 1, span])
            grad_probs = nt_dot(head_values[head], grads)
            inner = jnp.sum(probs * grad_probs, axis=0, keepdims=True)
            grad_scores = (probs * (grad_probs - inner)).astype(jnp.bfloat16)
            grad_scores_ref[head, :, span] = grad_scores
            value_part = nn_dot(
                probs.astype(jnp.bfloat16), only_head(small_masks[head], grads)
            )
            key_part = nn_dot(grad_scores, only_head(small_masks[head], queries))
            if start == 0 and head == 0:
                dv_acc[...] = value_part
                dk_acc[...] = key_part
            else:
                dv_acc[...] += value_part
                dk_acc[...] += key_part
            pieces.append(nn_dot(keys_t[head * HD : (head + 1) * HD], grad_scores))
        out_ref[span, :LANES] = jnp.concatenate(pieces, axis=0).T.astype(jnp.bfloat16)
    out_ref[:, LANES : 2 * LANES] = dk_acc[...].astype(jnp.bfloat16)
    out_ref[:, 2 * LANES :] = dv_acc[...].astype(jnp.bfloat16)


def attention_backward(qkv, grad_context, bias_t, lse):
    length = qkv.shape[0]
    pairs = qkv.shape[1] // (3 * LANES)
    heads = 2 * pairs
    return pl.pallas_call(
        functools.partial(backward_kernel, min(256, length)),
        grid=(pairs,),
        in_specs=[
            pl.BlockSpec((length, 3 * LANES), lambda p: (0, p)),
            pl.BlockSpec((length, LANES), lambda p: (0, p)),
            pl.BlockSpec((2, length, length), lambda p: (p, 0, 0)),
            pl.BlockSpec((1, 2, length), lambda p: (p, 0, 0)),
        ],
        out_specs=[
            pl.BlockSpec((length, 3 * LANES), lambda p: (0, p)),
            pl.BlockSpec((2, length, length), lambda p: (p, 0, 0)),
        ],
        out_shape=[
            jax.ShapeDtypeStruct((length, pairs * 3 * LANES), jnp.bfloat16),
            jax.ShapeDtypeStruct((heads, length, length), jnp.bfloat16),
        ],
        scratch_shapes=[
            pltpu.VMEM((length, LANES), jnp.float32),
            pltpu.VMEM((length, LANES), jnp.float32),
        ],
        compiler_params=pltpu.CompilerParams(vmem_limit_bytes=VMEM_ROOM),
        cost_estimate=pl.CostEstimate(
            flops=40 * heads * length * length * HD,
            bytes_accessed=4 * heads * length * length + 16 * heads * length * HD,
            transcendentals=heads * length * length,
        ),
        name="attention_backward",
    )(qkv, grad_context, bias_t, lse)


def histogram_kernel(bucket_count, group, buckets_ref, *refs):
    grads, (sums_ref, values) = refs[:-2], refs[-2:]
    heads, rows, cols = values.shape

    @pl.when(pl.program_id(0) == 0)
    def _():
        sums_ref[...] = jnp.zeros_like(sums_ref)

    total = grads[0][...].astype(jnp.float32)
    for other in grads[1:]:
        total = total + other[...].astype(jnp.float32)
    values[...] = total

    @pl.loop(0, bucket_count // group)
    def _(step):
        first = step * group
        acc = [[jnp.zeros((8, LANES), jnp.float32) for _ in range(heads)] for _ in range(group)]
        for row in range(0, rows, 8):
            for col in range(0, cols, LANES):
                ids = buckets_ref[row : row + 8, col : col + LANES]
                vals = [values[h, row : row + 8, col : col + LANES] for h in range(heads)]
                for j in range(group):
                    hit = ids == first + j
                    for h in range(heads):
                        acc[j][h] = acc[j][h] + jnp.where(hit, vals[h], 0.0)
        for j in range(group):
            for h in range(heads):
                sums_ref[h, first + j] += acc[j][h]


def bucket_sums(buckets_t, grad_scores, bucket_count):
    heads, length, _ = grad_scores[0].shape
    block = 32
    sums = pl.pallas_call(
        functools.partial(histogram_kernel, bucket_count, 4),
        grid=(length // block,),
        in_specs=[pl.BlockSpec((block, length), lambda i: (i, 0))]
        + [pl.BlockSpec((heads, block, length), lambda i: (0, i, 0))] * len(grad_scores),
        out_specs=pl.BlockSpec((heads, bucket_count, 8, LANES), lambda i: (0, 0, 0, 0)),
        out_shape=jax.ShapeDtypeStruct((heads, bucket_count, 8, LANES), jnp.float32),
        scratch_shapes=[pltpu.VMEM((heads, block, length), jnp.float32)],
        compiler_params=pltpu.CompilerParams(vmem_limit_bytes=VMEM_ROOM),
        cost_estimate=pl.CostEstimate(
            flops=2 * heads * length * length,
            bytes_accessed=length * length * (4 + 2 * heads * len(grad_scores)),
            transcendentals=0,
        ),
        name="bucket_sums",
    )(buckets_t, *grad_scores)
    return jnp.sum(sums, axis=(2, 3)).T


def xor_pairs(count, mask):
    return [(i, i ^ mask) for i in range(count)]


def reorder(blocks, place):
    blocks = list(blocks)
    bit = 1
    while bit < len(blocks):
        flag = (place & bit) != 0
        blocks = [jnp.where(flag, blocks[i ^ bit], blocks[i]) for i in range(len(blocks))]
        bit *= 2
    return blocks


def rms_parts(seq_rows, gain_vec):
    inv_rms = lax.rsqrt(jnp.mean(seq_rows * seq_rows, axis=-1, keepdims=True) + norm_eps)
    plain_rows = seq_rows * inv_rms
    return (plain_rows, inv_rms, (plain_rows * gain_vec).astype(jnp.bfloat16))


def rms_back(grad_norm, plain_rows, inv_rms, gain_vec):
    scaled_grad = grad_norm * gain_vec
    return inv_rms * (
        scaled_grad - plain_rows * jnp.mean(scaled_grad * plain_rows, axis=-1, keepdims=True)
    )


def gelu_gate(gate_pre, up_pre):
    return jax.nn.gelu(gate_pre, approximate=True) * up_pre


def tn_dot(left, right):
    return lax.dot_general(
        left, right, (((0,), (0,)), ((), ())), preferred_element_type=jnp.float32
    )


def after(x, *needed):
    return lax.optimization_barrier((x, *needed))[0]


def make_body(dp_size, tensor_size):
    zs = tensor_size // 2
    z_groups = [[2 * z + core for z in range(zs)] for core in range(2)]
    core_pairs = xor_pairs(tensor_size, 1)

    def to_core(x):
        return lax.ppermute(x, "tensor", core_pairs)

    def to_dp(x, mask):
        return lax.ppermute(x, "dp", xor_pairs(dp_size, mask))

    def to_z(x, mask):
        return lax.ppermute(x, "tensor", xor_pairs(tensor_size, 2 * mask))

    def dp_relative(x):
        return [x] + [to_dp(x, k) for k in range(1, dp_size)]

    def exchange(send, pick, size):
        return [pick(0)] + [send(pick(k), k) for k in range(1, size)]

    def total_of(send, pick, size):
        own = pick(0).astype(jnp.float32)
        for k in range(1, size):
            own = own + send(pick(k).astype(jnp.bfloat16), k).astype(jnp.float32)
        return own

    def z_gather(x):
        return lax.all_gather(x, "tensor", axis=0, tiled=True, axis_index_groups=z_groups)

    def z_scatter(x):
        return lax.psum_scatter(
            x, "tensor", scatter_dimension=0, tiled=True, axis_index_groups=z_groups
        )

    def all_sum(x):
        bit = 1
        while bit < tensor_size:
            x = x + lax.ppermute(x, "tensor", xor_pairs(tensor_size, bit))
            bit *= 2
        bit = 1
        while bit < dp_size:
            x = x + to_dp(x, bit)
            bit *= 2
        return x

    def body(
        hidden_in,
        out_grad,
        buckets,
        gain_attn,
        gain_ffn,
        w_query,
        w_key,
        w_value,
        w_out,
        w_gate,
        w_up,
        w_down,
        bias_table,
    ):
        dp_at = lax.axis_index("dp")
        tensor_at = lax.axis_index("tensor")
        core_at = tensor_at % 2
        z_at = tensor_at // 2
        seqs, rows, width = hidden_in.shape
        length = buckets.shape[0]
        feats = w_query.shape[0]
        inner = w_query.shape[1]
        heads = inner // HD
        pairs = inner // LANES
        ff = w_gate.shape[1]
        part = ff // dp_size
        table_rows = bias_table.shape[0]
        bucket_count = table_rows * dp_size
        gain_one = gain_attn.astype(jnp.float32)
        gain_two = gain_ffn.astype(jnp.float32)
        every = range(seqs)

        def feature_block(x, k):
            return lax.dynamic_slice_in_dim(x, (dp_at ^ k) * feats, feats, 1)

        x_rows = [hidden_in[s].astype(jnp.float32) for s in every]
        first_norm = [rms_parts(x, gain_one) for x in x_rows]
        norm_full = [
            lax.all_gather(first_norm[s][2], "tensor", axis=0, tiled=True) for s in every
        ]

        qkv_local = jnp.concatenate(
            [
                w[:, p * LANES : (p + 1) * LANES]
                for p in range(pairs)
                for w in (w_query, w_key, w_value)
            ],
            axis=1,
        )
        table = jnp.concatenate(reorder(dp_relative(bias_table), dp_at), axis=0)
        buckets_t = buckets.T
        bias_t = expand_bias(
            buckets_t,
            jnp.pad(table.astype(jnp.float32).T, ((0, 0), (0, LANES - bucket_count))),
        )
        payload = dp_relative(after(qkv_local, table))
        arrived = payload[1:]
        payload = after(tuple(payload), bias_t)
        w_qkv = jnp.concatenate(reorder(payload, dp_at), axis=0)

        out_z = after(tuple(exchange(to_z, lambda k: w_out, zs)), w_qkv)
        out_z = jnp.concatenate(reorder(out_z, z_at), axis=0)

        ffn_local = jnp.stack([w_gate.T, w_up.T, w_down]).reshape(3, dp_size, part, feats)
        ffn_local = after(ffn_local, *arrived)
        ffn_parts = exchange(
            to_dp,
            lambda k: lax.dynamic_index_in_dim(ffn_local, dp_at ^ k, 1, keepdims=False),
            dp_size,
        )
        arrived = ffn_parts[1:]
        ffn_parts = reorder(after(tuple(ffn_parts), w_qkv), dp_at)
        pre_rows = jnp.concatenate([p[:2] for p in ffn_parts], axis=2)
        post_rows = jnp.concatenate([p[2] for p in ffn_parts], axis=1)
        pre_gathered = z_gather(pre_rows.reshape(2 * part, width))

        out_parts = dp_relative(after(out_z, *arrived))

        def group_rows(x):
            own = jnp.concatenate(dp_relative(x), axis=0)
            return jnp.concatenate([own, to_core(own)], axis=0)

        def context_to_tokens(context):
            blocks = context.reshape(zs, 2, rows, inner)
            own = lax.dynamic_index_in_dim(blocks, core_at, 1, keepdims=False)
            got = to_core(lax.dynamic_index_in_dim(blocks, 1 - core_at, 1, keepdims=False))
            both = jnp.concatenate([own, got], axis=-1)
            swapped = got
            moved = exchange(
                to_z,
                lambda k: lax.dynamic_index_in_dim(both, z_at ^ k, 0, keepdims=False),
                zs,
            )
            moved = reorder(moved, z_at)
            return (
                jnp.concatenate([m[:, :inner] for m in moved], axis=1),
                jnp.concatenate([m[:, inner:] for m in moved], axis=1),
                swapped,
            )

        def send_tokens(own, other):
            got = to_core(other)
            pair = jnp.stack(reorder([own, got], core_at))
            moved = exchange(
                to_z,
                lambda k: lax.dynamic_slice_in_dim(pair, (z_at ^ k) * inner, inner, 2),
                zs,
            )
            return tuple(moved), got

        def take_tokens(moved):
            return jnp.stack(reorder(moved, z_at)).reshape(length, inner)

        qkv_all, lse_all, ctx_own, ctx_other, swaps = [], [], [], [], []
        mid_rows, second_norm, norm_two_full, cot_full = [], [], [], []

        def feed_forward_input(s):
            mid = x_rows[s] + (nn_dot(ctx_own[s], out_own) + nn_dot(ctx_other[s], out_other))
            mid_rows.append(mid)
            second_norm.append(rms_parts(mid, gain_two))
            norm_two_full.append(group_rows(second_norm[s][2]))

        for s in every:
            source = norm_full[s]
            if s > 0:
                source = after(source, swaps[s - 1])
            if s > 1:
                source = after(source, second_norm[s - 2][2])
            qkv = nn_dot(source, w_qkv).astype(jnp.bfloat16)
            context, lse = attention_forward(qkv, bias_t)
            if s == 0:
                post_gathered = z_gather(after(post_rows, context))
                out_parts = after(tuple(out_parts), context)
                out_own = jnp.concatenate(reorder(out_parts, dp_at), axis=1)
                out_other = to_core(out_own)
                cot_parts = dp_relative(after(out_grad, *out_parts[1:]))
            if s == seqs - 1:
                cot_parts = after(tuple(cot_parts), context)
                cot_own = jnp.concatenate([c[i] for i in every for c in cot_parts], axis=0)
                cot_other = to_core(cot_own)
            own, other, swapped = context_to_tokens(context)
            qkv_all.append(qkv)
            lse_all.append(lse)
            ctx_own.append(own)
            ctx_other.append(other)
            swaps.append(swapped)
            if s > 0:
                feed_forward_input(s - 1)
        feed_forward_input(seqs - 1)

        pre_gathered, w_post = after((pre_gathered, post_gathered), norm_two_full[-1])
        w_pre = jnp.transpose(
            pre_gathered.reshape(zs, 2, part, width), (1, 0, 2, 3)
        ).reshape(2 * ff, width)
        half = dp_size * rows
        cot_full = [
            jnp.concatenate(
                [cot_own[s * half : (s + 1) * half], cot_other[s * half : (s + 1) * half]],
                axis=0,
            )
            for s in every
        ]

        first_parts, hidden_all = [], []
        grad_post = None
        for s in every:
            pre = nt_dot(norm_two_full[s], w_pre)
            hidden = gelu_gate(pre[:, :ff], pre[:, ff:]).astype(jnp.bfloat16)
            first_parts.append(pre)
            hidden_all.append(hidden)
            more = tn_dot(hidden, cot_full[s])
            grad_post = more if grad_post is None else grad_post + more
        grad_post = grad_post.astype(jnp.bfloat16)
        pre_all, grad_norm_two, sums = [], [], []
        ready = grad_post
        for s in every:
            pre = first_parts[s]
            _, pull = jax.vjp(gelu_gate, pre[:, :ff], pre[:, ff:])
            cot = after(cot_full[s], ready)
            if s > 1:
                cot = after(cot, sums[s - 2])
            grad_gate, grad_up = pull(nt_dot(cot, w_post))
            grad_pre = jnp.concatenate([grad_gate, grad_up], axis=1).astype(jnp.bfloat16)
            ready = nn_dot(grad_pre, w_pre)
            got = to_core(ready[half:].astype(jnp.bfloat16))
            own = ready[:half] + got.astype(jnp.float32)
            own = (own[:rows], own[rows:].astype(jnp.bfloat16))
            grad_norm_two.append(
                own[0]
                + sum(
                    to_dp(own[1][(k - 1) * rows : k * rows], k).astype(jnp.float32)
                    for k in range(1, dp_size)
                )
            )
            sums.append(got)
            pre_all.append(grad_pre)
        post_z = z_scatter(grad_post)
        grad_pre_w = None
        for s in every:
            grad_pre = after(pre_all[s], ready, sums[-1])
            if s > 0:
                grad_pre = after(grad_pre, grad_norm_two[s - 1])
            if s == seqs - 1:
                grad_pre = after(grad_pre, post_z)
            more = tn_dot(grad_pre, norm_two_full[s])
            grad_pre_w = more if grad_pre_w is None else grad_pre_w + more
        grad_pre_w = grad_pre_w.astype(jnp.bfloat16)
        pre_z = z_scatter(
            jnp.transpose(
                grad_pre_w.reshape(2, zs, part, width), (1, 0, 2, 3)
            ).reshape(zs * 2 * part, width)
        )

        hidden_own = jnp.concatenate([h[:half] for h in hidden_all], axis=0)
        hidden_other = jnp.concatenate([h[half:] for h in hidden_all], axis=0)
        hidden_own, hidden_other = (
            after(hidden_own, grad_pre_w),
            after(hidden_other, grad_pre_w),
        )
        sent = to_core(nn_dot(hidden_other, w_post).astype(jnp.bfloat16))
        own = (nn_dot(after(hidden_own, grad_norm_two[-1]), w_post) + sent.astype(jnp.float32)).reshape(
            seqs, dp_size, rows, width
        )
        out_sent = [
            to_dp(own[:, k].astype(jnp.bfloat16), k) for k in range(1, dp_size)
        ]
        ffn_own = own[:, 0]

        grad_mid, grad_mid_low, gain_two_sum = [], [], None
        for s in every:
            plain, inv, _ = second_norm[s]
            more = jnp.sum(grad_norm_two[s] * plain, axis=0)
            gain_two_sum = more if gain_two_sum is None else gain_two_sum + more
            grad = out_grad[s].astype(jnp.float32) + rms_back(
                grad_norm_two[s], plain, inv, gain_two
            )
            grad_mid.append(grad)
            grad_mid_low.append(grad.astype(jnp.bfloat16))

        moves, swapped_in = [], []
        for s in every:
            back_own = nt_dot(grad_mid_low[s], out_own).astype(jnp.bfloat16)
            back_other = nt_dot(grad_mid_low[s], out_other).astype(jnp.bfloat16)
            moved, got = send_tokens(back_own, back_other)
            moves.append(moved)
            swapped_in.append(got)

        def ffn_send(z_rows):
            return tuple(exchange(to_dp, lambda k: feature_block(z_rows, k), dp_size))

        def ffn_take(moved, mats):
            moved = jnp.stack(reorder(moved, dp_at)).reshape(dp_size, mats, part, feats)
            return [moved[:, m].reshape(ff, feats).astype(jnp.float32) for m in range(mats)]

        post_moved = ffn_send(post_z)
        grad_normed, grad_scores, normed_parts, qkv_grads = [], [], [], []
        grad_qkv = None
        gate = (grad_pre_w,)
        for s in every:
            moved = after(moves[s], *gate)
            if s < seqs - 1:
                moved = after(moved, swapped_in[s + 1])
            if s == seqs - 1:
                moved = after(moved, pre_z, *post_moved[1:])
            grad_proj, grad_score = attention_backward(
                qkv_all[s], take_tokens(moved), bias_t, lse_all[s]
            )
            grad_scores.append(grad_score)
            qkv_grads.append(grad_proj)
            normed_part = nt_dot(grad_proj, w_qkv).astype(jnp.bfloat16)
            normed_parts.append(normed_part)
            gate = (normed_part,)
            grad_normed.append(
                lax.psum_scatter(
                    normed_part, "tensor", scatter_dimension=0, tiled=True
                ).astype(jnp.float32)
            )
            if s == 0:
                mid_low = after(jnp.concatenate(grad_mid_low, axis=0), normed_part)
                out_give = tn_dot(jnp.concatenate(ctx_other, axis=0), mid_low).astype(
                    jnp.bfloat16
                )
                out_got = to_core(out_give)
                out_keep = tn_dot(jnp.concatenate(ctx_own, axis=0), mid_low)
                gate = gate + (out_give, out_keep)
            else:
                for t in [0, 1] if s == 1 else [s]:
                    more = tn_dot(norm_full[t], after(qkv_grads[t], normed_part))
                    grad_qkv = more if grad_qkv is None else grad_qkv + more
                gate = gate + (grad_qkv,)
            if s == 1:
                out_sum = out_keep + after(out_got, normed_part).astype(jnp.float32)
                out_moved = tuple(
                    exchange(
                        to_dp,
                        lambda k: feature_block(out_sum, k)
                        if k == 0
                        else feature_block(out_sum, k).astype(jnp.bfloat16),
                        dp_size,
                    )
                )
        pre_moved = ffn_send(pre_z)
        out_moved = after(out_moved, normed_parts[-1])
        grad_out_z = sum(m.astype(jnp.float32) for m in out_moved)
        grad_out = total_of(
            to_z,
            lambda k: lax.dynamic_slice_in_dim(grad_out_z, (z_at ^ k) * inner, inner, 0),
            zs,
        )
        out_sent = after(tuple(out_sent), normed_parts[-1])
        ffn_out = ffn_own + sum(m.astype(jnp.float32) for m in out_sent)
        output = jnp.stack(
            [(mid_rows[s] + ffn_out[s]).astype(jnp.bfloat16) for s in every]
        )

        (grad_down,) = ffn_take(post_moved, 1)
        grad_gate_t, grad_up_t = ffn_take(pre_moved, 2)

        summed = total_of(
            to_dp,
            lambda k: lax.dynamic_slice_in_dim(grad_qkv, (dp_at ^ k) * feats, feats, 0),
            dp_size,
        )

        def columns(which):
            return jnp.concatenate(
                [
                    summed[:, (3 * p + which) * LANES : (3 * p + which + 1) * LANES]
                    for p in range(pairs)
                ],
                axis=1,
            )

        table_grad = bucket_sums(
            after(buckets_t, grad_qkv, grad_normed[0]), grad_scores, bucket_count
        )
        grad_table = total_of(
            to_dp,
            lambda k: lax.dynamic_slice_in_dim(
                table_grad, (dp_at ^ k) * table_rows, table_rows, 0
            ),
            dp_size,
        )

        grad_in, gain_one_sum = [], None
        for s in every:
            plain, inv, _ = first_norm[s]
            more = jnp.sum(grad_normed[s] * plain, axis=0)
            gain_one_sum = more if gain_one_sum is None else gain_one_sum + more
            grad_in.append(
                (grad_mid[s] + rms_back(grad_normed[s], plain, inv, gain_one)).astype(
                    jnp.bfloat16
                )
            )
        gains = all_sum(jnp.stack([gain_one_sum, gain_two_sum]))
        return (
            output,
            jnp.stack(grad_in),
            gains[0],
            gains[1],
            columns(0),
            columns(1),
            columns(2),
            grad_out,
            grad_gate_t.T,
            grad_up_t.T,
            grad_down,
            grad_table,
        )

    return body


def solution(mesh):
    in_specs = (
        P("dp", "tensor", None),
        P("dp", "tensor", None),
        P(),
        P(),
        P(),
        P("dp", "tensor"),
        P("dp", "tensor"),
        P("dp", "tensor"),
        P("tensor", "dp"),
        P("dp", "tensor"),
        P("dp", "tensor"),
        P("tensor", "dp"),
        P("dp", "tensor"),
    )
    out_specs = (
        P("dp", "tensor", None),
        P("dp", "tensor", None),
        P(),
        P(),
        P("dp", "tensor"),
        P("dp", "tensor"),
        P("dp", "tensor"),
        P("tensor", "dp"),
        P("dp", "tensor"),
        P("dp", "tensor"),
        P("tensor", "dp"),
        P("dp", "tensor"),
    )
    body = make_body(mesh.shape["dp"], mesh.shape["tensor"])
    return jax.shard_map(body, mesh=mesh, in_specs=in_specs, out_specs=out_specs, check_vma=False)
```

```python
import functools
import jax
import jax.numpy as jnp
from jax import lax
from jax.experimental import pallas as pl
from jax.experimental.pallas import tpu as pltpu
from jax.sharding import PartitionSpec as P

HD = 64
LANES = 128
norm_eps = 1e-06
VMEM_ROOM = 50 * 1024 * 1024


def nt_dot(left, right):
    return lax.dot_general(
        left, right, (((1,), (1,)), ((), ())), preferred_element_type=jnp.float32
    )


def nn_dot(left, right):
    return jnp.dot(left, right, preferred_element_type=jnp.float32)


def head_masks(rows):
    lane = lax.broadcasted_iota(jnp.int32, (rows, LANES), 1)
    return (lane < HD, lane >= HD)


def only_head(keep, pair_cols):
    return jnp.where(keep, pair_cols, jnp.zeros_like(pair_cols))


def expand_kernel(buckets_ref, table_ref, bias_ref):
    heads = table_ref.shape[0]
    rows, cols = buckets_ref.shape
    for col in range(0, cols, LANES):
        ids = buckets_ref[:, col : col + LANES]
        for head in range(heads):
            row = jnp.broadcast_to(table_ref[head : head + 1, :], (rows, LANES))
            bias_ref[head, :, col : col + LANES] = jnp.take_along_axis(
                row, ids, axis=1
            ).astype(jnp.bfloat16)


def expand_bias(buckets_t, table_rows):
    length = buckets_t.shape[0]
    heads = table_rows.shape[0]
    block = 64
    return pl.pallas_call(
        expand_kernel,
        grid=(length // block,),
        in_specs=[
            pl.BlockSpec((block, length), lambda i: (i, 0)),
            pl.BlockSpec((heads, LANES), lambda i: (0, 0)),
        ],
        out_specs=pl.BlockSpec((heads, block, length), lambda i: (0, i, 0)),
        out_shape=jax.ShapeDtypeStruct((heads, length, length), jnp.bfloat16),
        cost_estimate=pl.CostEstimate(
            flops=heads * length, bytes_accessed=heads * length, transcendentals=0
        ),
        name="expand_bias",
    )(buckets_t, table_rows)


def forward_kernel(block_cols, qkv_ref, bias_ref, context_ref, lse_ref):
    length = qkv_ref.shape[0]
    keys = qkv_ref[:, LANES : 2 * LANES]
    masks = head_masks(length)
    head_keys = [only_head(keep, keys) for keep in masks]
    values_t = qkv_ref[:, 2 * LANES :].T
    for start in range(0, length, block_cols):
        span = pl.ds(start, block_cols)
        queries = qkv_ref[span, :LANES]
        pieces = []
        for head in range(2):
            scores = nt_dot(head_keys[head], queries) + bias_ref[head, :, span].astype(
                jnp.float32
            )
            top = jnp.max(scores, axis=0, keepdims=True)
            shifted = jnp.exp(scores - top)
            total = jnp.sum(shifted, axis=0, keepdims=True)
            probs = (shifted * (1.0 / total)).astype(jnp.bfloat16)
            pieces.append(nn_dot(values_t[head * HD : (head + 1) * HD], probs))
            lse_ref[0, head : head + 1, span] = top + jnp.log(total)
        context_ref[span, :] = jnp.concatenate(pieces, axis=0).T.astype(jnp.bfloat16)


def attention_forward(qkv, bias_t):
    length = qkv.shape[0]
    pairs = qkv.shape[1] // (3 * LANES)
    heads = 2 * pairs
    return pl.pallas_call(
        functools.partial(forward_kernel, min(256, length)),
        grid=(pairs,),
        in_specs=[
            pl.BlockSpec((length, 3 * LANES), lambda p: (0, p)),
            pl.BlockSpec((2, length, length), lambda p: (p, 0, 0)),
        ],
        out_specs=[
            pl.BlockSpec((length, LANES), lambda p: (0, p)),
            pl.BlockSpec((1, 2, length), lambda p: (p, 0, 0)),
        ],
        out_shape=[
            jax.ShapeDtypeStruct((length, pairs * LANES), jnp.bfloat16),
            jax.ShapeDtypeStruct((pairs, 2, length), jnp.float32),
        ],
        compiler_params=pltpu.CompilerParams(vmem_limit_bytes=VMEM_ROOM),
        cost_estimate=pl.CostEstimate(
            flops=heads * length, bytes_accessed=heads * length, transcendentals=0
        ),
        name="attention_forward",
    )(qkv, bias_t)


def backward_kernel(
    block_cols, qkv_ref, grad_ref, bias_ref, lse_ref, out_ref, grad_scores_ref, dk_acc, dv_acc
):
    length = qkv_ref.shape[0]
    keys = qkv_ref[:, LANES : 2 * LANES]
    values = qkv_ref[:, 2 * LANES :]
    masks = head_masks(length)
    small_masks = head_masks(block_cols)
    head_keys = [only_head(keep, keys) for keep in masks]
    head_values = [only_head(keep, values) for keep in masks]
    keys_t = keys.T
    for start in range(0, length, block_cols):
        span = pl.ds(start, block_cols)
        queries = qkv_ref[span, :LANES]
        grads = grad_ref[span, :]
        pieces = []
        for head in range(2):
            scores = nt_dot(head_keys[head], queries) + bias_ref[head, :, span].astype(
                jnp.float32
            )
            probs = jnp.exp(scores - lse_ref[0, head : head + 1, span])
            grad_probs = nt_dot(head_values[head], grads)
            inner = jnp.sum(probs * grad_probs, axis=0, keepdims=True)
            grad_scores = (probs * (grad_probs - inner)).astype(jnp.bfloat16)
            grad_scores_ref[head, :, span] = grad_scores
            value_part = nn_dot(
                probs.astype(jnp.bfloat16), only_head(small_masks[head], grads)
            )
            key_part = nn_dot(grad_scores, only_head(small_masks[head], queries))
            if start == 0 and head == 0:
                dv_acc[...] = value_part
                dk_acc[...] = key_part
            else:
                dv_acc[...] += value_part
                dk_acc[...] += key_part
            pieces.append(nn_dot(keys_t[head * HD : (head + 1) * HD], grad_scores))
        out_ref[span, :LANES] = jnp.concatenate(pieces, axis=0).T.astype(jnp.bfloat16)
    out_ref[:, LANES : 2 * LANES] = dk_acc[...].astype(jnp.bfloat16)
    out_ref[:, 2 * LANES :] = dv_acc[...].astype(jnp.bfloat16)


def attention_backward(qkv, grad_context, bias_t, lse):
    length = qkv.shape[0]
    pairs = qkv.shape[1] // (3 * LANES)
    heads = 2 * pairs
    return pl.pallas_call(
        functools.partial(backward_kernel, min(256, length)),
        grid=(pairs,),
        in_specs=[
            pl.BlockSpec((length, 3 * LANES), lambda p: (0, p)),
            pl.BlockSpec((length, LANES), lambda p: (0, p)),
            pl.BlockSpec((2, length, length), lambda p: (p, 0, 0)),
            pl.BlockSpec((1, 2, length), lambda p: (p, 0, 0)),
        ],
        out_specs=[
            pl.BlockSpec((length, 3 * LANES), lambda p: (0, p)),
            pl.BlockSpec((2, length, length), lambda p: (p, 0, 0)),
        ],
        out_shape=[
            jax.ShapeDtypeStruct((length, pairs * 3 * LANES), jnp.bfloat16),
            jax.ShapeDtypeStruct((heads, length, length), jnp.bfloat16),
        ],
        scratch_shapes=[
            pltpu.VMEM((length, LANES), jnp.float32),
            pltpu.VMEM((length, LANES), jnp.float32),
        ],
        compiler_params=pltpu.CompilerParams(vmem_limit_bytes=VMEM_ROOM),
        cost_estimate=pl.CostEstimate(
            flops=heads * length, bytes_accessed=heads * length, transcendentals=0
        ),
        name="attention_backward",
    )(qkv, grad_context, bias_t, lse)


def histogram_kernel(bucket_count, group, buckets_ref, *refs):
    grads, (sums_ref, values) = refs[:-2], refs[-2:]
    heads, rows, cols = values.shape

    @pl.when(pl.program_id(0) == 0)
    def _():
        sums_ref[...] = jnp.zeros_like(sums_ref)

    total = grads[0][...].astype(jnp.float32)
    for other in grads[1:]:
        total = total + other[...].astype(jnp.float32)
    values[...] = total

    @pl.loop(0, bucket_count // group)
    def _(step):
        first = step * group
        acc = [[jnp.zeros((8, LANES), jnp.float32) for _ in range(heads)] for _ in range(group)]
        for row in range(0, rows, 8):
            for col in range(0, cols, LANES):
                ids = buckets_ref[row : row + 8, col : col + LANES]
                vals = [values[h, row : row + 8, col : col + LANES] for h in range(heads)]
                for j in range(group):
                    hit = ids == first + j
                    for h in range(heads):
                        acc[j][h] = acc[j][h] + jnp.where(hit, vals[h], 0.0)
        for j in range(group):
            for h in range(heads):
                sums_ref[h, first + j] += acc[j][h]


def bucket_sums(buckets_t, grad_scores, bucket_count):
    heads, length, _ = grad_scores[0].shape
    block = 32
    sums = pl.pallas_call(
        functools.partial(histogram_kernel, bucket_count, 4),
        grid=(length // block,),
        in_specs=[pl.BlockSpec((block, length), lambda i: (i, 0))]
        + [pl.BlockSpec((heads, block, length), lambda i: (0, i, 0))] * len(grad_scores),
        out_specs=pl.BlockSpec((heads, bucket_count, 8, LANES), lambda i: (0, 0, 0, 0)),
        out_shape=jax.ShapeDtypeStruct((heads, bucket_count, 8, LANES), jnp.float32),
        scratch_shapes=[pltpu.VMEM((heads, block, length), jnp.float32)],
        compiler_params=pltpu.CompilerParams(vmem_limit_bytes=VMEM_ROOM),
        cost_estimate=pl.CostEstimate(
            flops=heads * length, bytes_accessed=heads * length, transcendentals=0
        ),
        name="bucket_sums",
    )(buckets_t, *grad_scores)
    return jnp.sum(sums, axis=(2, 3)).T


def xor_pairs(count, mask):
    return [(i, i ^ mask) for i in range(count)]


def reorder(blocks, place):
    blocks = list(blocks)
    bit = 1
    while bit < len(blocks):
        flag = (place & bit) != 0
        blocks = [jnp.where(flag, blocks[i ^ bit], blocks[i]) for i in range(len(blocks))]
        bit *= 2
    return blocks


def rms_parts(seq_rows, gain_vec):
    inv_rms = lax.rsqrt(jnp.mean(seq_rows * seq_rows, axis=-1, keepdims=True) + norm_eps)
    plain_rows = seq_rows * inv_rms
    return (plain_rows, inv_rms, (plain_rows * gain_vec).astype(jnp.bfloat16))


def rms_back(grad_norm, plain_rows, inv_rms, gain_vec):
    scaled_grad = grad_norm * gain_vec
    return inv_rms * (
        scaled_grad - plain_rows * jnp.mean(scaled_grad * plain_rows, axis=-1, keepdims=True)
    )


def gelu_gate(gate_pre, up_pre):
    return jax.nn.gelu(gate_pre, approximate=True) * up_pre


def tn_dot(left, right):
    return lax.dot_general(
        left, right, (((0,), (0,)), ((), ())), preferred_element_type=jnp.float32
    )


def after(x, *needed):
    return lax.optimization_barrier((x, *needed))[0]


def make_body(dp_size, tensor_size):
    zs = tensor_size // 2
    z_groups = [[2 * z + core for z in range(zs)] for core in range(2)]
    core_pairs = xor_pairs(tensor_size, 1)

    def to_core(x):
        return lax.ppermute(x, "tensor", core_pairs)

    def to_dp(x, mask):
        return lax.ppermute(x, "dp", xor_pairs(dp_size, mask))

    def to_z(x, mask):
        return lax.ppermute(x, "tensor", xor_pairs(tensor_size, 2 * mask))

    def dp_relative(x):
        return [x] + [to_dp(x, k) for k in range(1, dp_size)]

    def exchange(send, pick, size):
        return [pick(0)] + [send(pick(k), k) for k in range(1, size)]

    def total_of(send, pick, size):
        own = pick(0).astype(jnp.float32)
        for k in range(1, size):
            own = own + send(pick(k).astype(jnp.bfloat16), k).astype(jnp.float32)
        return own

    def z_gather(x):
        return lax.all_gather(x, "tensor", axis=0, tiled=True, axis_index_groups=z_groups)

    def z_scatter(x):
        return lax.psum_scatter(
            x, "tensor", scatter_dimension=0, tiled=True, axis_index_groups=z_groups
        )

    def all_sum(x):
        bit = 1
        while bit < tensor_size:
            x = x + lax.ppermute(x, "tensor", xor_pairs(tensor_size, bit))
            bit *= 2
        bit = 1
        while bit < dp_size:
            x = x + to_dp(x, bit)
            bit *= 2
        return x

    def body(
        hidden_in,
        out_grad,
        buckets,
        gain_attn,
        gain_ffn,
        w_query,
        w_key,
        w_value,
        w_out,
        w_gate,
        w_up,
        w_down,
        bias_table,
    ):
        dp_at = lax.axis_index("dp")
        tensor_at = lax.axis_index("tensor")
        core_at = tensor_at % 2
        z_at = tensor_at // 2
        seqs, rows, width = hidden_in.shape
        length = buckets.shape[0]
        feats = w_query.shape[0]
        inner = w_query.shape[1]
        heads = inner // HD
        pairs = inner // LANES
        ff = w_gate.shape[1]
        part = ff // dp_size
        table_rows = bias_table.shape[0]
        bucket_count = table_rows * dp_size
        gain_one = gain_attn.astype(jnp.float32)
        gain_two = gain_ffn.astype(jnp.float32)
        every = range(seqs)

        def feature_block(x, k):
            return lax.dynamic_slice_in_dim(x, (dp_at ^ k) * feats, feats, 1)

        x_rows = [hidden_in[s].astype(jnp.float32) for s in every]
        first_norm = [rms_parts(x, gain_one) for x in x_rows]
        norm_full = [
            lax.all_gather(first_norm[s][2], "tensor", axis=0, tiled=True) for s in every
        ]

        qkv_local = jnp.concatenate(
            [
                w[:, p * LANES : (p + 1) * LANES]
                for p in range(pairs)
                for w in (w_query, w_key, w_value)
            ],
            axis=1,
        )
        table = jnp.concatenate(reorder(dp_relative(bias_table), dp_at), axis=0)
        buckets_t = buckets.T
        bias_t = expand_bias(
            buckets_t,
            jnp.pad(table.astype(jnp.float32).T, ((0, 0), (0, LANES - bucket_count))),
        )
        payload = dp_relative(after(qkv_local, table))
        arrived = payload[1:]
        payload = after(tuple(payload), bias_t)
        w_qkv = jnp.concatenate(reorder(payload, dp_at), axis=0)

        out_z = tuple(exchange(to_z, lambda k: w_out, zs))
        first_qkv = nn_dot(norm_full[0], w_qkv).astype(jnp.bfloat16)

        ffn_local = jnp.stack([w_gate.T, w_up.T, w_down]).reshape(3, dp_size, part, feats)
        ffn_local = after(ffn_local, *arrived)
        ffn_parts = exchange(
            to_dp,
            lambda k: lax.dynamic_index_in_dim(ffn_local, dp_at ^ k, 1, keepdims=False),
            dp_size,
        )
        arrived = ffn_parts[1:]
        ffn_parts = reorder(after(tuple(ffn_parts), first_qkv), dp_at)
        pre_rows = jnp.concatenate([p[:2] for p in ffn_parts], axis=2)
        post_rows = jnp.concatenate([p[2] for p in ffn_parts], axis=1)
        pre_rows = pre_rows.reshape(2 * part, width)
        pre_gathered = z_gather(pre_rows)

        def group_rows(x):
            parts = dp_relative(x)
            own = jnp.concatenate(parts, axis=0)
            return jnp.concatenate([own, to_core(own)], axis=0), parts[1:]

        def context_to_tokens(context):
            blocks = context.reshape(zs, 2, rows, inner)
            own = lax.dynamic_index_in_dim(blocks, core_at, 1, keepdims=False)
            got = to_core(lax.dynamic_index_in_dim(blocks, 1 - core_at, 1, keepdims=False))
            both = jnp.concatenate([own, got], axis=-1)
            swapped = got
            moved = exchange(
                to_z,
                lambda k: lax.dynamic_index_in_dim(both, z_at ^ k, 0, keepdims=False),
                zs,
            )
            moved = reorder(moved, z_at)
            return (
                jnp.concatenate([m[:, :inner] for m in moved], axis=1),
                jnp.concatenate([m[:, inner:] for m in moved], axis=1),
                swapped,
            )

        def send_tokens(own, other):
            got = to_core(other)
            pair = jnp.stack(reorder([own, got], core_at))
            moved = exchange(
                to_z,
                lambda k: lax.dynamic_slice_in_dim(pair, (z_at ^ k) * inner, inner, 2),
                zs,
            )
            return tuple(moved), got

        def take_tokens(moved):
            return jnp.stack(reorder(moved, z_at)).reshape(length, inner)

        qkv_all, lse_all, ctx_own, ctx_other, swaps = [], [], [], [], []
        mid_rows, second_norm, norm_two_full, cot_full = [], [], [], []

        def feed_forward_input(s):
            own, other = ctx_own[s], ctx_other[s]
            mid = x_rows[s] + (nn_dot(own, out_own) + nn_dot(other, out_other))
            mid_rows.append(mid)
            second_norm.append(rms_parts(mid, gain_two))
            normed = second_norm[s][2]
            if s == 0:
                normed = after(normed, *cot_parts[1:])
            norm_two_full.append(group_rows(normed)[0])

        for s in every:
            if s == 0:
                qkv = first_qkv
            else:
                source = after(norm_full[s], swaps[s - 1])
                if s > 1:
                    source = after(source, second_norm[s - 2][2])
                if s == 1:
                    source = after(source, pre_rows)
                qkv = nn_dot(source, w_qkv).astype(jnp.bfloat16)
            context, lse = attention_forward(qkv, bias_t)
            if s == 0:
                post_gathered = z_gather(after(post_rows, context))
                out_z = jnp.concatenate(reorder(after(out_z, context), z_at), axis=0)
                out_parts = dp_relative(after(out_z, *arrived))
                cot_parts = dp_relative(after(out_grad, *out_parts[1:]))
            if s == 1:
                out_parts = after(tuple(out_parts), context)
                out_own = jnp.concatenate(reorder(out_parts, dp_at), axis=1)
                out_other = to_core(out_own)
            if s > 0:
                feed_forward_input(s - 1)
                context = after(context, second_norm[s - 1][2])
            own, other, swapped = context_to_tokens(context)
            qkv_all.append(qkv)
            lse_all.append(lse)
            ctx_own.append(own)
            ctx_other.append(other)
            swaps.append(swapped)
        feed_forward_input(seqs - 1)
        cot_parts = after(tuple(cot_parts), second_norm[-1][2])
        cot_own = jnp.concatenate([c[i] for i in every for c in cot_parts], axis=0)
        cot_other = to_core(cot_own)

        pre_gathered = after(pre_gathered, norm_two_full[-1])
        w_pre = jnp.transpose(
            pre_gathered.reshape(zs, 2, part, width), (1, 0, 2, 3)
        ).reshape(2 * ff, width)
        half = dp_size * rows
        cot_full = [
            jnp.concatenate(
                [cot_own[s * half : (s + 1) * half], cot_other[s * half : (s + 1) * half]],
                axis=0,
            )
            for s in every
        ]

        first_parts, hidden_all = [], []
        grad_post = None
        for s in every:
            pre = nt_dot(norm_two_full[s], w_pre)
            hidden = gelu_gate(pre[:, :ff], pre[:, ff:]).astype(jnp.bfloat16)
            first_parts.append(pre)
            hidden_all.append(hidden)
            more = tn_dot(hidden, cot_full[s])
            grad_post = more if grad_post is None else grad_post + more
        grad_post = grad_post.astype(jnp.bfloat16)
        w_post = after(post_gathered, grad_post)
        post_z = z_scatter(grad_post)
        pre_all, grad_norm_two, sums, swaps_in, sent_in = [], [], [], [], []
        ready = grad_post
        for s in every:
            pre = first_parts[s]
            _, pull = jax.vjp(gelu_gate, pre[:, :ff], pre[:, ff:])
            cot = after(cot_full[s], ready)
            if s > 1:
                cot = after(cot, *sums[s - 2])
            grad_gate, grad_up = pull(nt_dot(cot, w_post))
            grad_pre = jnp.concatenate([grad_gate, grad_up], axis=1).astype(jnp.bfloat16)
            if s == seqs - 1:
                grad_pre = after(grad_pre, post_z)
            ready = nn_dot(grad_pre, w_pre)
            got = to_core(ready[half:].astype(jnp.bfloat16))
            own = ready[:half] + got.astype(jnp.float32)
            blocks = [
                own[k * rows : (k + 1) * rows].astype(jnp.bfloat16) for k in range(1, dp_size)
            ]
            sent = [to_dp(blocks[k - 1], k) for k in range(1, dp_size)]
            grad_norm_two.append(own[:rows] + sum(x.astype(jnp.float32) for x in sent))
            sums.append(blocks)
            swaps_in.append(got)
            sent_in.append(sent)
            pre_all.append(grad_pre)
        grad_pre_w = None
        for s in every:
            grad_pre = after(pre_all[s], ready)
            if s < seqs - 1:
                grad_pre = after(grad_pre, *sent_in[s], *sums[s + 1])
            more = tn_dot(grad_pre, norm_two_full[s])
            grad_pre_w = more if grad_pre_w is None else grad_pre_w + more
        grad_pre_w = grad_pre_w.astype(jnp.bfloat16)
        pre_z = z_scatter(
            jnp.transpose(
                grad_pre_w.reshape(2, zs, part, width), (1, 0, 2, 3)
            ).reshape(zs * 2 * part, width)
        )

        hidden_own = jnp.concatenate([h[:half] for h in hidden_all], axis=0)
        hidden_other = jnp.concatenate([h[half:] for h in hidden_all], axis=0)
        hidden_own, hidden_other = (
            after(hidden_own, grad_pre_w),
            after(hidden_other, grad_pre_w),
        )
        sent = to_core(nn_dot(hidden_other, w_post).astype(jnp.bfloat16))
        own = (nn_dot(after(hidden_own, grad_norm_two[-1]), w_post) + sent.astype(jnp.float32)).reshape(
            seqs, dp_size, rows, width
        )
        out_blocks = [own[:, k].astype(jnp.bfloat16) for k in range(1, dp_size)]
        out_sent = [to_dp(out_blocks[k - 1], k) for k in range(1, dp_size)]
        ffn_own = own[:, 0]

        grad_mid, grad_mid_low, gain_two_sum = [], [], None
        for s in every:
            plain, inv, _ = second_norm[s]
            more = jnp.sum(grad_norm_two[s] * plain, axis=0)
            gain_two_sum = more if gain_two_sum is None else gain_two_sum + more
            grad = out_grad[s].astype(jnp.float32) + rms_back(
                grad_norm_two[s], plain, inv, gain_two
            )
            grad_mid.append(grad)
            grad_mid_low.append(grad.astype(jnp.bfloat16))

        moves, swapped_in = [], []
        for s in every:
            back_own = nt_dot(grad_mid_low[s], out_own).astype(jnp.bfloat16)
            back_other = nt_dot(grad_mid_low[s], out_other).astype(jnp.bfloat16)
            moved, got = send_tokens(back_own, back_other)
            moves.append(moved)
            swapped_in.append(got)

        def ffn_send(z_rows):
            return tuple(exchange(to_dp, lambda k: feature_block(z_rows, k), dp_size))

        def ffn_take(moved, mats):
            moved = jnp.stack(reorder(moved, dp_at)).reshape(dp_size, mats, part, feats)
            return [moved[:, m].reshape(ff, feats).astype(jnp.float32) for m in range(mats)]

        post_moved = ffn_send(post_z)
        grad_normed, grad_scores, normed_parts, qkv_grads = [], [], [], []
        grad_qkv = None
        gate = (grad_pre_w, *out_blocks)
        for s in every:
            moved = after(moves[s], *gate)
            if s < seqs - 1:
                moved = after(moved, swapped_in[s + 1])
            if s == 1:
                moved = after(moved, *out_sent)
            if s == seqs - 1:
                moved = after(moved, pre_z, *post_moved[1:])
            grad_proj, grad_score = attention_backward(
                qkv_all[s], take_tokens(moved), bias_t, lse_all[s]
            )
            grad_scores.append(grad_score)
            qkv_grads.append(grad_proj)
            normed_part = nt_dot(grad_proj, w_qkv).astype(jnp.bfloat16)
            normed_parts.append(normed_part)
            gate = (normed_part,)
            grad_normed.append(
                lax.psum_scatter(
                    normed_part, "tensor", scatter_dimension=0, tiled=True
                ).astype(jnp.float32)
            )
            if s == 0:
                mid_low = after(jnp.concatenate(grad_mid_low, axis=0), normed_part)
                out_give = tn_dot(jnp.concatenate(ctx_other, axis=0), mid_low).astype(
                    jnp.bfloat16
                )
                out_got = to_core(out_give)
                out_keep = tn_dot(jnp.concatenate(ctx_own, axis=0), mid_low)
                gate = gate + (out_give, out_keep)
            else:
                for t in [0, 1] if s == 1 else [s]:
                    more = tn_dot(norm_full[t], after(qkv_grads[t], normed_part))
                    grad_qkv = more if grad_qkv is None else grad_qkv + more
                gate = gate + (grad_qkv,)
            if s == 1:
                out_sum = out_keep + after(out_got, normed_part).astype(jnp.float32)
                out_moved = tuple(
                    exchange(
                        to_dp,
                        lambda k: feature_block(out_sum, k)
                        if k == 0
                        else feature_block(out_sum, k).astype(jnp.bfloat16),
                        dp_size,
                    )
                )
        pre_moved = ffn_send(pre_z)
        out_moved = after(out_moved, normed_parts[-1])
        grad_out_z = sum(m.astype(jnp.float32) for m in out_moved)
        grad_out_keep = lax.dynamic_slice_in_dim(grad_out_z, z_at * inner, inner, 0)
        grad_out_blocks = [
            lax.dynamic_slice_in_dim(grad_out_z, (z_at ^ k) * inner, inner, 0).astype(
                jnp.bfloat16
            )
            for k in range(1, zs)
        ]
        grad_out_sent = [to_z(grad_out_blocks[k - 1], k) for k in range(1, zs)]
        qkv_blocks = [
            lax.dynamic_slice_in_dim(grad_qkv, (dp_at ^ k) * feats, feats, 0).astype(
                jnp.bfloat16
            )
            for k in range(1, dp_size)
        ]
        qkv_sent = [to_dp(qkv_blocks[k - 1], k) for k in range(1, dp_size)]
        bucket_gate = after(
            buckets_t, *pre_moved[1:], *grad_out_blocks, *qkv_blocks, grad_normed[0]
        )
        table_grad = bucket_sums(bucket_gate, grad_scores, bucket_count)
        grad_out = grad_out_keep + sum(
            x.astype(jnp.float32) for x in after(tuple(grad_out_sent), table_grad)
        )
        summed = lax.dynamic_slice_in_dim(grad_qkv, dp_at * feats, feats, 0) + sum(
            x.astype(jnp.float32) for x in after(tuple(qkv_sent), table_grad)
        )
        out_sent = after(tuple(out_sent), normed_parts[-1])
        ffn_out = ffn_own + sum(m.astype(jnp.float32) for m in out_sent)
        output = jnp.stack(
            [(mid_rows[s] + ffn_out[s]).astype(jnp.bfloat16) for s in every]
        )

        (grad_down,) = ffn_take(post_moved, 1)
        grad_gate_t, grad_up_t = ffn_take(pre_moved, 2)

        def columns(which):
            return jnp.concatenate(
                [
                    summed[:, (3 * p + which) * LANES : (3 * p + which + 1) * LANES]
                    for p in range(pairs)
                ],
                axis=1,
            )

        grad_table = total_of(
            to_dp,
            lambda k: lax.dynamic_slice_in_dim(
                table_grad, (dp_at ^ k) * table_rows, table_rows, 0
            ),
            dp_size,
        )

        grad_in, gain_one_sum = [], None
        for s in every:
            plain, inv, _ = first_norm[s]
            more = jnp.sum(grad_normed[s] * plain, axis=0)
            gain_one_sum = more if gain_one_sum is None else gain_one_sum + more
            grad_in.append(
                (grad_mid[s] + rms_back(grad_normed[s], plain, inv, gain_one)).astype(
                    jnp.bfloat16
                )
            )
        gains = all_sum(jnp.stack([gain_one_sum, gain_two_sum]))
        return (
            output,
            jnp.stack(grad_in),
            gains[0],
            gains[1],
            columns(0),
            columns(1),
            columns(2),
            grad_out,
            grad_gate_t.T,
            grad_up_t.T,
            grad_down,
            grad_table,
        )

    return body


def solution(mesh):
    in_specs = (
        P("dp", "tensor", None),
        P("dp", "tensor", None),
        P(),
        P(),
        P(),
        P("dp", "tensor"),
        P("dp", "tensor"),
        P("dp", "tensor"),
        P("tensor", "dp"),
        P("dp", "tensor"),
        P("dp", "tensor"),
        P("tensor", "dp"),
        P("dp", "tensor"),
    )
    out_specs = (
        P("dp", "tensor", None),
        P("dp", "tensor", None),
        P(),
        P(),
        P("dp", "tensor"),
        P("dp", "tensor"),
        P("dp", "tensor"),
        P("tensor", "dp"),
        P("dp", "tensor"),
        P("dp", "tensor"),
        P("tensor", "dp"),
        P("dp", "tensor"),
    )
    body = make_body(mesh.shape["dp"], mesh.shape["tensor"])
    return jax.shard_map(body, mesh=mesh, in_specs=in_specs, out_specs=out_specs, check_vma=False)
```

```python
import functools
import jax
import jax.numpy as jnp
from jax import lax
from jax.experimental import pallas as pl
from jax.experimental.pallas import tpu as pltpu
from jax.sharding import PartitionSpec as P

HD = 64
LANES = 128
norm_eps = 1e-06
VMEM_ROOM = 50 * 1024 * 1024


def nt_dot(left, right):
    return lax.dot_general(
        left, right, (((1,), (1,)), ((), ())), preferred_element_type=jnp.float32
    )


def nn_dot(left, right):
    return jnp.dot(left, right, preferred_element_type=jnp.float32)


def head_masks(rows):
    lane = lax.broadcasted_iota(jnp.int32, (rows, LANES), 1)
    return (lane < HD, lane >= HD)


def only_head(keep, pair_cols):
    return jnp.where(keep, pair_cols, jnp.zeros_like(pair_cols))


def expand_kernel(buckets_ref, table_ref, bias_ref):
    heads = table_ref.shape[0]
    rows, cols = buckets_ref.shape
    for col in range(0, cols, LANES):
        ids = buckets_ref[:, col : col + LANES]
        for head in range(heads):
            row = jnp.broadcast_to(table_ref[head : head + 1, :], (rows, LANES))
            bias_ref[head, :, col : col + LANES] = jnp.take_along_axis(
                row, ids, axis=1
            ).astype(jnp.bfloat16)


def expand_bias(buckets_t, table_rows):
    length = buckets_t.shape[0]
    heads = table_rows.shape[0]
    block = 64
    return pl.pallas_call(
        expand_kernel,
        grid=(length // block,),
        in_specs=[
            pl.BlockSpec((block, length), lambda i: (i, 0)),
            pl.BlockSpec((heads, LANES), lambda i: (0, 0)),
        ],
        out_specs=pl.BlockSpec((heads, block, length), lambda i: (0, i, 0)),
        out_shape=jax.ShapeDtypeStruct((heads, length, length), jnp.bfloat16),
        cost_estimate=pl.CostEstimate(
            flops=heads * length, bytes_accessed=heads * length, transcendentals=0
        ),
        name="expand_bias",
    )(buckets_t, table_rows)


def forward_kernel(block_cols, qkv_ref, bias_ref, context_ref, lse_ref):
    length = qkv_ref.shape[0]
    keys = qkv_ref[:, LANES : 2 * LANES]
    masks = head_masks(length)
    head_keys = [only_head(keep, keys) for keep in masks]
    values_t = qkv_ref[:, 2 * LANES :].T
    for start in range(0, length, block_cols):
        span = pl.ds(start, block_cols)
        queries = qkv_ref[span, :LANES]
        pieces = []
        for head in range(2):
            scores = nt_dot(head_keys[head], queries) + bias_ref[head, :, span].astype(
                jnp.float32
            )
            top = jnp.max(scores, axis=0, keepdims=True)
            shifted = jnp.exp(scores - top)
            total = jnp.sum(shifted, axis=0, keepdims=True)
            probs = (shifted * (1.0 / total)).astype(jnp.bfloat16)
            pieces.append(nn_dot(values_t[head * HD : (head + 1) * HD], probs))
            lse_ref[0, head : head + 1, span] = top + jnp.log(total)
        context_ref[span, :] = jnp.concatenate(pieces, axis=0).T.astype(jnp.bfloat16)


def attention_forward(qkv, bias_t):
    length = qkv.shape[0]
    pairs = qkv.shape[1] // (3 * LANES)
    heads = 2 * pairs
    return pl.pallas_call(
        functools.partial(forward_kernel, min(256, length)),
        grid=(pairs,),
        in_specs=[
            pl.BlockSpec((length, 3 * LANES), lambda p: (0, p)),
            pl.BlockSpec((2, length, length), lambda p: (p, 0, 0)),
        ],
        out_specs=[
            pl.BlockSpec((length, LANES), lambda p: (0, p)),
            pl.BlockSpec((1, 2, length), lambda p: (p, 0, 0)),
        ],
        out_shape=[
            jax.ShapeDtypeStruct((length, pairs * LANES), jnp.bfloat16),
            jax.ShapeDtypeStruct((pairs, 2, length), jnp.float32),
        ],
        compiler_params=pltpu.CompilerParams(vmem_limit_bytes=VMEM_ROOM),
        cost_estimate=pl.CostEstimate(
            flops=heads * length, bytes_accessed=heads * length, transcendentals=0
        ),
        name="attention_forward",
    )(qkv, bias_t)


def backward_kernel(
    block_cols, qkv_ref, grad_ref, bias_ref, lse_ref, out_ref, grad_scores_ref, dk_acc, dv_acc
):
    length = qkv_ref.shape[0]
    keys = qkv_ref[:, LANES : 2 * LANES]
    values = qkv_ref[:, 2 * LANES :]
    masks = head_masks(length)
    small_masks = head_masks(block_cols)
    head_keys = [only_head(keep, keys) for keep in masks]
    head_values = [only_head(keep, values) for keep in masks]
    keys_t = keys.T
    for start in range(0, length, block_cols):
        span = pl.ds(start, block_cols)
        queries = qkv_ref[span, :LANES]
        grads = grad_ref[span, :]
        pieces = []
        for head in range(2):
            scores = nt_dot(head_keys[head], queries) + bias_ref[head, :, span].astype(
                jnp.float32
            )
            probs = jnp.exp(scores - lse_ref[0, head : head + 1, span])
            grad_probs = nt_dot(head_values[head], grads)
            inner = jnp.sum(probs * grad_probs, axis=0, keepdims=True)
            grad_scores = (probs * (grad_probs - inner)).astype(jnp.bfloat16)
            grad_scores_ref[head, :, span] = grad_scores
            value_part = nn_dot(
                probs.astype(jnp.bfloat16), only_head(small_masks[head], grads)
            )
            key_part = nn_dot(grad_scores, only_head(small_masks[head], queries))
            if start == 0 and head == 0:
                dv_acc[...] = value_part
                dk_acc[...] = key_part
            else:
                dv_acc[...] += value_part
                dk_acc[...] += key_part
            pieces.append(nn_dot(keys_t[head * HD : (head + 1) * HD], grad_scores))
        out_ref[span, :LANES] = jnp.concatenate(pieces, axis=0).T.astype(jnp.bfloat16)
    out_ref[:, LANES : 2 * LANES] = dk_acc[...].astype(jnp.bfloat16)
    out_ref[:, 2 * LANES :] = dv_acc[...].astype(jnp.bfloat16)


def attention_backward(qkv, grad_context, bias_t, lse):
    length = qkv.shape[0]
    pairs = qkv.shape[1] // (3 * LANES)
    heads = 2 * pairs
    return pl.pallas_call(
        functools.partial(backward_kernel, min(256, length)),
        grid=(pairs,),
        in_specs=[
            pl.BlockSpec((length, 3 * LANES), lambda p: (0, p)),
            pl.BlockSpec((length, LANES), lambda p: (0, p)),
            pl.BlockSpec((2, length, length), lambda p: (p, 0, 0)),
            pl.BlockSpec((1, 2, length), lambda p: (p, 0, 0)),
        ],
        out_specs=[
            pl.BlockSpec((length, 3 * LANES), lambda p: (0, p)),
            pl.BlockSpec((2, length, length), lambda p: (p, 0, 0)),
        ],
        out_shape=[
            jax.ShapeDtypeStruct((length, pairs * 3 * LANES), jnp.bfloat16),
            jax.ShapeDtypeStruct((heads, length, length), jnp.bfloat16),
        ],
        scratch_shapes=[
            pltpu.VMEM((length, LANES), jnp.float32),
            pltpu.VMEM((length, LANES), jnp.float32),
        ],
        compiler_params=pltpu.CompilerParams(vmem_limit_bytes=VMEM_ROOM),
        cost_estimate=pl.CostEstimate(
            flops=heads * length, bytes_accessed=heads * length, transcendentals=0
        ),
        name="attention_backward",
    )(qkv, grad_context, bias_t, lse)


def histogram_kernel(bucket_count, group, buckets_ref, *refs):
    grads, (sums_ref, values) = refs[:-2], refs[-2:]
    heads, rows, cols = values.shape

    @pl.when(pl.program_id(0) == 0)
    def _():
        sums_ref[...] = jnp.zeros_like(sums_ref)

    total = grads[0][...].astype(jnp.float32)
    for other in grads[1:]:
        total = total + other[...].astype(jnp.float32)
    values[...] = total

    @pl.loop(0, bucket_count // group)
    def _(step):
        first = step * group
        acc = [[jnp.zeros((8, LANES), jnp.float32) for _ in range(heads)] for _ in range(group)]
        for row in range(0, rows, 8):
            for col in range(0, cols, LANES):
                ids = buckets_ref[row : row + 8, col : col + LANES]
                vals = [values[h, row : row + 8, col : col + LANES] for h in range(heads)]
                for j in range(group):
                    hit = ids == first + j
                    for h in range(heads):
                        acc[j][h] = acc[j][h] + jnp.where(hit, vals[h], 0.0)
        for j in range(group):
            for h in range(heads):
                sums_ref[h, first + j] += acc[j][h]


def bucket_sums(buckets_t, grad_scores, bucket_count):
    heads, length, _ = grad_scores[0].shape
    block = 32
    sums = pl.pallas_call(
        functools.partial(histogram_kernel, bucket_count, 4),
        grid=(length // block,),
        in_specs=[pl.BlockSpec((block, length), lambda i: (i, 0))]
        + [pl.BlockSpec((heads, block, length), lambda i: (0, i, 0))] * len(grad_scores),
        out_specs=pl.BlockSpec((heads, bucket_count, 8, LANES), lambda i: (0, 0, 0, 0)),
        out_shape=jax.ShapeDtypeStruct((heads, bucket_count, 8, LANES), jnp.float32),
        scratch_shapes=[pltpu.VMEM((heads, block, length), jnp.float32)],
        compiler_params=pltpu.CompilerParams(vmem_limit_bytes=VMEM_ROOM),
        cost_estimate=pl.CostEstimate(
            flops=heads * length, bytes_accessed=heads * length, transcendentals=0
        ),
        name="bucket_sums",
    )(buckets_t, *grad_scores)
    return jnp.sum(sums, axis=(2, 3)).T


def xor_pairs(count, mask):
    return [(i, i ^ mask) for i in range(count)]


def reorder(blocks, place):
    blocks = list(blocks)
    bit = 1
    while bit < len(blocks):
        flag = (place & bit) != 0
        blocks = [jnp.where(flag, blocks[i ^ bit], blocks[i]) for i in range(len(blocks))]
        bit *= 2
    return blocks


def rms_parts(seq_rows, gain_vec):
    inv_rms = lax.rsqrt(jnp.mean(seq_rows * seq_rows, axis=-1, keepdims=True) + norm_eps)
    plain_rows = seq_rows * inv_rms
    return (plain_rows, inv_rms, (plain_rows * gain_vec).astype(jnp.bfloat16))


def rms_back(grad_norm, plain_rows, inv_rms, gain_vec):
    scaled_grad = grad_norm * gain_vec
    return inv_rms * (
        scaled_grad - plain_rows * jnp.mean(scaled_grad * plain_rows, axis=-1, keepdims=True)
    )


def gelu_gate(gate_pre, up_pre):
    return jax.nn.gelu(gate_pre, approximate=True) * up_pre


def tn_dot(left, right):
    return lax.dot_general(
        left, right, (((0,), (0,)), ((), ())), preferred_element_type=jnp.float32
    )


def after(x, *needed):
    return lax.optimization_barrier((x, *needed))[0]


def make_body(dp_size, tensor_size):
    zs = tensor_size // 2
    z_groups = [[2 * z + core for z in range(zs)] for core in range(2)]
    core_pairs = xor_pairs(tensor_size, 1)

    def to_core(x):
        return lax.ppermute(x, "tensor", core_pairs)

    def to_dp(x, mask):
        return lax.ppermute(x, "dp", xor_pairs(dp_size, mask))

    def to_z(x, mask):
        return lax.ppermute(x, "tensor", xor_pairs(tensor_size, 2 * mask))

    def dp_relative(x):
        return [x] + [to_dp(x, k) for k in range(1, dp_size)]

    def exchange(send, pick, size):
        return [pick(0)] + [send(pick(k), k) for k in range(1, size)]

    def total_of(send, pick, size):
        own = pick(0).astype(jnp.float32)
        for k in range(1, size):
            own = own + send(pick(k).astype(jnp.bfloat16), k).astype(jnp.float32)
        return own

    def z_gather(x):
        return lax.all_gather(x, "tensor", axis=0, tiled=True, axis_index_groups=z_groups)

    def z_scatter(x):
        return lax.psum_scatter(
            x, "tensor", scatter_dimension=0, tiled=True, axis_index_groups=z_groups
        )

    def all_sum(x):
        bit = 1
        while bit < tensor_size:
            x = x + lax.ppermute(x, "tensor", xor_pairs(tensor_size, bit))
            bit *= 2
        bit = 1
        while bit < dp_size:
            x = x + to_dp(x, bit)
            bit *= 2
        return x

    def body(
        hidden_in,
        out_grad,
        buckets,
        gain_attn,
        gain_ffn,
        w_query,
        w_key,
        w_value,
        w_out,
        w_gate,
        w_up,
        w_down,
        bias_table,
    ):
        dp_at = lax.axis_index("dp")
        tensor_at = lax.axis_index("tensor")
        core_at = tensor_at % 2
        z_at = tensor_at // 2
        seqs, rows, width = hidden_in.shape
        length = buckets.shape[0]
        feats = w_query.shape[0]
        inner = w_query.shape[1]
        heads = inner // HD
        pairs = inner // LANES
        ff = w_gate.shape[1]
        part = ff // dp_size
        table_rows = bias_table.shape[0]
        bucket_count = table_rows * dp_size
        gain_one = gain_attn.astype(jnp.float32)
        gain_two = gain_ffn.astype(jnp.float32)
        every = range(seqs)

        def feature_block(x, k):
            return lax.dynamic_slice_in_dim(x, (dp_at ^ k) * feats, feats, 1)

        x_rows = [hidden_in[s].astype(jnp.float32) for s in every]
        first_norm = [rms_parts(x, gain_one) for x in x_rows]
        norm_full = [
            lax.all_gather(first_norm[s][2], "tensor", axis=0, tiled=True) for s in every
        ]

        qkv_local = jnp.concatenate(
            [
                w[:, p * LANES : (p + 1) * LANES]
                for p in range(pairs)
                for w in (w_query, w_key, w_value)
            ],
            axis=1,
        )
        table = jnp.concatenate(reorder(dp_relative(bias_table), dp_at), axis=0)
        buckets_t = buckets.T
        bias_t = expand_bias(
            buckets_t,
            jnp.pad(table.astype(jnp.float32).T, ((0, 0), (0, LANES - bucket_count))),
        )
        payload = dp_relative(after(qkv_local, table))
        arrived = payload[1:]
        payload = after(tuple(payload), bias_t)
        w_qkv = jnp.concatenate(reorder(payload, dp_at), axis=0)

        out_z = tuple(exchange(to_z, lambda k: w_out, zs))
        first_qkv = nn_dot(norm_full[0], w_qkv).astype(jnp.bfloat16)

        ffn_local = jnp.stack([w_gate.T, w_up.T, w_down]).reshape(3, dp_size, part, feats)
        ffn_local = after(ffn_local, *arrived)
        ffn_parts = exchange(
            to_dp,
            lambda k: lax.dynamic_index_in_dim(ffn_local, dp_at ^ k, 1, keepdims=False),
            dp_size,
        )
        arrived = ffn_parts[1:]
        ffn_parts = reorder(after(tuple(ffn_parts), first_qkv), dp_at)
        pre_rows = jnp.concatenate([p[:2] for p in ffn_parts], axis=2)
        post_rows = jnp.concatenate([p[2] for p in ffn_parts], axis=1)
        pre_rows = pre_rows.reshape(2 * part, width)
        pre_gathered = z_gather(pre_rows)

        def both_cores(blocks):
            own = jnp.concatenate(blocks, axis=0)
            return jnp.concatenate([own, to_core(own)], axis=0)

        def context_to_tokens(context):
            blocks = context.reshape(zs, 2, rows, inner)
            own = lax.dynamic_index_in_dim(blocks, core_at, 1, keepdims=False)
            got = to_core(lax.dynamic_index_in_dim(blocks, 1 - core_at, 1, keepdims=False))
            both = jnp.concatenate([own, got], axis=-1)
            swapped = got
            moved = exchange(
                to_z,
                lambda k: lax.dynamic_index_in_dim(both, z_at ^ k, 0, keepdims=False),
                zs,
            )
            moved = reorder(moved, z_at)
            return (
                jnp.concatenate([m[:, :inner] for m in moved], axis=1),
                jnp.concatenate([m[:, inner:] for m in moved], axis=1),
                swapped,
            )

        def send_tokens(own, other):
            got = to_core(other)
            pair = jnp.stack(reorder([own, got], core_at))
            moved = exchange(
                to_z,
                lambda k: lax.dynamic_slice_in_dim(pair, (z_at ^ k) * inner, inner, 2),
                zs,
            )
            return tuple(moved), got

        def take_tokens(moved):
            return jnp.stack(reorder(moved, z_at)).reshape(length, inner)

        qkv_all, lse_all, ctx_own, ctx_other, swaps = [], [], [], [], []
        mid_rows, second_norm, norm_two_full = [], [], []

        early = dp_relative(
            after(jnp.concatenate([out_grad[0], out_grad[1]], axis=0), *arrived)
        )
        recent = [early[1:]]
        cot_full = []

        def feed_forward_input(s):
            own, other = ctx_own[s], ctx_other[s]
            if s == 1:
                own = after(own, *recent[-1])
            mid = x_rows[s] + (nn_dot(own, out_own) + nn_dot(other, out_other))
            mid_rows.append(mid)
            second_norm.append(rms_parts(mid, gain_two))
            normed = second_norm[s][2]
            normed = after(normed, *recent[-1])
            riders = [out_grad[t] for t in every if 1 <= s == t - 1]
            parts = dp_relative(jnp.concatenate([normed, *riders], axis=0))
            recent.append(parts[1:])
            norm_two_full.append(both_cores([x[:rows] for x in parts]))
            for i in range(1, len(riders) + 1):
                cot_full.append(both_cores([x[i * rows : (i + 1) * rows] for x in parts]))

        for s in every:
            if s == 0:
                qkv = first_qkv
            else:
                source = after(norm_full[s], swaps[s - 1])
                if s > 1:
                    source = after(source, second_norm[s - 2][2])
                if s == 1:
                    source = after(source, pre_rows)
                qkv = nn_dot(source, w_qkv).astype(jnp.bfloat16)
            context, lse = attention_forward(qkv, bias_t)
            if s == 0:
                post_gathered = z_gather(after(post_rows, context))
                out_z = jnp.concatenate(reorder(after(out_z, context), z_at), axis=0)
                out_parts = dp_relative(after(out_z, *arrived))
            if s == 1:
                out_parts = after(tuple(out_parts), context)
                out_own = jnp.concatenate(reorder(out_parts, dp_at), axis=1)
                out_other = to_core(out_own)
            if s == 1:
                taken = after(tuple(early), context)
                cot_full.append(both_cores([x[:rows] for x in taken]))
                cot_full.append(both_cores([x[rows:] for x in taken]))
            if s > 0:
                feed_forward_input(s - 1)
                context = after(context, second_norm[s - 1][2])
            own, other, swapped = context_to_tokens(context)
            qkv_all.append(qkv)
            lse_all.append(lse)
            ctx_own.append(own)
            ctx_other.append(other)
            swaps.append(swapped)
        feed_forward_input(seqs - 1)
        pre_gathered = after(pre_gathered, norm_two_full[-1])
        w_pre = jnp.transpose(
            pre_gathered.reshape(zs, 2, part, width), (1, 0, 2, 3)
        ).reshape(2 * ff, width)
        half = dp_size * rows
        first_parts, hidden_all = [], []
        grad_post = None
        for s in every:
            pre = nt_dot(norm_two_full[s], w_pre)
            hidden = gelu_gate(pre[:, :ff], pre[:, ff:]).astype(jnp.bfloat16)
            first_parts.append(pre)
            hidden_all.append(hidden)
            more = tn_dot(hidden, cot_full[s])
            grad_post = more if grad_post is None else grad_post + more
        grad_post = grad_post.astype(jnp.bfloat16)
        w_post = after(post_gathered, grad_post)
        post_z = z_scatter(grad_post)
        pre_all, grad_norm_two, sums, swaps_in, sent_in = [], [], [], [], []
        ready = grad_post
        for s in every:
            pre = first_parts[s]
            _, pull = jax.vjp(gelu_gate, pre[:, :ff], pre[:, ff:])
            cot = after(cot_full[s], ready)
            if s > 1:
                cot = after(cot, *sums[s - 2])
            grad_gate, grad_up = pull(nt_dot(cot, w_post))
            grad_pre = jnp.concatenate([grad_gate, grad_up], axis=1).astype(jnp.bfloat16)
            ready = nn_dot(grad_pre, w_pre)
            got = to_core(ready[half:].astype(jnp.bfloat16))
            own = ready[:half] + got.astype(jnp.float32)
            blocks = [
                own[k * rows : (k + 1) * rows].astype(jnp.bfloat16) for k in range(1, dp_size)
            ]
            sent = [to_dp(blocks[k - 1], k) for k in range(1, dp_size)]
            grad_norm_two.append(own[:rows] + sum(x.astype(jnp.float32) for x in sent))
            sums.append(blocks)
            swaps_in.append(got)
            sent_in.append(sent)
            pre_all.append(grad_pre)
        grad_mid, grad_mid_low, gain_two_sum = [], [], None
        for s in every:
            plain, inv, _ = second_norm[s]
            more = jnp.sum(grad_norm_two[s] * plain, axis=0)
            gain_two_sum = more if gain_two_sum is None else gain_two_sum + more
            grad = out_grad[s].astype(jnp.float32) + rms_back(
                grad_norm_two[s], plain, inv, gain_two
            )
            grad_mid.append(grad)
            grad_mid_low.append(grad.astype(jnp.bfloat16))

        moves, swapped_in = [], []
        for s in every:
            back_own = nt_dot(grad_mid_low[s], out_own).astype(jnp.bfloat16)
            back_other = nt_dot(grad_mid_low[s], out_other).astype(jnp.bfloat16)
            moved, got = send_tokens(back_own, back_other)
            moves.append(moved)
            swapped_in.append(got)

        grad_pre_w = None
        for s in every:
            grad_pre = after(pre_all[s], ready)
            if s == 0:
                grad_pre = after(grad_pre, *sums[1], post_z)
            else:
                grad_pre = after(grad_pre, swapped_in[s - 1])
            more = tn_dot(grad_pre, norm_two_full[s])
            grad_pre_w = more if grad_pre_w is None else grad_pre_w + more
        grad_pre_w = grad_pre_w.astype(jnp.bfloat16)
        pre_z = z_scatter(
            jnp.transpose(
                grad_pre_w.reshape(2, zs, part, width), (1, 0, 2, 3)
            ).reshape(zs * 2 * part, width)
        )

        hidden_own = jnp.concatenate([h[:half] for h in hidden_all], axis=0)
        hidden_other = jnp.concatenate([h[half:] for h in hidden_all], axis=0)
        hidden_own, hidden_other = (
            after(hidden_own, grad_pre_w),
            after(hidden_other, grad_pre_w),
        )
        sent = to_core(nn_dot(hidden_other, w_post).astype(jnp.bfloat16))
        own = (nn_dot(after(hidden_own, grad_norm_two[-1]), w_post) + sent.astype(jnp.float32)).reshape(
            seqs, dp_size, rows, width
        )
        out_blocks = [own[:, k].astype(jnp.bfloat16) for k in range(1, dp_size)]
        out_sent = [to_dp(out_blocks[k - 1], k) for k in range(1, dp_size)]
        ffn_own = own[:, 0]

        def ffn_send(z_rows):
            return tuple(exchange(to_dp, lambda k: feature_block(z_rows, k), dp_size))

        def ffn_take(moved, mats):
            moved = jnp.stack(reorder(moved, dp_at)).reshape(dp_size, mats, part, feats)
            return [moved[:, m].reshape(ff, feats).astype(jnp.float32) for m in range(mats)]

        post_moved = ffn_send(post_z)
        pre_moved = ffn_send(pre_z)
        grad_normed, grad_scores, normed_parts, qkv_grads = [], [], [], []
        grad_qkv = None
        gate = (grad_pre_w,)
        for s in every:
            moved = after(moves[s], *gate)
            if s < seqs - 1:
                moved = after(moved, swapped_in[s + 1])
            if s == 1:
                moved = after(moved, *out_blocks)
            if s == seqs - 1:
                moved = after(moved, *post_moved[1:], *pre_moved[1:], *out_give_dp)
            grad_proj, grad_score = attention_backward(
                qkv_all[s], take_tokens(moved), bias_t, lse_all[s]
            )
            grad_scores.append(grad_score)
            qkv_grads.append(grad_proj)
            ordered = grad_proj
            if s == 1:
                ordered = after(ordered, *out_sent)
            if s == seqs - 1:
                ordered = after(ordered, *out_moved[1:])
            normed_part = nt_dot(ordered, w_qkv).astype(jnp.bfloat16)
            normed_parts.append(normed_part)
            gate = (normed_part,)
            grad_normed.append(
                lax.psum_scatter(
                    normed_part, "tensor", scatter_dimension=0, tiled=True
                ).astype(jnp.float32)
            )
            if s == 0:
                mid_low = after(jnp.concatenate(grad_mid_low, axis=0), normed_part)
                out_give = tn_dot(jnp.concatenate(ctx_other, axis=0), mid_low).astype(
                    jnp.bfloat16
                )
                out_got = to_core(out_give)
                out_keep = tn_dot(jnp.concatenate(ctx_own, axis=0), mid_low)
                gate = gate + (out_give, out_keep)
            else:
                for t in [0, 1] if s == 1 else [s]:
                    more = tn_dot(norm_full[t], after(qkv_grads[t], normed_part))
                    grad_qkv = more if grad_qkv is None else grad_qkv + more
                gate = gate + (grad_qkv,)
            if s == 1:
                out_sum = out_keep + after(out_got, normed_part).astype(jnp.float32)
                out_give_dp = [
                    feature_block(out_sum, k).astype(jnp.bfloat16) for k in range(1, dp_size)
                ]
                out_moved = (
                    feature_block(out_sum, 0),
                    *[to_dp(out_give_dp[k - 1], k) for k in range(1, dp_size)],
                )
        out_moved = after(out_moved, normed_parts[-1])
        grad_out_z = sum(m.astype(jnp.float32) for m in out_moved)
        grad_out_keep = lax.dynamic_slice_in_dim(grad_out_z, z_at * inner, inner, 0)
        grad_out_blocks = [
            lax.dynamic_slice_in_dim(grad_out_z, (z_at ^ k) * inner, inner, 0).astype(
                jnp.bfloat16
            )
            for k in range(1, zs)
        ]
        grad_out_sent = [to_z(grad_out_blocks[k - 1], k) for k in range(1, zs)]
        qkv_blocks = [
            lax.dynamic_slice_in_dim(grad_qkv, (dp_at ^ k) * feats, feats, 0).astype(
                jnp.bfloat16
            )
            for k in range(1, dp_size)
        ]
        qkv_sent = [to_dp(qkv_blocks[k - 1], k) for k in range(1, dp_size)]
        bucket_gate = after(
            buckets_t, *grad_out_blocks, *qkv_blocks, grad_normed[0]
        )
        table_grad = bucket_sums(bucket_gate, grad_scores, bucket_count)
        grad_out = grad_out_keep + sum(
            x.astype(jnp.float32) for x in after(tuple(grad_out_sent), table_grad)
        )
        summed = lax.dynamic_slice_in_dim(grad_qkv, dp_at * feats, feats, 0) + sum(
            x.astype(jnp.float32) for x in after(tuple(qkv_sent), table_grad)
        )
        ffn_out = ffn_own + sum(
            m.astype(jnp.float32) for m in after(tuple(out_sent), normed_parts[-1])
        )
        output = jnp.stack(
            [(mid_rows[s] + ffn_out[s]).astype(jnp.bfloat16) for s in every]
        )

        (grad_down,) = ffn_take(post_moved, 1)
        grad_gate_t, grad_up_t = ffn_take(pre_moved, 2)

        def columns(which):
            return jnp.concatenate(
                [
                    summed[:, (3 * p + which) * LANES : (3 * p + which + 1) * LANES]
                    for p in range(pairs)
                ],
                axis=1,
            )

        grad_table = total_of(
            to_dp,
            lambda k: lax.dynamic_slice_in_dim(
                table_grad, (dp_at ^ k) * table_rows, table_rows, 0
            ),
            dp_size,
        )

        grad_in, gain_one_sum = [], None
        for s in every:
            plain, inv, _ = first_norm[s]
            more = jnp.sum(grad_normed[s] * plain, axis=0)
            gain_one_sum = more if gain_one_sum is None else gain_one_sum + more
            grad_in.append(
                (grad_mid[s] + rms_back(grad_normed[s], plain, inv, gain_one)).astype(
                    jnp.bfloat16
                )
            )
        gains = all_sum(jnp.stack([gain_one_sum, gain_two_sum]))
        return (
            output,
            jnp.stack(grad_in),
            gains[0],
            gains[1],
            columns(0),
            columns(1),
            columns(2),
            grad_out,
            grad_gate_t.T,
            grad_up_t.T,
            grad_down,
            grad_table,
        )

    return body


def solution(mesh):
    in_specs = (
        P("dp", "tensor", None),
        P("dp", "tensor", None),
        P(),
        P(),
        P(),
        P("dp", "tensor"),
        P("dp", "tensor"),
        P("dp", "tensor"),
        P("tensor", "dp"),
        P("dp", "tensor"),
        P("dp", "tensor"),
        P("tensor", "dp"),
        P("dp", "tensor"),
    )
    out_specs = (
        P("dp", "tensor", None),
        P("dp", "tensor", None),
        P(),
        P(),
        P("dp", "tensor"),
        P("dp", "tensor"),
        P("dp", "tensor"),
        P("tensor", "dp"),
        P("dp", "tensor"),
        P("dp", "tensor"),
        P("tensor", "dp"),
        P("dp", "tensor"),
    )
    body = make_body(mesh.shape["dp"], mesh.shape["tensor"])
    return jax.shard_map(body, mesh=mesh, in_specs=in_specs, out_specs=out_specs, check_vma=False)
```

```python
import functools
import jax
import jax.numpy as jnp
from jax import lax
from jax.experimental import pallas as pl
from jax.experimental.pallas import tpu as pltpu
from jax.sharding import PartitionSpec as P

HD = 64
LANES = 128
norm_eps = 1e-06
VMEM_ROOM = 50 * 1024 * 1024


def nt_dot(left, right):
    return lax.dot_general(
        left, right, (((1,), (1,)), ((), ())), preferred_element_type=jnp.float32
    )


def nn_dot(left, right):
    return jnp.dot(left, right, preferred_element_type=jnp.float32)


def head_masks(rows):
    lane = lax.broadcasted_iota(jnp.int32, (rows, LANES), 1)
    return (lane < HD, lane >= HD)


def only_head(keep, pair_cols):
    return jnp.where(keep, pair_cols, jnp.zeros_like(pair_cols))


def expand_kernel(buckets_ref, table_ref, bias_ref):
    heads = table_ref.shape[0]
    rows, cols = buckets_ref.shape
    for col in range(0, cols, LANES):
        ids = buckets_ref[:, col : col + LANES]
        for head in range(heads):
            row = jnp.broadcast_to(table_ref[head : head + 1, :], (rows, LANES))
            bias_ref[head, :, col : col + LANES] = jnp.take_along_axis(
                row, ids, axis=1
            ).astype(jnp.bfloat16)


def expand_bias(buckets_t, table_rows):
    length = buckets_t.shape[0]
    heads = table_rows.shape[0]
    block = 64
    return pl.pallas_call(
        expand_kernel,
        grid=(length // block,),
        in_specs=[
            pl.BlockSpec((block, length), lambda i: (i, 0)),
            pl.BlockSpec((heads, LANES), lambda i: (0, 0)),
        ],
        out_specs=pl.BlockSpec((heads, block, length), lambda i: (0, i, 0)),
        out_shape=jax.ShapeDtypeStruct((heads, length, length), jnp.bfloat16),
        cost_estimate=pl.CostEstimate(
            flops=heads * length, bytes_accessed=heads * length, transcendentals=0
        ),
        name="expand_bias",
    )(buckets_t, table_rows)


def forward_kernel(block_cols, qkv_ref, bias_ref, context_ref, lse_ref):
    length = qkv_ref.shape[0]
    keys = qkv_ref[:, LANES : 2 * LANES]
    masks = head_masks(length)
    head_keys = [only_head(keep, keys) for keep in masks]
    values_t = qkv_ref[:, 2 * LANES :].T
    for start in range(0, length, block_cols):
        span = pl.ds(start, block_cols)
        queries = qkv_ref[span, :LANES]
        pieces = []
        for head in range(2):
            scores = nt_dot(head_keys[head], queries) + bias_ref[head, :, span].astype(
                jnp.float32
            )
            top = jnp.max(scores, axis=0, keepdims=True)
            shifted = jnp.exp(scores - top)
            total = jnp.sum(shifted, axis=0, keepdims=True)
            probs = (shifted * (1.0 / total)).astype(jnp.bfloat16)
            pieces.append(nn_dot(values_t[head * HD : (head + 1) * HD], probs))
            lse_ref[0, head : head + 1, span] = top + jnp.log(total)
        context_ref[span, :] = jnp.concatenate(pieces, axis=0).T.astype(jnp.bfloat16)


def attention_forward(qkv, bias_t):
    length = qkv.shape[0]
    pairs = qkv.shape[1] // (3 * LANES)
    heads = 2 * pairs
    return pl.pallas_call(
        functools.partial(forward_kernel, min(256, length)),
        grid=(pairs,),
        in_specs=[
            pl.BlockSpec((length, 3 * LANES), lambda p: (0, p)),
            pl.BlockSpec((2, length, length), lambda p: (p, 0, 0)),
        ],
        out_specs=[
            pl.BlockSpec((length, LANES), lambda p: (0, p)),
            pl.BlockSpec((1, 2, length), lambda p: (p, 0, 0)),
        ],
        out_shape=[
            jax.ShapeDtypeStruct((length, pairs * LANES), jnp.bfloat16),
            jax.ShapeDtypeStruct((pairs, 2, length), jnp.float32),
        ],
        compiler_params=pltpu.CompilerParams(vmem_limit_bytes=VMEM_ROOM),
        cost_estimate=pl.CostEstimate(
            flops=heads * length, bytes_accessed=heads * length, transcendentals=0
        ),
        name="attention_forward",
    )(qkv, bias_t)


def backward_kernel(
    block_cols, qkv_ref, grad_ref, bias_ref, lse_ref, out_ref, grad_scores_ref, dk_acc, dv_acc
):
    length = qkv_ref.shape[0]
    keys = qkv_ref[:, LANES : 2 * LANES]
    values = qkv_ref[:, 2 * LANES :]
    masks = head_masks(length)
    small_masks = head_masks(block_cols)
    head_keys = [only_head(keep, keys) for keep in masks]
    head_values = [only_head(keep, values) for keep in masks]
    keys_t = keys.T
    for start in range(0, length, block_cols):
        span = pl.ds(start, block_cols)
        queries = qkv_ref[span, :LANES]
        grads = grad_ref[span, :]
        pieces = []
        for head in range(2):
            scores = nt_dot(head_keys[head], queries) + bias_ref[head, :, span].astype(
                jnp.float32
            )
            probs = jnp.exp(scores - lse_ref[0, head : head + 1, span])
            grad_probs = nt_dot(head_values[head], grads)
            inner = jnp.sum(probs * grad_probs, axis=0, keepdims=True)
            grad_scores = (probs * (grad_probs - inner)).astype(jnp.bfloat16)
            grad_scores_ref[head, :, span] = grad_scores
            value_part = nn_dot(
                probs.astype(jnp.bfloat16), only_head(small_masks[head], grads)
            )
            key_part = nn_dot(grad_scores, only_head(small_masks[head], queries))
            if start == 0 and head == 0:
                dv_acc[...] = value_part
                dk_acc[...] = key_part
            else:
                dv_acc[...] += value_part
                dk_acc[...] += key_part
            pieces.append(nn_dot(keys_t[head * HD : (head + 1) * HD], grad_scores))
        out_ref[span, :LANES] = jnp.concatenate(pieces, axis=0).T.astype(jnp.bfloat16)
    out_ref[:, LANES : 2 * LANES] = dk_acc[...].astype(jnp.bfloat16)
    out_ref[:, 2 * LANES :] = dv_acc[...].astype(jnp.bfloat16)


def attention_backward(qkv, grad_context, bias_t, lse):
    length = qkv.shape[0]
    pairs = qkv.shape[1] // (3 * LANES)
    heads = 2 * pairs
    return pl.pallas_call(
        functools.partial(backward_kernel, min(256, length)),
        grid=(pairs,),
        in_specs=[
            pl.BlockSpec((length, 3 * LANES), lambda p: (0, p)),
            pl.BlockSpec((length, LANES), lambda p: (0, p)),
            pl.BlockSpec((2, length, length), lambda p: (p, 0, 0)),
            pl.BlockSpec((1, 2, length), lambda p: (p, 0, 0)),
        ],
        out_specs=[
            pl.BlockSpec((length, 3 * LANES), lambda p: (0, p)),
            pl.BlockSpec((2, length, length), lambda p: (p, 0, 0)),
        ],
        out_shape=[
            jax.ShapeDtypeStruct((length, pairs * 3 * LANES), jnp.bfloat16),
            jax.ShapeDtypeStruct((heads, length, length), jnp.bfloat16),
        ],
        scratch_shapes=[
            pltpu.VMEM((length, LANES), jnp.float32),
            pltpu.VMEM((length, LANES), jnp.float32),
        ],
        compiler_params=pltpu.CompilerParams(vmem_limit_bytes=VMEM_ROOM),
        cost_estimate=pl.CostEstimate(
            flops=heads * length, bytes_accessed=heads * length, transcendentals=0
        ),
        name="attention_backward",
    )(qkv, grad_context, bias_t, lse)


def histogram_kernel(bucket_count, group, buckets_ref, *refs):
    grads, (sums_ref, values) = refs[:-2], refs[-2:]
    heads, rows, cols = values.shape

    @pl.when(pl.program_id(0) == 0)
    def _():
        sums_ref[...] = jnp.zeros_like(sums_ref)

    total = grads[0][...].astype(jnp.float32)
    for other in grads[1:]:
        total = total + other[...].astype(jnp.float32)
    values[...] = total

    @pl.loop(0, bucket_count // group)
    def _(step):
        first = step * group
        acc = [[jnp.zeros((8, LANES), jnp.float32) for _ in range(heads)] for _ in range(group)]
        for row in range(0, rows, 8):
            for col in range(0, cols, LANES):
                ids = buckets_ref[row : row + 8, col : col + LANES]
                vals = [values[h, row : row + 8, col : col + LANES] for h in range(heads)]
                for j in range(group):
                    hit = ids == first + j
                    for h in range(heads):
                        acc[j][h] = acc[j][h] + jnp.where(hit, vals[h], 0.0)
        for j in range(group):
            for h in range(heads):
                sums_ref[h, first + j] += acc[j][h]


def bucket_sums(buckets_t, grad_scores, bucket_count):
    heads, length, _ = grad_scores[0].shape
    block = 32
    sums = pl.pallas_call(
        functools.partial(histogram_kernel, bucket_count, 4),
        grid=(length // block,),
        in_specs=[pl.BlockSpec((block, length), lambda i: (i, 0))]
        + [pl.BlockSpec((heads, block, length), lambda i: (0, i, 0))] * len(grad_scores),
        out_specs=pl.BlockSpec((heads, bucket_count, 8, LANES), lambda i: (0, 0, 0, 0)),
        out_shape=jax.ShapeDtypeStruct((heads, bucket_count, 8, LANES), jnp.float32),
        scratch_shapes=[pltpu.VMEM((heads, block, length), jnp.float32)],
        compiler_params=pltpu.CompilerParams(vmem_limit_bytes=VMEM_ROOM),
        cost_estimate=pl.CostEstimate(
            flops=heads * length, bytes_accessed=heads * length, transcendentals=0
        ),
        name="bucket_sums",
    )(buckets_t, *grad_scores)
    return jnp.sum(sums, axis=(2, 3)).T


def xor_pairs(count, mask):
    return [(i, i ^ mask) for i in range(count)]


def reorder(blocks, place):
    blocks = list(blocks)
    bit = 1
    while bit < len(blocks):
        flag = (place & bit) != 0
        blocks = [jnp.where(flag, blocks[i ^ bit], blocks[i]) for i in range(len(blocks))]
        bit *= 2
    return blocks


def rms_parts(seq_rows, gain_vec):
    inv_rms = lax.rsqrt(jnp.mean(seq_rows * seq_rows, axis=-1, keepdims=True) + norm_eps)
    plain_rows = seq_rows * inv_rms
    return (plain_rows, inv_rms, (plain_rows * gain_vec).astype(jnp.bfloat16))


def rms_back(grad_norm, plain_rows, inv_rms, gain_vec):
    scaled_grad = grad_norm * gain_vec
    return inv_rms * (
        scaled_grad - plain_rows * jnp.mean(scaled_grad * plain_rows, axis=-1, keepdims=True)
    )


def gelu_gate(gate_pre, up_pre):
    return jax.nn.gelu(gate_pre, approximate=True) * up_pre


def tn_dot(left, right):
    return lax.dot_general(
        left, right, (((0,), (0,)), ((), ())), preferred_element_type=jnp.float32
    )


def after(x, *needed):
    return lax.optimization_barrier((x, *needed))[0]


def make_body(dp_size, tensor_size):
    zs = tensor_size // 2
    z_groups = [[2 * z + core for z in range(zs)] for core in range(2)]
    core_pairs = xor_pairs(tensor_size, 1)

    def to_core(x):
        return lax.ppermute(x, "tensor", core_pairs)

    def to_dp(x, mask):
        return lax.ppermute(x, "dp", xor_pairs(dp_size, mask))

    def to_z(x, mask):
        return lax.ppermute(x, "tensor", xor_pairs(tensor_size, 2 * mask))

    def dp_relative(x):
        return [x] + [to_dp(x, k) for k in range(1, dp_size)]

    def exchange(send, pick, size):
        return [pick(0)] + [send(pick(k), k) for k in range(1, size)]

    def total_of(send, pick, size):
        own = pick(0).astype(jnp.float32)
        for k in range(1, size):
            own = own + send(pick(k).astype(jnp.bfloat16), k).astype(jnp.float32)
        return own

    def z_gather(x):
        return lax.all_gather(x, "tensor", axis=0, tiled=True, axis_index_groups=z_groups)

    def z_scatter(x):
        return lax.psum_scatter(
            x, "tensor", scatter_dimension=0, tiled=True, axis_index_groups=z_groups
        )

    def all_sum(x, dp_at, z_at, core_at):
        x = sum(reorder([x, to_core(x)], core_at))
        x = sum(reorder(exchange(to_z, lambda k: x, zs), z_at))
        return sum(reorder(dp_relative(x), dp_at))

    def body(
        hidden_in,
        out_grad,
        buckets,
        gain_attn,
        gain_ffn,
        w_query,
        w_key,
        w_value,
        w_out,
        w_gate,
        w_up,
        w_down,
        bias_table,
    ):
        dp_at = lax.axis_index("dp")
        tensor_at = lax.axis_index("tensor")
        core_at = tensor_at % 2
        z_at = tensor_at // 2
        seqs, rows, width = hidden_in.shape
        length = buckets.shape[0]
        feats = w_query.shape[0]
        inner = w_query.shape[1]
        heads = inner // HD
        pairs = inner // LANES
        ff = w_gate.shape[1]
        part = ff // dp_size
        table_rows = bias_table.shape[0]
        bucket_count = table_rows * dp_size
        gain_one = gain_attn.astype(jnp.float32)
        gain_two = gain_ffn.astype(jnp.float32)
        every = range(seqs)

        def feature_block(x, k):
            return lax.dynamic_slice_in_dim(x, (dp_at ^ k) * feats, feats, 1)

        x_rows = [hidden_in[s].astype(jnp.float32) for s in every]
        first_norm = [rms_parts(x, gain_one) for x in x_rows]
        norm_full = [
            lax.all_gather(first_norm[s][2], "tensor", axis=0, tiled=True) for s in every
        ]

        qkv_local = jnp.concatenate(
            [
                w[:, p * LANES : (p + 1) * LANES]
                for p in range(pairs)
                for w in (w_query, w_key, w_value)
            ],
            axis=1,
        )
        table = jnp.concatenate(reorder(dp_relative(bias_table), dp_at), axis=0)
        buckets_t = buckets.T
        bias_t = expand_bias(
            buckets_t,
            jnp.pad(table.astype(jnp.float32).T, ((0, 0), (0, LANES - bucket_count))),
        )
        payload = dp_relative(after(qkv_local, table))
        arrived = payload[1:]
        payload = after(tuple(payload), bias_t)
        w_qkv = jnp.concatenate(reorder(payload, dp_at), axis=0)

        out_z = tuple(exchange(to_z, lambda k: w_out, zs))
        first_qkv = nn_dot(after(norm_full[0], *out_z[1:]), w_qkv).astype(jnp.bfloat16)

        ffn_local = jnp.stack([w_gate.T, w_up.T, w_down]).reshape(3, dp_size, part, feats)
        ffn_local = after(ffn_local, *arrived)
        ffn_parts = exchange(
            to_dp,
            lambda k: lax.dynamic_index_in_dim(ffn_local, dp_at ^ k, 1, keepdims=False),
            dp_size,
        )
        arrived = ffn_parts[1:]
        ffn_parts = reorder(after(tuple(ffn_parts), first_qkv), dp_at)
        pre_rows = jnp.concatenate([p[:2] for p in ffn_parts], axis=2)
        post_rows = jnp.concatenate([p[2] for p in ffn_parts], axis=1)
        pre_rows = pre_rows.reshape(2 * part, width)
        pre_gathered = z_gather(pre_rows)

        out_rows = after(jnp.concatenate(reorder(out_z, z_at), axis=0), *arrived)

        def both_cores(blocks):
            own = jnp.concatenate(blocks, axis=0)
            return jnp.concatenate([own, to_core(own)], axis=0)

        def context_to_tokens(context):
            blocks = context.reshape(zs, 2, rows, inner)
            own = lax.dynamic_index_in_dim(blocks, core_at, 1, keepdims=False)
            got = to_core(lax.dynamic_index_in_dim(blocks, 1 - core_at, 1, keepdims=False))
            both = jnp.concatenate([own, got], axis=-1)
            swapped = got
            moved = exchange(
                to_z,
                lambda k: lax.dynamic_index_in_dim(both, z_at ^ k, 0, keepdims=False),
                zs,
            )
            moved = reorder(moved, z_at)
            return (
                jnp.concatenate([m[:, :inner] for m in moved], axis=1),
                jnp.concatenate([m[:, inner:] for m in moved], axis=1),
                swapped,
            )

        def send_tokens(own, other):
            got = to_core(other)
            pair = jnp.stack(reorder([own, got], core_at))
            moved = exchange(
                to_z,
                lambda k: lax.dynamic_slice_in_dim(pair, (z_at ^ k) * inner, inner, 2),
                zs,
            )
            return tuple(moved), got

        def take_tokens(moved):
            return jnp.stack(reorder(moved, z_at)).reshape(length, inner)

        qkv_all, lse_all, ctx_own, ctx_other, swaps = [], [], [], [], []
        mid_rows, second_norm, norm_two_full = [], [], []

        recent = []
        cot_full = []

        def feed_forward_input(s):
            own, other = ctx_own[s], ctx_other[s]
            if s == 1:
                own = after(own, *recent[-1])
            mid = x_rows[s] + (nn_dot(own, out_own) + nn_dot(other, out_other))
            mid_rows.append(mid)
            second_norm.append(rms_parts(mid, gain_two))
            normed = second_norm[s][2]
            normed = after(normed, *recent[-1])
            riders = [out_grad[t] for t in every if 1 <= s == t - 1]
            parts = dp_relative(jnp.concatenate([normed, *riders], axis=0))
            recent.append(parts[1:])
            norm_two_full.append(both_cores([x[:rows] for x in parts]))
            for i in range(1, len(riders) + 1):
                cot_full.append(both_cores([x[i * rows : (i + 1) * rows] for x in parts]))

        for s in every:
            if s == 0:
                qkv = first_qkv
            else:
                source = after(norm_full[s], swaps[s - 1])
                if s > 1:
                    source = after(source, second_norm[s - 2][2])
                if s == 1:
                    source = after(source, pre_rows)
                qkv = nn_dot(source, w_qkv).astype(jnp.bfloat16)
            context, lse = attention_forward(qkv, bias_t)
            if s == 0:
                post_gathered = z_gather(after(post_rows, context))
                out_parts = dp_relative(out_rows)
                early = dp_relative(
                    after(jnp.concatenate([out_grad[0], out_grad[1]], axis=0), context, *out_parts[1:])
                )
                recent.append(early[1:])
            if s == 1:
                out_parts = after(tuple(out_parts), context)
                out_own = jnp.concatenate(reorder(out_parts, dp_at), axis=1)
                out_other = to_core(out_own)
            if s == 1:
                taken = after(tuple(early), context)
                cot_full.append(both_cores([x[:rows] for x in taken]))
                cot_full.append(both_cores([x[rows:] for x in taken]))
            if s > 0:
                feed_forward_input(s - 1)
                context = after(context, second_norm[s - 1][2])
            own, other, swapped = context_to_tokens(context)
            qkv_all.append(qkv)
            lse_all.append(lse)
            ctx_own.append(own)
            ctx_other.append(other)
            swaps.append(swapped)
        feed_forward_input(seqs - 1)
        pre_gathered = after(pre_gathered, norm_two_full[-1])
        w_pre = jnp.transpose(
            pre_gathered.reshape(zs, 2, part, width), (1, 0, 2, 3)
        ).reshape(2 * ff, width)
        half = dp_size * rows
        first_parts, hidden_all = [], []
        grad_post = None
        for s in every:
            pre = nt_dot(norm_two_full[s], w_pre)
            hidden = gelu_gate(pre[:, :ff], pre[:, ff:]).astype(jnp.bfloat16)
            first_parts.append(pre)
            hidden_all.append(hidden)
            more = tn_dot(hidden, cot_full[s])
            grad_post = more if grad_post is None else grad_post + more
        grad_post = grad_post.astype(jnp.bfloat16)
        w_post = after(post_gathered, grad_post)
        post_z = z_scatter(grad_post)
        pre_all, kept, sums, swaps_in, sent_in = [], [], [], [], []
        ready = grad_post
        for s in every:
            pre = first_parts[s]
            _, pull = jax.vjp(gelu_gate, pre[:, :ff], pre[:, ff:])
            cot = after(cot_full[s], ready)
            if s > 1:
                cot = after(cot, *sums[s - 2])
            grad_gate, grad_up = pull(nt_dot(cot, w_post))
            grad_pre = jnp.concatenate([grad_gate, grad_up], axis=1).astype(jnp.bfloat16)
            ready = nn_dot(grad_pre, w_pre)
            got = to_core(ready[half:].astype(jnp.bfloat16))
            own = ready[:half] + got.astype(jnp.float32)
            blocks = [
                own[k * rows : (k + 1) * rows].astype(jnp.bfloat16) for k in range(1, dp_size)
            ]
            sent = [to_dp(blocks[k - 1], k) for k in range(1, dp_size)]
            kept.append(own[:rows])
            sums.append(blocks)
            swaps_in.append(got)
            sent_in.append(sent)
            pre_all.append(grad_pre)
        grad_mid, grad_mid_low, gain_two_sum = [], [], None
        moves, swapped_in, received = [], [], []
        grad_pre_w = None
        for s in every:
            grad_pre = after(pre_all[s], ready)
            if s == 0:
                grad_pre = after(grad_pre, *sums[1])
            else:
                grad_pre = after(grad_pre, swapped_in[s - 1], *sums[-1])
            if s == seqs - 1:
                grad_pre = after(grad_pre, post_z)
            more = tn_dot(grad_pre, norm_two_full[s])
            grad_pre_w = more if grad_pre_w is None else grad_pre_w + more
            if s == seqs - 1:
                grad_pre_w = grad_pre_w.astype(jnp.bfloat16)
                more = grad_pre_w
            sent = after(tuple(sent_in[s]), more)
            received.append(sent)
            grad_norm = kept[s] + sum(x.astype(jnp.float32) for x in sent)
            plain, inv, _ = second_norm[s]
            more = jnp.sum(grad_norm * plain, axis=0)
            gain_two_sum = more if gain_two_sum is None else gain_two_sum + more
            grad = out_grad[s].astype(jnp.float32) + rms_back(grad_norm, plain, inv, gain_two)
            grad_mid.append(grad)
            grad_mid_low.append(grad.astype(jnp.bfloat16))
            back_own = nt_dot(grad_mid_low[s], out_own).astype(jnp.bfloat16)
            back_other = nt_dot(grad_mid_low[s], out_other).astype(jnp.bfloat16)
            moved, got = send_tokens(back_own, back_other)
            moves.append(moved)
            swapped_in.append(got)
        pre_z = z_scatter(
            jnp.transpose(
                grad_pre_w.reshape(2, zs, part, width), (1, 0, 2, 3)
            ).reshape(zs * 2 * part, width)
        )

        hidden_own = jnp.concatenate([h[:half] for h in hidden_all], axis=0)
        hidden_other = jnp.concatenate([h[half:] for h in hidden_all], axis=0)
        hidden_own, hidden_other = (
            after(hidden_own, grad_pre_w),
            after(hidden_other, grad_pre_w),
        )
        sent = to_core(nn_dot(hidden_other, w_post).astype(jnp.bfloat16))
        own = nn_dot(after(hidden_own, *sent_in[-1]), w_post) + sent.astype(jnp.float32)
        own = own.reshape(seqs, dp_size, rows, width)
        out_blocks = [own[:, k].astype(jnp.bfloat16) for k in range(1, dp_size)]
        out_sent = [to_dp(out_blocks[k - 1], k) for k in range(1, dp_size)]
        ffn_own = own[:, 0]

        def ffn_send(z_rows):
            return tuple(exchange(to_dp, lambda k: feature_block(z_rows, k), dp_size))

        def ffn_take(moved, mats):
            moved = jnp.stack(reorder(moved, dp_at)).reshape(dp_size, mats, part, feats)
            return [moved[:, m].reshape(ff, feats).astype(jnp.float32) for m in range(mats)]

        post_moved = ffn_send(post_z)
        pre_moved = ffn_send(pre_z)
        grad_normed, grad_scores, normed_parts, qkv_grads = [], [], [], []
        grad_qkv = None
        gate = (grad_pre_w,)
        for s in every:
            moved = after(moves[s], *gate)
            if s < seqs - 1:
                moved = after(moved, swapped_in[s + 1])
            if s == 1:
                moved = after(moved, *out_blocks)
            if s == seqs - 1:
                moved = after(moved, *post_moved[1:], *out_give_dp)
            grad_proj, grad_score = attention_backward(
                qkv_all[s], take_tokens(moved), bias_t, lse_all[s]
            )
            grad_scores.append(grad_score)
            qkv_grads.append(grad_proj)
            ordered = grad_proj
            if s == 0:
                ordered = after(ordered, *sent_in[-1])
            if s == 1:
                ordered = after(ordered, *out_sent)
            if s == seqs - 1:
                ordered = after(ordered, *out_moved[1:])
            normed_part = nt_dot(ordered, w_qkv).astype(jnp.bfloat16)
            normed_parts.append(normed_part)
            gate = (normed_part,)
            grad_normed.append(
                lax.psum_scatter(
                    normed_part, "tensor", scatter_dimension=0, tiled=True
                ).astype(jnp.float32)
            )
            if s == 0:
                mid_low = after(jnp.concatenate(grad_mid_low, axis=0), normed_part)
                out_give = tn_dot(jnp.concatenate(ctx_other, axis=0), mid_low).astype(
                    jnp.bfloat16
                )
                out_got = to_core(out_give)
                out_keep = tn_dot(jnp.concatenate(ctx_own, axis=0), mid_low)
                gate = gate + (out_give, out_keep)
            else:
                for t in [0, 1] if s == 1 else [s]:
                    more = tn_dot(norm_full[t], after(qkv_grads[t], normed_part))
                    grad_qkv = more if grad_qkv is None else grad_qkv + more
                gate = gate + (grad_qkv,)
            if s == 1:
                out_sum = out_keep + after(out_got, normed_part).astype(jnp.float32)
                out_give_dp = [
                    feature_block(out_sum, k).astype(jnp.bfloat16) for k in range(1, dp_size)
                ]
                out_moved = (
                    feature_block(out_sum, 0),
                    *[to_dp(out_give_dp[k - 1], k) for k in range(1, dp_size)],
                )
        out_moved = after(out_moved, normed_parts[-1])
        grad_out_z = sum(m.astype(jnp.float32) for m in out_moved)
        grad_out_keep = lax.dynamic_slice_in_dim(grad_out_z, z_at * inner, inner, 0)
        grad_out_blocks = [
            lax.dynamic_slice_in_dim(grad_out_z, (z_at ^ k) * inner, inner, 0).astype(
                jnp.bfloat16
            )
            for k in range(1, zs)
        ]
        grad_out_sent = [to_z(grad_out_blocks[k - 1], k) for k in range(1, zs)]
        qkv_blocks = [
            lax.dynamic_slice_in_dim(grad_qkv, (dp_at ^ k) * feats, feats, 0).astype(
                jnp.bfloat16
            )
            for k in range(1, dp_size)
        ]
        qkv_sent = [to_dp(qkv_blocks[k - 1], k) for k in range(1, dp_size)]
        bucket_gate = after(
            buckets_t, *pre_moved[1:], *grad_out_blocks, *qkv_blocks, grad_normed[0]
        )
        table_grad = bucket_sums(bucket_gate, grad_scores, bucket_count)
        grad_out = grad_out_keep + sum(
            x.astype(jnp.float32) for x in after(tuple(grad_out_sent), table_grad)
        )
        summed = lax.dynamic_slice_in_dim(grad_qkv, dp_at * feats, feats, 0) + sum(
            x.astype(jnp.float32) for x in after(tuple(qkv_sent), table_grad)
        )
        ffn_out = ffn_own + sum(
            m.astype(jnp.float32) for m in after(tuple(out_sent), normed_parts[-1])
        )
        output = jnp.stack(
            [(mid_rows[s] + ffn_out[s]).astype(jnp.bfloat16) for s in every]
        )

        (grad_down,) = ffn_take(post_moved, 1)
        grad_gate_t, grad_up_t = ffn_take(pre_moved, 2)

        def columns(which):
            return jnp.concatenate(
                [
                    summed[:, (3 * p + which) * LANES : (3 * p + which + 1) * LANES]
                    for p in range(pairs)
                ],
                axis=1,
            )

        grad_table = total_of(
            to_dp,
            lambda k: lax.dynamic_slice_in_dim(
                table_grad, (dp_at ^ k) * table_rows, table_rows, 0
            ),
            dp_size,
        )

        grad_in, gain_one_sum = [], None
        for s in every:
            plain, inv, _ = first_norm[s]
            more = jnp.sum(grad_normed[s] * plain, axis=0)
            gain_one_sum = more if gain_one_sum is None else gain_one_sum + more
            grad_in.append(
                (grad_mid[s] + rms_back(grad_normed[s], plain, inv, gain_one)).astype(
                    jnp.bfloat16
                )
            )
        gains = all_sum(jnp.stack([gain_one_sum, gain_two_sum]), dp_at, z_at, core_at)
        return (
            output,
            jnp.stack(grad_in),
            gains[0],
            gains[1],
            columns(0),
            columns(1),
            columns(2),
            grad_out,
            grad_gate_t.T,
            grad_up_t.T,
            grad_down,
            grad_table,
        )

    return body


def solution(mesh):
    in_specs = (
        P("dp", "tensor", None),
        P("dp", "tensor", None),
        P(),
        P(),
        P(),
        P("dp", "tensor"),
        P("dp", "tensor"),
        P("dp", "tensor"),
        P("tensor", "dp"),
        P("dp", "tensor"),
        P("dp", "tensor"),
        P("tensor", "dp"),
        P("dp", "tensor"),
    )
    out_specs = (
        P("dp", "tensor", None),
        P("dp", "tensor", None),
        P(),
        P(),
        P("dp", "tensor"),
        P("dp", "tensor"),
        P("dp", "tensor"),
        P("tensor", "dp"),
        P("dp", "tensor"),
        P("dp", "tensor"),
        P("tensor", "dp"),
        P("dp", "tensor"),
    )
    body = make_body(mesh.shape["dp"], mesh.shape["tensor"])
    return jax.shard_map(body, mesh=mesh, in_specs=in_specs, out_specs=out_specs, check_vma=False)
```

```python
import functools
import jax
import jax.numpy as jnp
from jax import lax
from jax.experimental import pallas as pl
from jax.experimental.pallas import tpu as pltpu
from jax.sharding import PartitionSpec as P

HD = 64
LANES = 128
norm_eps = 1e-06
VMEM_ROOM = 50 * 1024 * 1024


def nt_dot(left, right):
    return lax.dot_general(
        left, right, (((1,), (1,)), ((), ())), preferred_element_type=jnp.float32
    )


def nn_dot(left, right):
    return jnp.dot(left, right, preferred_element_type=jnp.float32)


def head_masks(rows):
    lane = lax.broadcasted_iota(jnp.int32, (rows, LANES), 1)
    return (lane < HD, lane >= HD)


def only_head(keep, pair_cols):
    return jnp.where(keep, pair_cols, jnp.zeros_like(pair_cols))


def expand_kernel(buckets_ref, table_ref, bias_ref):
    heads = table_ref.shape[0]
    rows, cols = buckets_ref.shape
    for col in range(0, cols, LANES):
        ids = buckets_ref[:, col : col + LANES]
        for head in range(heads):
            row = jnp.broadcast_to(table_ref[head : head + 1, :], (rows, LANES))
            bias_ref[head, :, col : col + LANES] = jnp.take_along_axis(
                row, ids, axis=1
            ).astype(jnp.bfloat16)


def expand_bias(buckets_t, table_rows):
    length = buckets_t.shape[0]
    heads = table_rows.shape[0]
    block = 64
    return pl.pallas_call(
        expand_kernel,
        grid=(length // block,),
        in_specs=[
            pl.BlockSpec((block, length), lambda i: (i, 0)),
            pl.BlockSpec((heads, LANES), lambda i: (0, 0)),
        ],
        out_specs=pl.BlockSpec((heads, block, length), lambda i: (0, i, 0)),
        out_shape=jax.ShapeDtypeStruct((heads, length, length), jnp.bfloat16),
        cost_estimate=pl.CostEstimate(
            flops=heads * length, bytes_accessed=heads * length, transcendentals=0
        ),
        name="expand_bias",
    )(buckets_t, table_rows)


def forward_kernel(block_cols, qkv_ref, bias_ref, context_ref, lse_ref):
    length = qkv_ref.shape[0]
    keys = qkv_ref[:, LANES : 2 * LANES]
    masks = head_masks(length)
    head_keys = [only_head(keep, keys) for keep in masks]
    values_t = qkv_ref[:, 2 * LANES :].T
    for start in range(0, length, block_cols):
        span = pl.ds(start, block_cols)
        queries = qkv_ref[span, :LANES]
        pieces = []
        for head in range(2):
            scores = nt_dot(head_keys[head], queries) + bias_ref[head, :, span].astype(
                jnp.float32
            )
            top = jnp.max(scores, axis=0, keepdims=True)
            shifted = jnp.exp(scores - top)
            total = jnp.sum(shifted, axis=0, keepdims=True)
            probs = (shifted * (1.0 / total)).astype(jnp.bfloat16)
            pieces.append(nn_dot(values_t[head * HD : (head + 1) * HD], probs))
            lse_ref[0, head : head + 1, span] = top + jnp.log(total)
        context_ref[span, :] = jnp.concatenate(pieces, axis=0).T.astype(jnp.bfloat16)


def attention_forward(qkv, bias_t):
    length = qkv.shape[0]
    pairs = qkv.shape[1] // (3 * LANES)
    heads = 2 * pairs
    return pl.pallas_call(
        functools.partial(forward_kernel, min(256, length)),
        grid=(pairs,),
        in_specs=[
            pl.BlockSpec((length, 3 * LANES), lambda p: (0, p)),
            pl.BlockSpec((2, length, length), lambda p: (p, 0, 0)),
        ],
        out_specs=[
            pl.BlockSpec((length, LANES), lambda p: (0, p)),
            pl.BlockSpec((1, 2, length), lambda p: (p, 0, 0)),
        ],
        out_shape=[
            jax.ShapeDtypeStruct((length, pairs * LANES), jnp.bfloat16),
            jax.ShapeDtypeStruct((pairs, 2, length), jnp.float32),
        ],
        compiler_params=pltpu.CompilerParams(vmem_limit_bytes=VMEM_ROOM),
        cost_estimate=pl.CostEstimate(
            flops=heads * length, bytes_accessed=heads * length, transcendentals=0
        ),
        name="attention_forward",
    )(qkv, bias_t)


def backward_kernel(
    block_cols, qkv_ref, grad_ref, bias_ref, lse_ref, out_ref, grad_scores_ref, dk_acc, dv_acc
):
    length = qkv_ref.shape[0]
    keys = qkv_ref[:, LANES : 2 * LANES]
    values = qkv_ref[:, 2 * LANES :]
    masks = head_masks(length)
    small_masks = head_masks(block_cols)
    head_keys = [only_head(keep, keys) for keep in masks]
    head_values = [only_head(keep, values) for keep in masks]
    keys_t = keys.T
    for start in range(0, length, block_cols):
        span = pl.ds(start, block_cols)
        queries = qkv_ref[span, :LANES]
        grads = grad_ref[span, :]
        pieces = []
        for head in range(2):
            scores = nt_dot(head_keys[head], queries) + bias_ref[head, :, span].astype(
                jnp.float32
            )
            probs = jnp.exp(scores - lse_ref[0, head : head + 1, span])
            grad_probs = nt_dot(head_values[head], grads)
            inner = jnp.sum(probs * grad_probs, axis=0, keepdims=True)
            grad_scores = (probs * (grad_probs - inner)).astype(jnp.bfloat16)
            grad_scores_ref[head, :, span] = grad_scores
            value_part = nn_dot(
                probs.astype(jnp.bfloat16), only_head(small_masks[head], grads)
            )
            key_part = nn_dot(grad_scores, only_head(small_masks[head], queries))
            if start == 0 and head == 0:
                dv_acc[...] = value_part
                dk_acc[...] = key_part
            else:
                dv_acc[...] += value_part
                dk_acc[...] += key_part
            pieces.append(nn_dot(keys_t[head * HD : (head + 1) * HD], grad_scores))
        out_ref[span, :LANES] = jnp.concatenate(pieces, axis=0).T.astype(jnp.bfloat16)
    out_ref[:, LANES : 2 * LANES] = dk_acc[...].astype(jnp.bfloat16)
    out_ref[:, 2 * LANES :] = dv_acc[...].astype(jnp.bfloat16)


def attention_backward(qkv, grad_context, bias_t, lse):
    length = qkv.shape[0]
    pairs = qkv.shape[1] // (3 * LANES)
    heads = 2 * pairs
    return pl.pallas_call(
        functools.partial(backward_kernel, min(256, length)),
        grid=(pairs,),
        in_specs=[
            pl.BlockSpec((length, 3 * LANES), lambda p: (0, p)),
            pl.BlockSpec((length, LANES), lambda p: (0, p)),
            pl.BlockSpec((2, length, length), lambda p: (p, 0, 0)),
            pl.BlockSpec((1, 2, length), lambda p: (p, 0, 0)),
        ],
        out_specs=[
            pl.BlockSpec((length, 3 * LANES), lambda p: (0, p)),
            pl.BlockSpec((2, length, length), lambda p: (p, 0, 0)),
        ],
        out_shape=[
            jax.ShapeDtypeStruct((length, pairs * 3 * LANES), jnp.bfloat16),
            jax.ShapeDtypeStruct((heads, length, length), jnp.bfloat16),
        ],
        scratch_shapes=[
            pltpu.VMEM((length, LANES), jnp.float32),
            pltpu.VMEM((length, LANES), jnp.float32),
        ],
        compiler_params=pltpu.CompilerParams(vmem_limit_bytes=VMEM_ROOM),
        cost_estimate=pl.CostEstimate(
            flops=heads * length, bytes_accessed=heads * length, transcendentals=0
        ),
        name="attention_backward",
    )(qkv, grad_context, bias_t, lse)


def histogram_kernel(bucket_count, group, buckets_ref, *refs):
    grads, (sums_ref, values) = refs[:-2], refs[-2:]
    heads, rows, cols = values.shape

    @pl.when(pl.program_id(0) == 0)
    def _():
        sums_ref[...] = jnp.zeros_like(sums_ref)

    total = grads[0][...].astype(jnp.float32)
    for other in grads[1:]:
        total = total + other[...].astype(jnp.float32)
    values[...] = total

    @pl.loop(0, bucket_count // group)
    def _(step):
        first = step * group
        acc = [[jnp.zeros((8, LANES), jnp.float32) for _ in range(heads)] for _ in range(group)]
        for row in range(0, rows, 8):
            for col in range(0, cols, LANES):
                ids = buckets_ref[row : row + 8, col : col + LANES]
                vals = [values[h, row : row + 8, col : col + LANES] for h in range(heads)]
                for j in range(group):
                    hit = ids == first + j
                    for h in range(heads):
                        acc[j][h] = acc[j][h] + jnp.where(hit, vals[h], 0.0)
        for j in range(group):
            for h in range(heads):
                sums_ref[h, first + j] += acc[j][h]


def bucket_sums(buckets_t, grad_scores, bucket_count):
    heads, length, _ = grad_scores[0].shape
    block = 32
    sums = pl.pallas_call(
        functools.partial(histogram_kernel, bucket_count, 4),
        grid=(length // block,),
        in_specs=[pl.BlockSpec((block, length), lambda i: (i, 0))]
        + [pl.BlockSpec((heads, block, length), lambda i: (0, i, 0))] * len(grad_scores),
        out_specs=pl.BlockSpec((heads, bucket_count, 8, LANES), lambda i: (0, 0, 0, 0)),
        out_shape=jax.ShapeDtypeStruct((heads, bucket_count, 8, LANES), jnp.float32),
        scratch_shapes=[pltpu.VMEM((heads, block, length), jnp.float32)],
        compiler_params=pltpu.CompilerParams(vmem_limit_bytes=VMEM_ROOM),
        cost_estimate=pl.CostEstimate(
            flops=heads * length, bytes_accessed=heads * length, transcendentals=0
        ),
        name="bucket_sums",
    )(buckets_t, *grad_scores)
    return jnp.sum(sums, axis=(2, 3)).T


def xor_pairs(count, mask):
    return [(i, i ^ mask) for i in range(count)]


def reorder(blocks, place):
    blocks = list(blocks)
    bit = 1
    while bit < len(blocks):
        flag = (place & bit) != 0
        blocks = [jnp.where(flag, blocks[i ^ bit], blocks[i]) for i in range(len(blocks))]
        bit *= 2
    return blocks


def rms_parts(seq_rows, gain_vec):
    inv_rms = lax.rsqrt(jnp.mean(seq_rows * seq_rows, axis=-1, keepdims=True) + norm_eps)
    plain_rows = seq_rows * inv_rms
    return (plain_rows, inv_rms, (plain_rows * gain_vec).astype(jnp.bfloat16))


def rms_back(grad_norm, plain_rows, inv_rms, gain_vec):
    scaled_grad = grad_norm * gain_vec
    return inv_rms * (
        scaled_grad - plain_rows * jnp.mean(scaled_grad * plain_rows, axis=-1, keepdims=True)
    )


def gelu_gate(gate_pre, up_pre):
    return jax.nn.gelu(gate_pre, approximate=True) * up_pre


def tn_dot(left, right):
    return lax.dot_general(
        left, right, (((0,), (0,)), ((), ())), preferred_element_type=jnp.float32
    )


def after(x, *needed):
    return lax.optimization_barrier((x, *needed))[0]


def make_body(dp_size, tensor_size):
    zs = tensor_size // 2
    z_groups = [[2 * z + core for z in range(zs)] for core in range(2)]
    core_pairs = xor_pairs(tensor_size, 1)

    def to_core(x):
        return lax.ppermute(x, "tensor", core_pairs)

    def to_dp(x, mask):
        return lax.ppermute(x, "dp", xor_pairs(dp_size, mask))

    def to_z(x, mask):
        return lax.ppermute(x, "tensor", xor_pairs(tensor_size, 2 * mask))

    def dp_relative(x):
        return [x] + [to_dp(x, k) for k in range(1, dp_size)]

    def exchange(send, pick, size):
        return [pick(0)] + [send(pick(k), k) for k in range(1, size)]

    def total_of(send, pick, size):
        own = pick(0).astype(jnp.float32)
        for k in range(1, size):
            own = own + send(pick(k).astype(jnp.bfloat16), k).astype(jnp.float32)
        return own

    def z_gather(x):
        return lax.all_gather(x, "tensor", axis=0, tiled=True, axis_index_groups=z_groups)

    def z_scatter(x):
        return lax.psum_scatter(
            x, "tensor", scatter_dimension=0, tiled=True, axis_index_groups=z_groups
        )

    def all_sum(x, dp_at, z_at, core_at):
        x = sum(reorder([x, to_core(x)], core_at))
        x = sum(reorder(exchange(to_z, lambda k: x, zs), z_at))
        return sum(reorder(dp_relative(x), dp_at))

    def body(
        hidden_in,
        out_grad,
        buckets,
        gain_attn,
        gain_ffn,
        w_query,
        w_key,
        w_value,
        w_out,
        w_gate,
        w_up,
        w_down,
        bias_table,
    ):
        dp_at = lax.axis_index("dp")
        tensor_at = lax.axis_index("tensor")
        core_at = tensor_at % 2
        z_at = tensor_at // 2
        seqs, rows, width = hidden_in.shape
        length = buckets.shape[0]
        feats = w_query.shape[0]
        inner = w_query.shape[1]
        heads = inner // HD
        pairs = inner // LANES
        ff = w_gate.shape[1]
        part = ff // dp_size
        table_rows = bias_table.shape[0]
        bucket_count = table_rows * dp_size
        gain_one = gain_attn.astype(jnp.float32)
        gain_two = gain_ffn.astype(jnp.float32)
        every = range(seqs)

        def feature_block(x, k):
            return lax.dynamic_slice_in_dim(x, (dp_at ^ k) * feats, feats, 1)

        x_rows = [hidden_in[s].astype(jnp.float32) for s in every]
        first_norm = [rms_parts(x, gain_one) for x in x_rows]
        norm_full = [
            lax.all_gather(first_norm[s][2], "tensor", axis=0, tiled=True) for s in every
        ]

        qkv_local = jnp.concatenate(
            [
                w[:, p * LANES : (p + 1) * LANES]
                for p in range(pairs)
                for w in (w_query, w_key, w_value)
            ],
            axis=1,
        )
        table = jnp.concatenate(reorder(dp_relative(bias_table), dp_at), axis=0)
        buckets_t = buckets.T
        bias_t = expand_bias(
            buckets_t,
            jnp.pad(table.astype(jnp.float32).T, ((0, 0), (0, LANES - bucket_count))),
        )
        payload = dp_relative(after(qkv_local, table))
        arrived = payload[1:]
        payload = after(tuple(payload), bias_t)
        w_qkv = jnp.concatenate(reorder(payload, dp_at), axis=0)

        out_z = tuple(exchange(to_z, lambda k: w_out, zs))
        first_qkv = nn_dot(after(norm_full[0], *out_z[1:]), w_qkv).astype(jnp.bfloat16)

        ffn_local = jnp.stack([w_gate.T, w_up.T, w_down]).reshape(3, dp_size, part, feats)
        ffn_local = after(ffn_local, *arrived)
        ffn_parts = exchange(
            to_dp,
            lambda k: lax.dynamic_index_in_dim(ffn_local, dp_at ^ k, 1, keepdims=False),
            dp_size,
        )
        arrived = ffn_parts[1:]
        ffn_parts = reorder(after(tuple(ffn_parts), first_qkv), dp_at)
        pre_rows = jnp.concatenate([p[:2] for p in ffn_parts], axis=2)
        post_rows = jnp.concatenate([p[2] for p in ffn_parts], axis=1)
        pre_rows = pre_rows.reshape(2 * part, width)
        pre_gathered = z_gather(pre_rows)

        out_rows = after(jnp.concatenate(reorder(out_z, z_at), axis=0), *arrived)

        def both_cores(blocks):
            own = jnp.concatenate(blocks, axis=0)
            return jnp.concatenate([own, to_core(own)], axis=0)

        def context_to_tokens(context):
            blocks = context.reshape(zs, 2, rows, inner)
            own = lax.dynamic_index_in_dim(blocks, core_at, 1, keepdims=False)
            got = to_core(lax.dynamic_index_in_dim(blocks, 1 - core_at, 1, keepdims=False))
            both = jnp.concatenate([own, got], axis=-1)
            swapped = got
            moved = exchange(
                to_z,
                lambda k: lax.dynamic_index_in_dim(both, z_at ^ k, 0, keepdims=False),
                zs,
            )
            moved = reorder(moved, z_at)
            return (
                jnp.concatenate([m[:, :inner] for m in moved], axis=1),
                jnp.concatenate([m[:, inner:] for m in moved], axis=1),
                swapped,
            )

        def send_tokens(own, other):
            got = to_core(other)
            pair = jnp.stack(reorder([own, got], core_at))
            moved = exchange(
                to_z,
                lambda k: lax.dynamic_slice_in_dim(pair, (z_at ^ k) * inner, inner, 2),
                zs,
            )
            return tuple(moved), got

        def take_tokens(moved):
            return jnp.stack(reorder(moved, z_at)).reshape(length, inner)

        qkv_all, lse_all, ctx_own, ctx_other, swaps = [], [], [], [], []
        mid_rows, second_norm, norm_two_full = [], [], []

        early = dp_relative(after(out_grad.reshape(seqs * rows, width), *arrived))
        for s in every:
            if s == 0:
                qkv = first_qkv
            else:
                source = after(norm_full[s], swaps[s - 1])
                if s == 1:
                    source = after(source, pre_rows)
                qkv = nn_dot(source, w_qkv).astype(jnp.bfloat16)
            context, lse = attention_forward(qkv, bias_t)
            if s == 0:
                post_gathered = z_gather(after(post_rows, context))
            if s == min(1, seqs - 1):
                out_parts = dp_relative(after(out_rows, context, *early[1:]))
            own, other, swapped = context_to_tokens(context)
            qkv_all.append(qkv)
            lse_all.append(lse)
            ctx_own.append(own)
            ctx_other.append(other)
            swaps.append(swapped)
        out_parts = after(tuple(out_parts), context)
        out_own = jnp.concatenate(reorder(out_parts, dp_at), axis=1)
        out_other = to_core(out_own)
        for s in every:
            own, other = ctx_own[s], ctx_other[s]
            mid = x_rows[s] + (nn_dot(own, out_own) + nn_dot(other, out_other))
            mid_rows.append(mid)
            second_norm.append(rms_parts(mid, gain_two))
            norm_two_full.append(both_cores(dp_relative(second_norm[s][2])))
        taken = after(tuple(early), second_norm[-1][2])
        cot_full = [
            both_cores([x[s * rows : (s + 1) * rows] for x in taken]) for s in every
        ]
        pre_gathered = after(pre_gathered, norm_two_full[-1])
        w_pre = jnp.transpose(
            pre_gathered.reshape(zs, 2, part, width), (1, 0, 2, 3)
        ).reshape(2 * ff, width)
        half = dp_size * rows
        first_parts, hidden_all = [], []
        grad_post = None
        for s in every:
            pre = nt_dot(norm_two_full[s], w_pre)
            hidden = gelu_gate(pre[:, :ff], pre[:, ff:]).astype(jnp.bfloat16)
            first_parts.append(pre)
            hidden_all.append(hidden)
            more = tn_dot(hidden, cot_full[s])
            grad_post = more if grad_post is None else grad_post + more
        grad_post = grad_post.astype(jnp.bfloat16)
        w_post = after(post_gathered, grad_post)
        post_z = z_scatter(grad_post)
        pre_all, kept, sums, swaps_in, sent_in = [], [], [], [], []
        ready = grad_post
        for s in every:
            pre = first_parts[s]
            _, pull = jax.vjp(gelu_gate, pre[:, :ff], pre[:, ff:])
            cot = after(cot_full[s], ready)
            if s > 1:
                cot = after(cot, *sums[s - 2])
            grad_gate, grad_up = pull(nt_dot(cot, w_post))
            grad_pre = jnp.concatenate([grad_gate, grad_up], axis=1).astype(jnp.bfloat16)
            ready = nn_dot(grad_pre, w_pre)
            got = to_core(ready[half:].astype(jnp.bfloat16))
            own = ready[:half] + got.astype(jnp.float32)
            blocks = [
                own[k * rows : (k + 1) * rows].astype(jnp.bfloat16) for k in range(1, dp_size)
            ]
            sent = [to_dp(blocks[k - 1], k) for k in range(1, dp_size)]
            kept.append(own[:rows])
            sums.append(blocks)
            swaps_in.append(got)
            sent_in.append(sent)
            pre_all.append(grad_pre)
        grad_mid, grad_mid_low, gain_two_sum = [], [], None
        moves, swapped_in, received = [], [], []
        grad_pre_w = None
        for s in every:
            grad_pre = after(pre_all[s], ready)
            if s == 0:
                grad_pre = after(grad_pre, *sums[1])
            else:
                grad_pre = after(grad_pre, swapped_in[s - 1], *sums[-1])
            if s == seqs - 1:
                grad_pre = after(grad_pre, post_z, *moves[0][1:])
            more = tn_dot(grad_pre, norm_two_full[s])
            grad_pre_w = more if grad_pre_w is None else grad_pre_w + more
            if s == seqs - 1:
                grad_pre_w = grad_pre_w.astype(jnp.bfloat16)
                more = grad_pre_w
            sent = after(tuple(sent_in[s]), more)
            received.append(sent)
            grad_norm = kept[s] + sum(x.astype(jnp.float32) for x in sent)
            plain, inv, _ = second_norm[s]
            more = jnp.sum(grad_norm * plain, axis=0)
            gain_two_sum = more if gain_two_sum is None else gain_two_sum + more
            grad = out_grad[s].astype(jnp.float32) + rms_back(grad_norm, plain, inv, gain_two)
            grad_mid.append(grad)
            grad_mid_low.append(grad.astype(jnp.bfloat16))
            back_own = nt_dot(grad_mid_low[s], out_own).astype(jnp.bfloat16)
            back_other = nt_dot(grad_mid_low[s], out_other).astype(jnp.bfloat16)
            moved, got = send_tokens(back_own, back_other)
            moves.append(moved)
            swapped_in.append(got)
        pre_z = z_scatter(
            jnp.transpose(
                grad_pre_w.reshape(2, zs, part, width), (1, 0, 2, 3)
            ).reshape(zs * 2 * part, width)
        )

        hidden_own = jnp.concatenate([h[:half] for h in hidden_all], axis=0)
        hidden_other = jnp.concatenate([h[half:] for h in hidden_all], axis=0)
        hidden_own, hidden_other = (
            after(hidden_own, grad_pre_w),
            after(hidden_other, grad_pre_w),
        )
        sent = to_core(nn_dot(hidden_other, w_post).astype(jnp.bfloat16))
        own = nn_dot(after(hidden_own, *sent_in[-1]), w_post) + sent.astype(jnp.float32)
        own = own.reshape(seqs, dp_size, rows, width)
        out_blocks = [own[:, k].astype(jnp.bfloat16) for k in range(1, dp_size)]
        out_sent = [to_dp(out_blocks[k - 1], k) for k in range(1, dp_size)]
        ffn_own = own[:, 0]

        def ffn_send(z_rows):
            return tuple(exchange(to_dp, lambda k: feature_block(z_rows, k), dp_size))

        def ffn_take(moved, mats):
            moved = jnp.stack(reorder(moved, dp_at)).reshape(dp_size, mats, part, feats)
            return [moved[:, m].reshape(ff, feats).astype(jnp.float32) for m in range(mats)]

        post_moved = ffn_send(post_z)
        pre_moved = ffn_send(pre_z)
        grad_normed, grad_scores, normed_parts, qkv_grads = [], [], [], []
        grad_qkv = None
        gate = (grad_pre_w,)
        for s in every:
            moved = after(moves[s], *gate)
            if s < seqs - 1:
                moved = after(moved, swapped_in[s + 1])
            if s == 1:
                moved = after(moved, *out_blocks)
            if s == seqs - 1:
                moved = after(moved, *post_moved[1:], *out_give_dp)
            grad_proj, grad_score = attention_backward(
                qkv_all[s], take_tokens(moved), bias_t, lse_all[s]
            )
            grad_scores.append(grad_score)
            qkv_grads.append(grad_proj)
            ordered = grad_proj
            if s == 0:
                ordered = after(ordered, *sent_in[-1])
            if s == 1:
                ordered = after(ordered, *out_sent)
            if s == seqs - 1:
                ordered = after(ordered, *out_moved[1:])
            normed_part = nt_dot(ordered, w_qkv).astype(jnp.bfloat16)
            normed_parts.append(normed_part)
            gate = (normed_part,)
            grad_normed.append(
                lax.psum_scatter(
                    normed_part, "tensor", scatter_dimension=0, tiled=True
                ).astype(jnp.float32)
            )
            if s == 0:
                mid_low = after(jnp.concatenate(grad_mid_low, axis=0), normed_part)
                out_give = tn_dot(jnp.concatenate(ctx_other, axis=0), mid_low).astype(
                    jnp.bfloat16
                )
                out_got = to_core(out_give)
                out_keep = tn_dot(jnp.concatenate(ctx_own, axis=0), mid_low)
                gate = gate + (out_give, out_keep)
            else:
                for t in [0, 1] if s == 1 else [s]:
                    more = tn_dot(norm_full[t], after(qkv_grads[t], normed_part))
                    grad_qkv = more if grad_qkv is None else grad_qkv + more
                gate = gate + (grad_qkv,)
            if s == 1:
                out_sum = out_keep + after(out_got, normed_part).astype(jnp.float32)
                out_give_dp = [
                    feature_block(out_sum, k).astype(jnp.bfloat16) for k in range(1, dp_size)
                ]
                out_moved = (
                    feature_block(out_sum, 0),
                    *[to_dp(out_give_dp[k - 1], k) for k in range(1, dp_size)],
                )
        out_moved = after(out_moved, normed_parts[-1])
        grad_out_z = sum(m.astype(jnp.float32) for m in out_moved)
        grad_out_keep = lax.dynamic_slice_in_dim(grad_out_z, z_at * inner, inner, 0)
        grad_out_blocks = [
            lax.dynamic_slice_in_dim(grad_out_z, (z_at ^ k) * inner, inner, 0).astype(
                jnp.bfloat16
            )
            for k in range(1, zs)
        ]
        grad_out_sent = [to_z(grad_out_blocks[k - 1], k) for k in range(1, zs)]
        qkv_blocks = [
            lax.dynamic_slice_in_dim(grad_qkv, (dp_at ^ k) * feats, feats, 0).astype(
                jnp.bfloat16
            )
            for k in range(1, dp_size)
        ]
        qkv_sent = [to_dp(qkv_blocks[k - 1], k) for k in range(1, dp_size)]
        bucket_gate = after(
            buckets_t, *pre_moved[1:], *grad_out_blocks, *qkv_blocks, grad_normed[0]
        )
        table_grad = bucket_sums(bucket_gate, grad_scores, bucket_count)
        grad_out = grad_out_keep + sum(
            x.astype(jnp.float32) for x in after(tuple(grad_out_sent), table_grad)
        )
        summed = lax.dynamic_slice_in_dim(grad_qkv, dp_at * feats, feats, 0) + sum(
            x.astype(jnp.float32) for x in after(tuple(qkv_sent), table_grad)
        )
        ffn_out = ffn_own + sum(
            m.astype(jnp.float32) for m in after(tuple(out_sent), normed_parts[-1])
        )
        output = jnp.stack(
            [(mid_rows[s] + ffn_out[s]).astype(jnp.bfloat16) for s in every]
        )

        (grad_down,) = ffn_take(post_moved, 1)
        grad_gate_t, grad_up_t = ffn_take(pre_moved, 2)

        def columns(which):
            return jnp.concatenate(
                [
                    summed[:, (3 * p + which) * LANES : (3 * p + which + 1) * LANES]
                    for p in range(pairs)
                ],
                axis=1,
            )

        grad_table = total_of(
            to_dp,
            lambda k: lax.dynamic_slice_in_dim(
                table_grad, (dp_at ^ k) * table_rows, table_rows, 0
            ),
            dp_size,
        )

        grad_in, gain_one_sum = [], None
        for s in every:
            plain, inv, _ = first_norm[s]
            more = jnp.sum(grad_normed[s] * plain, axis=0)
            gain_one_sum = more if gain_one_sum is None else gain_one_sum + more
            grad_in.append(
                (grad_mid[s] + rms_back(grad_normed[s], plain, inv, gain_one)).astype(
                    jnp.bfloat16
                )
            )
        gains = all_sum(jnp.stack([gain_one_sum, gain_two_sum]), dp_at, z_at, core_at)
        return (
            output,
            jnp.stack(grad_in),
            gains[0],
            gains[1],
            columns(0),
            columns(1),
            columns(2),
            grad_out,
            grad_gate_t.T,
            grad_up_t.T,
            grad_down,
            grad_table,
        )

    return body


def solution(mesh):
    in_specs = (
        P("dp", "tensor", None),
        P("dp", "tensor", None),
        P(),
        P(),
        P(),
        P("dp", "tensor"),
        P("dp", "tensor"),
        P("dp", "tensor"),
        P("tensor", "dp"),
        P("dp", "tensor"),
        P("dp", "tensor"),
        P("tensor", "dp"),
        P("dp", "tensor"),
    )
    out_specs = (
        P("dp", "tensor", None),
        P("dp", "tensor", None),
        P(),
        P(),
        P("dp", "tensor"),
        P("dp", "tensor"),
        P("dp", "tensor"),
        P("tensor", "dp"),
        P("dp", "tensor"),
        P("dp", "tensor"),
        P("tensor", "dp"),
        P("dp", "tensor"),
    )
    body = make_body(mesh.shape["dp"], mesh.shape["tensor"])
    return jax.shard_map(body, mesh=mesh, in_specs=in_specs, out_specs=out_specs, check_vma=False)
```

```python
import functools
import jax
import jax.numpy as jnp
from jax import lax
from jax.experimental import pallas as pl
from jax.experimental.pallas import tpu as pltpu
from jax.sharding import PartitionSpec as P

HD = 64
LANES = 128
norm_eps = 1e-06
VMEM_ROOM = 50 * 1024 * 1024


def nt_dot(left, right):
    return lax.dot_general(
        left, right, (((1,), (1,)), ((), ())), preferred_element_type=jnp.float32
    )


def nn_dot(left, right):
    return jnp.dot(left, right, preferred_element_type=jnp.float32)


def head_masks(rows):
    lane = lax.broadcasted_iota(jnp.int32, (rows, LANES), 1)
    return (lane < HD, lane >= HD)


def only_head(keep, pair_cols):
    return jnp.where(keep, pair_cols, jnp.zeros_like(pair_cols))


def expand_kernel(buckets_ref, table_ref, bias_ref):
    heads = table_ref.shape[0]
    rows, cols = buckets_ref.shape
    for col in range(0, cols, LANES):
        ids = buckets_ref[:, col : col + LANES]
        for head in range(heads):
            row = jnp.broadcast_to(table_ref[head : head + 1, :], (rows, LANES))
            bias_ref[head, :, col : col + LANES] = jnp.take_along_axis(
                row, ids, axis=1
            ).astype(jnp.bfloat16)


def expand_bias(buckets_t, table_rows):
    length = buckets_t.shape[0]
    heads = table_rows.shape[0]
    block = 64
    return pl.pallas_call(
        expand_kernel,
        grid=(length // block,),
        in_specs=[
            pl.BlockSpec((block, length), lambda i: (i, 0)),
            pl.BlockSpec((heads, LANES), lambda i: (0, 0)),
        ],
        out_specs=pl.BlockSpec((heads, block, length), lambda i: (0, i, 0)),
        out_shape=jax.ShapeDtypeStruct((heads, length, length), jnp.bfloat16),
        cost_estimate=pl.CostEstimate(
            flops=heads * length, bytes_accessed=heads * length, transcendentals=0
        ),
        name="expand_bias",
    )(buckets_t, table_rows)


def forward_kernel(block_cols, qkv_ref, bias_ref, context_ref, lse_ref):
    length = qkv_ref.shape[0]
    keys = qkv_ref[:, LANES : 2 * LANES]
    masks = head_masks(length)
    head_keys = [only_head(keep, keys) for keep in masks]
    values_t = qkv_ref[:, 2 * LANES :].T
    for start in range(0, length, block_cols):
        span = pl.ds(start, block_cols)
        queries = qkv_ref[span, :LANES]
        pieces = []
        for head in range(2):
            scores = nt_dot(head_keys[head], queries) + bias_ref[head, :, span].astype(
                jnp.float32
            )
            top = jnp.max(scores, axis=0, keepdims=True)
            shifted = jnp.exp(scores - top)
            total = jnp.sum(shifted, axis=0, keepdims=True)
            probs = (shifted * (1.0 / total)).astype(jnp.bfloat16)
            pieces.append(nn_dot(values_t[head * HD : (head + 1) * HD], probs))
            lse_ref[0, head : head + 1, span] = top + jnp.log(total)
        context_ref[span, :] = jnp.concatenate(pieces, axis=0).T.astype(jnp.bfloat16)


def attention_forward(qkv, bias_t):
    length = qkv.shape[0]
    pairs = qkv.shape[1] // (3 * LANES)
    heads = 2 * pairs
    return pl.pallas_call(
        functools.partial(forward_kernel, min(256, length)),
        grid=(pairs,),
        in_specs=[
            pl.BlockSpec((length, 3 * LANES), lambda p: (0, p)),
            pl.BlockSpec((2, length, length), lambda p: (p, 0, 0)),
        ],
        out_specs=[
            pl.BlockSpec((length, LANES), lambda p: (0, p)),
            pl.BlockSpec((1, 2, length), lambda p: (p, 0, 0)),
        ],
        out_shape=[
            jax.ShapeDtypeStruct((length, pairs * LANES), jnp.bfloat16),
            jax.ShapeDtypeStruct((pairs, 2, length), jnp.float32),
        ],
        compiler_params=pltpu.CompilerParams(vmem_limit_bytes=VMEM_ROOM),
        cost_estimate=pl.CostEstimate(
            flops=heads * length, bytes_accessed=heads * length, transcendentals=0
        ),
        name="attention_forward",
    )(qkv, bias_t)


def backward_kernel(
    block_cols, qkv_ref, grad_ref, bias_ref, lse_ref, out_ref, grad_scores_ref, dk_acc, dv_acc
):
    length = qkv_ref.shape[0]
    keys = qkv_ref[:, LANES : 2 * LANES]
    values = qkv_ref[:, 2 * LANES :]
    masks = head_masks(length)
    small_masks = head_masks(block_cols)
    head_keys = [only_head(keep, keys) for keep in masks]
    head_values = [only_head(keep, values) for keep in masks]
    keys_t = keys.T
    for start in range(0, length, block_cols):
        span = pl.ds(start, block_cols)
        queries = qkv_ref[span, :LANES]
        grads = grad_ref[span, :]
        pieces = []
        for head in range(2):
            scores = nt_dot(head_keys[head], queries) + bias_ref[head, :, span].astype(
                jnp.float32
            )
            probs = jnp.exp(scores - lse_ref[0, head : head + 1, span])
            grad_probs = nt_dot(head_values[head], grads)
            inner = jnp.sum(probs * grad_probs, axis=0, keepdims=True)
            grad_scores = (probs * (grad_probs - inner)).astype(jnp.bfloat16)
            grad_scores_ref[head, :, span] = grad_scores
            value_part = nn_dot(
                probs.astype(jnp.bfloat16), only_head(small_masks[head], grads)
            )
            key_part = nn_dot(grad_scores, only_head(small_masks[head], queries))
            if start == 0 and head == 0:
                dv_acc[...] = value_part
                dk_acc[...] = key_part
            else:
                dv_acc[...] += value_part
                dk_acc[...] += key_part
            pieces.append(nn_dot(keys_t[head * HD : (head + 1) * HD], grad_scores))
        out_ref[span, :LANES] = jnp.concatenate(pieces, axis=0).T.astype(jnp.bfloat16)
    out_ref[:, LANES : 2 * LANES] = dk_acc[...].astype(jnp.bfloat16)
    out_ref[:, 2 * LANES :] = dv_acc[...].astype(jnp.bfloat16)


def attention_backward(qkv, grad_context, bias_t, lse):
    length = qkv.shape[0]
    pairs = qkv.shape[1] // (3 * LANES)
    heads = 2 * pairs
    return pl.pallas_call(
        functools.partial(backward_kernel, min(256, length)),
        grid=(pairs,),
        in_specs=[
            pl.BlockSpec((length, 3 * LANES), lambda p: (0, p)),
            pl.BlockSpec((length, LANES), lambda p: (0, p)),
            pl.BlockSpec((2, length, length), lambda p: (p, 0, 0)),
            pl.BlockSpec((1, 2, length), lambda p: (p, 0, 0)),
        ],
        out_specs=[
            pl.BlockSpec((length, 3 * LANES), lambda p: (0, p)),
            pl.BlockSpec((2, length, length), lambda p: (p, 0, 0)),
        ],
        out_shape=[
            jax.ShapeDtypeStruct((length, pairs * 3 * LANES), jnp.bfloat16),
            jax.ShapeDtypeStruct((heads, length, length), jnp.bfloat16),
        ],
        scratch_shapes=[
            pltpu.VMEM((length, LANES), jnp.float32),
            pltpu.VMEM((length, LANES), jnp.float32),
        ],
        compiler_params=pltpu.CompilerParams(vmem_limit_bytes=VMEM_ROOM),
        cost_estimate=pl.CostEstimate(
            flops=heads * length, bytes_accessed=heads * length, transcendentals=0
        ),
        name="attention_backward",
    )(qkv, grad_context, bias_t, lse)


def histogram_kernel(bucket_count, group, buckets_ref, *refs):
    grads, (sums_ref, values) = refs[:-2], refs[-2:]
    heads, rows, cols = values.shape

    @pl.when(pl.program_id(0) == 0)
    def _():
        sums_ref[...] = jnp.zeros_like(sums_ref)

    total = grads[0][...].astype(jnp.float32)
    for other in grads[1:]:
        total = total + other[...].astype(jnp.float32)
    values[...] = total

    @pl.loop(0, bucket_count // group)
    def _(step):
        first = step * group
        acc = [[jnp.zeros((8, LANES), jnp.float32) for _ in range(heads)] for _ in range(group)]
        for row in range(0, rows, 8):
            for col in range(0, cols, LANES):
                ids = buckets_ref[row : row + 8, col : col + LANES]
                vals = [values[h, row : row + 8, col : col + LANES] for h in range(heads)]
                for j in range(group):
                    hit = ids == first + j
                    for h in range(heads):
                        acc[j][h] = acc[j][h] + jnp.where(hit, vals[h], 0.0)
        for j in range(group):
            for h in range(heads):
                sums_ref[h, first + j] += acc[j][h]


def bucket_sums(buckets_t, grad_scores, bucket_count):
    heads, length, _ = grad_scores[0].shape
    block = 32
    sums = pl.pallas_call(
        functools.partial(histogram_kernel, bucket_count, 4),
        grid=(length // block,),
        in_specs=[pl.BlockSpec((block, length), lambda i: (i, 0))]
        + [pl.BlockSpec((heads, block, length), lambda i: (0, i, 0))] * len(grad_scores),
        out_specs=pl.BlockSpec((heads, bucket_count, 8, LANES), lambda i: (0, 0, 0, 0)),
        out_shape=jax.ShapeDtypeStruct((heads, bucket_count, 8, LANES), jnp.float32),
        scratch_shapes=[pltpu.VMEM((heads, block, length), jnp.float32)],
        compiler_params=pltpu.CompilerParams(vmem_limit_bytes=VMEM_ROOM),
        cost_estimate=pl.CostEstimate(
            flops=heads * length, bytes_accessed=heads * length, transcendentals=0
        ),
        name="bucket_sums",
    )(buckets_t, *grad_scores)
    return jnp.sum(sums, axis=(2, 3)).T


def xor_pairs(count, mask):
    return [(i, i ^ mask) for i in range(count)]


def reorder(blocks, place):
    blocks = list(blocks)
    bit = 1
    while bit < len(blocks):
        flag = (place & bit) != 0
        blocks = [jnp.where(flag, blocks[i ^ bit], blocks[i]) for i in range(len(blocks))]
        bit *= 2
    return blocks


def rms_parts(seq_rows, gain_vec):
    inv_rms = lax.rsqrt(jnp.mean(seq_rows * seq_rows, axis=-1, keepdims=True) + norm_eps)
    plain_rows = seq_rows * inv_rms
    return (plain_rows, inv_rms, (plain_rows * gain_vec).astype(jnp.bfloat16))


def rms_back(grad_norm, plain_rows, inv_rms, gain_vec):
    scaled_grad = grad_norm * gain_vec
    return inv_rms * (
        scaled_grad - plain_rows * jnp.mean(scaled_grad * plain_rows, axis=-1, keepdims=True)
    )


def gelu_gate(gate_pre, up_pre):
    return jax.nn.gelu(gate_pre, approximate=True) * up_pre


def tn_dot(left, right):
    return lax.dot_general(
        left, right, (((0,), (0,)), ((), ())), preferred_element_type=jnp.float32
    )


def after(x, *needed):
    return lax.optimization_barrier((x, *needed))[0]


def make_body(dp_size, tensor_size):
    zs = tensor_size // 2
    z_groups = [[2 * z + core for z in range(zs)] for core in range(2)]
    core_pairs = xor_pairs(tensor_size, 1)

    def to_core(x):
        return lax.ppermute(x, "tensor", core_pairs)

    def to_dp(x, mask):
        return lax.ppermute(x, "dp", xor_pairs(dp_size, mask))

    def to_z(x, mask):
        return lax.ppermute(x, "tensor", xor_pairs(tensor_size, 2 * mask))

    def dp_relative(x):
        return [x] + [to_dp(x, k) for k in range(1, dp_size)]

    def exchange(send, pick, size):
        return [pick(0)] + [send(pick(k), k) for k in range(1, size)]

    def total_of(send, pick, size):
        own = pick(0).astype(jnp.float32)
        for k in range(1, size):
            own = own + send(pick(k).astype(jnp.bfloat16), k).astype(jnp.float32)
        return own

    def z_gather(x):
        return lax.all_gather(x, "tensor", axis=0, tiled=True, axis_index_groups=z_groups)

    def z_scatter(x):
        return lax.psum_scatter(
            x, "tensor", scatter_dimension=0, tiled=True, axis_index_groups=z_groups
        )

    def all_sum(x, dp_at, z_at, core_at):
        x = sum(reorder([x, to_core(x)], core_at))
        x = sum(reorder(exchange(to_z, lambda k: x, zs), z_at))
        return sum(reorder(dp_relative(x), dp_at))

    def body(
        hidden_in,
        out_grad,
        buckets,
        gain_attn,
        gain_ffn,
        w_query,
        w_key,
        w_value,
        w_out,
        w_gate,
        w_up,
        w_down,
        bias_table,
    ):
        dp_at = lax.axis_index("dp")
        tensor_at = lax.axis_index("tensor")
        core_at = tensor_at % 2
        z_at = tensor_at // 2
        seqs, rows, width = hidden_in.shape
        length = buckets.shape[0]
        feats = w_query.shape[0]
        inner = w_query.shape[1]
        heads = inner // HD
        pairs = inner // LANES
        ff = w_gate.shape[1]
        part = ff // dp_size
        table_rows = bias_table.shape[0]
        bucket_count = table_rows * dp_size
        gain_one = gain_attn.astype(jnp.float32)
        gain_two = gain_ffn.astype(jnp.float32)
        every = range(seqs)

        def feature_block(x, k):
            return lax.dynamic_slice_in_dim(x, (dp_at ^ k) * feats, feats, 1)

        x_rows = [hidden_in[s].astype(jnp.float32) for s in every]
        first_norm = [rms_parts(x, gain_one) for x in x_rows]
        norm_full = [
            lax.all_gather(first_norm[s][2], "tensor", axis=0, tiled=True) for s in every
        ]

        qkv_local = jnp.concatenate(
            [
                w[:, p * LANES : (p + 1) * LANES]
                for p in range(pairs)
                for w in (w_query, w_key, w_value)
            ],
            axis=1,
        )
        table = jnp.concatenate(reorder(dp_relative(bias_table), dp_at), axis=0)
        buckets_t = buckets.T
        bias_t = expand_bias(
            buckets_t,
            jnp.pad(table.astype(jnp.float32).T, ((0, 0), (0, LANES - bucket_count))),
        )
        payload = dp_relative(after(qkv_local, table))
        arrived = payload[1:]
        payload = after(tuple(payload), bias_t)
        w_qkv = jnp.concatenate(reorder(payload, dp_at), axis=0)

        out_z = tuple(exchange(to_z, lambda k: w_out, zs))
        first_qkv = nn_dot(after(norm_full[0], *out_z[1:]), w_qkv).astype(jnp.bfloat16)

        ffn_local = jnp.stack([w_gate.T, w_up.T, w_down]).reshape(3, dp_size, part, feats)
        ffn_local = after(ffn_local, *arrived)
        ffn_parts = exchange(
            to_dp,
            lambda k: lax.dynamic_index_in_dim(ffn_local, dp_at ^ k, 1, keepdims=False),
            dp_size,
        )
        arrived = ffn_parts[1:]
        ffn_parts = reorder(after(tuple(ffn_parts), first_qkv), dp_at)
        pre_rows = jnp.concatenate([p[:2] for p in ffn_parts], axis=2)
        post_rows = jnp.concatenate([p[2] for p in ffn_parts], axis=1)
        pre_rows = pre_rows.reshape(2 * part, width)
        pre_gathered = z_gather(pre_rows)

        out_rows = after(jnp.concatenate(reorder(out_z, z_at), axis=0), *arrived)

        def both_cores(blocks):
            own = jnp.concatenate(blocks, axis=0)
            return jnp.concatenate([own, to_core(own)], axis=0)

        def context_to_tokens(context):
            blocks = context.reshape(zs, 2, rows, inner)
            own = lax.dynamic_index_in_dim(blocks, core_at, 1, keepdims=False)
            got = to_core(lax.dynamic_index_in_dim(blocks, 1 - core_at, 1, keepdims=False))
            both = jnp.concatenate([own, got], axis=-1)
            swapped = got
            moved = exchange(
                to_z,
                lambda k: lax.dynamic_index_in_dim(both, z_at ^ k, 0, keepdims=False),
                zs,
            )
            moved = reorder(moved, z_at)
            return (
                jnp.concatenate([m[:, :inner] for m in moved], axis=1),
                jnp.concatenate([m[:, inner:] for m in moved], axis=1),
                swapped,
            )

        def send_tokens(own, other):
            got = to_core(other)
            pair = jnp.stack(reorder([own, got], core_at))
            moved = exchange(
                to_z,
                lambda k: lax.dynamic_slice_in_dim(pair, (z_at ^ k) * inner, inner, 2),
                zs,
            )
            return tuple(moved), got

        def take_tokens(moved):
            return jnp.stack(reorder(moved, z_at)).reshape(length, inner)

        qkv_all, lse_all, ctx_own, ctx_other, swaps = [], [], [], [], []
        mid_rows, second_norm, norm_two_full = [], [], []

        recent = []
        cot_full = []

        def feed_forward_input(s):
            own, other = ctx_own[s], ctx_other[s]
            if s == 1:
                own = after(own, *recent[-1])
            mid = x_rows[s] + (nn_dot(own, out_own) + nn_dot(other, out_other))
            mid_rows.append(mid)
            second_norm.append(rms_parts(mid, gain_two))
            normed = second_norm[s][2]
            normed = after(normed, *recent[-1])
            riders = [out_grad[t] for t in every if 1 <= s == t - 1]
            parts = dp_relative(jnp.concatenate([normed, *riders], axis=0))
            recent.append(parts[1:])
            norm_two_full.append(both_cores([x[:rows] for x in parts]))
            for i in range(1, len(riders) + 1):
                cot_full.append(both_cores([x[i * rows : (i + 1) * rows] for x in parts]))

        for s in every:
            if s == 0:
                qkv = first_qkv
            else:
                source = after(norm_full[s], swaps[s - 1])
                if s > 1:
                    source = after(source, second_norm[s - 2][2])
                if s == 1:
                    source = after(source, pre_rows)
                qkv = nn_dot(source, w_qkv).astype(jnp.bfloat16)
            context, lse = attention_forward(qkv, bias_t)
            if s == 0:
                post_gathered = z_gather(after(post_rows, context))
                out_parts = dp_relative(out_rows)
                early = dp_relative(
                    after(jnp.concatenate([out_grad[0], out_grad[1]], axis=0), context, *out_parts[1:])
                )
                recent.append(early[1:])
            if s == 1:
                out_parts = after(tuple(out_parts), context)
                out_own = jnp.concatenate(reorder(out_parts, dp_at), axis=1)
                out_other = to_core(out_own)
            if s == 1:
                taken = after(tuple(early), context)
                cot_full.append(both_cores([x[:rows] for x in taken]))
                cot_full.append(both_cores([x[rows:] for x in taken]))
            if s > 0:
                feed_forward_input(s - 1)
                context = after(context, second_norm[s - 1][2])
            own, other, swapped = context_to_tokens(context)
            qkv_all.append(qkv)
            lse_all.append(lse)
            ctx_own.append(own)
            ctx_other.append(other)
            swaps.append(swapped)
        feed_forward_input(seqs - 1)
        pre_gathered = after(pre_gathered, norm_two_full[-1])
        w_pre = jnp.transpose(
            pre_gathered.reshape(zs, 2, part, width), (1, 0, 2, 3)
        ).reshape(2 * ff, width)
        half = dp_size * rows
        first_parts, hidden_all = [], []
        grad_post = None
        for s in every:
            pre = nt_dot(norm_two_full[s], w_pre)
            hidden = gelu_gate(pre[:, :ff], pre[:, ff:]).astype(jnp.bfloat16)
            first_parts.append(pre)
            hidden_all.append(hidden)
            more = tn_dot(hidden, cot_full[s])
            grad_post = more if grad_post is None else grad_post + more
        grad_post = grad_post.astype(jnp.bfloat16)
        w_post = after(post_gathered, grad_post)
        post_z = z_scatter(grad_post)
        pre_all, kept, sums, swaps_in, sent_in = [], [], [], [], []
        ready = grad_post
        for s in every:
            pre = first_parts[s]
            _, pull = jax.vjp(gelu_gate, pre[:, :ff], pre[:, ff:])
            cot = after(cot_full[s], ready)
            if s > 1:
                cot = after(cot, *sums[s - 2])
            grad_gate, grad_up = pull(nt_dot(cot, w_post))
            grad_pre = jnp.concatenate([grad_gate, grad_up], axis=1).astype(jnp.bfloat16)
            ready = nn_dot(grad_pre, w_pre)
            got = to_core(ready[half:].astype(jnp.bfloat16))
            own = ready[:half] + got.astype(jnp.float32)
            blocks = [
                own[k * rows : (k + 1) * rows].astype(jnp.bfloat16) for k in range(1, dp_size)
            ]
            sent = [to_dp(blocks[k - 1], k) for k in range(1, dp_size)]
            kept.append(own[:rows])
            sums.append(blocks)
            swaps_in.append(got)
            sent_in.append(sent)
            pre_all.append(grad_pre)
        grad_mid, grad_mid_low, gain_two_sum = [], [], None
        moves, swapped_in, received = [], [], []
        grad_pre_w = None
        for s in every:
            grad_pre = after(pre_all[s], ready)
            if s == 0:
                grad_pre = after(grad_pre, *sums[1])
            else:
                grad_pre = after(grad_pre, swapped_in[s - 1], *sums[-1])
            if s == seqs - 1:
                grad_pre = after(grad_pre, post_z, *moves[0][1:], *sent_in[-1])
            more = tn_dot(grad_pre, norm_two_full[s])
            grad_pre_w = more if grad_pre_w is None else grad_pre_w + more
            if s == seqs - 1:
                grad_pre_w = grad_pre_w.astype(jnp.bfloat16)
                more = grad_pre_w
            sent = after(tuple(sent_in[s]), more)
            received.append(sent)
            grad_norm = kept[s] + sum(x.astype(jnp.float32) for x in sent)
            plain, inv, _ = second_norm[s]
            more = jnp.sum(grad_norm * plain, axis=0)
            gain_two_sum = more if gain_two_sum is None else gain_two_sum + more
            grad = out_grad[s].astype(jnp.float32) + rms_back(grad_norm, plain, inv, gain_two)
            grad_mid.append(grad)
            grad_mid_low.append(grad.astype(jnp.bfloat16))
            back_own = nt_dot(grad_mid_low[s], out_own).astype(jnp.bfloat16)
            back_other = nt_dot(grad_mid_low[s], out_other).astype(jnp.bfloat16)
            moved, got = send_tokens(back_own, back_other)
            moves.append(moved)
            swapped_in.append(got)
        pre_z = z_scatter(
            jnp.transpose(
                grad_pre_w.reshape(2, zs, part, width), (1, 0, 2, 3)
            ).reshape(zs * 2 * part, width)
        )

        hidden_own = jnp.concatenate([h[:half] for h in hidden_all], axis=0)
        hidden_other = jnp.concatenate([h[half:] for h in hidden_all], axis=0)
        hidden_own, hidden_other = (
            after(hidden_own, grad_pre_w),
            after(hidden_other, grad_pre_w),
        )
        sent = to_core(nn_dot(hidden_other, w_post).astype(jnp.bfloat16))
        own = nn_dot(after(hidden_own, *sent_in[-1]), w_post) + sent.astype(jnp.float32)
        own = own.reshape(seqs, dp_size, rows, width)
        out_blocks = [own[:, k].astype(jnp.bfloat16) for k in range(1, dp_size)]
        out_sent = [to_dp(out_blocks[k - 1], k) for k in range(1, dp_size)]
        ffn_own = own[:, 0]

        def ffn_send(z_rows):
            return tuple(exchange(to_dp, lambda k: feature_block(z_rows, k), dp_size))

        def ffn_take(moved, mats):
            moved = jnp.stack(reorder(moved, dp_at)).reshape(dp_size, mats, part, feats)
            return [moved[:, m].reshape(ff, feats).astype(jnp.float32) for m in range(mats)]

        post_moved = ffn_send(post_z)
        pre_moved = ffn_send(pre_z)
        grad_normed, grad_scores, normed_parts, qkv_grads = [], [], [], []
        grad_qkv = None
        gate = (grad_pre_w,)
        for s in every:
            moved = after(moves[s], *gate)
            if s < seqs - 1:
                moved = after(moved, swapped_in[s + 1])
            if s == 0:
                moved = after(moved, *out_blocks)
            if s == seqs - 1:
                moved = after(moved, *post_moved[1:], *out_give_dp)
            grad_proj, grad_score = attention_backward(
                qkv_all[s], take_tokens(moved), bias_t, lse_all[s]
            )
            grad_scores.append(grad_score)
            qkv_grads.append(grad_proj)
            ordered = grad_proj
            if s == 1:
                ordered = after(ordered, *out_sent)
            if s == seqs - 1:
                ordered = after(ordered, *out_moved[1:], *pre_moved[1:])
            normed_part = nt_dot(ordered, w_qkv).astype(jnp.bfloat16)
            normed_parts.append(normed_part)
            gate = (normed_part,)
            grad_normed.append(
                lax.psum_scatter(
                    normed_part, "tensor", scatter_dimension=0, tiled=True
                ).astype(jnp.float32)
            )
            if s == 0:
                mid_low = after(jnp.concatenate(grad_mid_low, axis=0), normed_part)
                out_give = tn_dot(jnp.concatenate(ctx_other, axis=0), mid_low).astype(
                    jnp.bfloat16
                )
                out_got = to_core(out_give)
                out_keep = tn_dot(jnp.concatenate(ctx_own, axis=0), mid_low)
                gate = gate + (out_give, out_keep)
            else:
                for t in [0, 1] if s == 1 else [s]:
                    more = tn_dot(norm_full[t], after(qkv_grads[t], normed_part))
                    grad_qkv = more if grad_qkv is None else grad_qkv + more
                gate = gate + (grad_qkv,)
            if s == 1:
                out_sum = out_keep + after(out_got, normed_part).astype(jnp.float32)
                out_give_dp = [
                    feature_block(out_sum, k).astype(jnp.bfloat16) for k in range(1, dp_size)
                ]
                out_moved = (
                    feature_block(out_sum, 0),
                    *[to_dp(out_give_dp[k - 1], k) for k in range(1, dp_size)],
                )
        out_moved = after(out_moved, normed_parts[-1])
        grad_out_z = sum(m.astype(jnp.float32) for m in out_moved)
        grad_out_keep = lax.dynamic_slice_in_dim(grad_out_z, z_at * inner, inner, 0)
        grad_out_blocks = [
            lax.dynamic_slice_in_dim(grad_out_z, (z_at ^ k) * inner, inner, 0).astype(
                jnp.bfloat16
            )
            for k in range(1, zs)
        ]
        qkv_blocks = [
            lax.dynamic_slice_in_dim(grad_qkv, (dp_at ^ k) * feats, feats, 0).astype(
                jnp.bfloat16
            )
            for k in range(1, dp_size)
        ]
        qkv_sent = [to_dp(qkv_blocks[k - 1], k) for k in range(1, dp_size)]
        grad_out_sent = [to_z(grad_out_blocks[k - 1], k) for k in range(1, zs)]
        bucket_gate = after(buckets_t, *grad_out_blocks, *qkv_blocks, grad_normed[0])
        table_grad = bucket_sums(bucket_gate, grad_scores, bucket_count)
        grad_out = grad_out_keep + sum(
            x.astype(jnp.float32) for x in after(tuple(grad_out_sent), table_grad)
        )
        summed = lax.dynamic_slice_in_dim(grad_qkv, dp_at * feats, feats, 0) + sum(
            x.astype(jnp.float32) for x in after(tuple(qkv_sent), table_grad)
        )
        ffn_out = ffn_own + sum(
            m.astype(jnp.float32) for m in after(tuple(out_sent), normed_parts[-1])
        )
        output = jnp.stack(
            [(mid_rows[s] + ffn_out[s]).astype(jnp.bfloat16) for s in every]
        )

        (grad_down,) = ffn_take(post_moved, 1)
        grad_gate_t, grad_up_t = ffn_take(pre_moved, 2)

        def columns(which):
            return jnp.concatenate(
                [
                    summed[:, (3 * p + which) * LANES : (3 * p + which + 1) * LANES]
                    for p in range(pairs)
                ],
                axis=1,
            )

        grad_table = total_of(
            to_dp,
            lambda k: lax.dynamic_slice_in_dim(
                table_grad, (dp_at ^ k) * table_rows, table_rows, 0
            ),
            dp_size,
        )

        grad_in, gain_one_sum = [], None
        for s in every:
            plain, inv, _ = first_norm[s]
            more = jnp.sum(grad_normed[s] * plain, axis=0)
            gain_one_sum = more if gain_one_sum is None else gain_one_sum + more
            grad_in.append(
                (grad_mid[s] + rms_back(grad_normed[s], plain, inv, gain_one)).astype(
                    jnp.bfloat16
                )
            )
        gains = all_sum(jnp.stack([gain_one_sum, gain_two_sum]), dp_at, z_at, core_at)
        return (
            output,
            jnp.stack(grad_in),
            gains[0],
            gains[1],
            columns(0),
            columns(1),
            columns(2),
            grad_out,
            grad_gate_t.T,
            grad_up_t.T,
            grad_down,
            grad_table,
        )

    return body


def solution(mesh):
    in_specs = (
        P("dp", "tensor", None),
        P("dp", "tensor", None),
        P(),
        P(),
        P(),
        P("dp", "tensor"),
        P("dp", "tensor"),
        P("dp", "tensor"),
        P("tensor", "dp"),
        P("dp", "tensor"),
        P("dp", "tensor"),
        P("tensor", "dp"),
        P("dp", "tensor"),
    )
    out_specs = (
        P("dp", "tensor", None),
        P("dp", "tensor", None),
        P(),
        P(),
        P("dp", "tensor"),
        P("dp", "tensor"),
        P("dp", "tensor"),
        P("tensor", "dp"),
        P("dp", "tensor"),
        P("dp", "tensor"),
        P("tensor", "dp"),
        P("dp", "tensor"),
    )
    body = make_body(mesh.shape["dp"], mesh.shape["tensor"])
    return jax.shard_map(body, mesh=mesh, in_specs=in_specs, out_specs=out_specs, check_vma=False)
```

```python
import functools
import jax
import jax.numpy as jnp
from jax import lax
from jax.experimental import pallas as pl
from jax.experimental.pallas import tpu as pltpu
from jax.sharding import PartitionSpec as P

HD = 64
LANES = 128
norm_eps = 1e-06
VMEM_ROOM = 50 * 1024 * 1024


def nt_dot(left, right):
    return lax.dot_general(
        left, right, (((1,), (1,)), ((), ())), preferred_element_type=jnp.float32
    )


def nn_dot(left, right):
    return jnp.dot(left, right, preferred_element_type=jnp.float32)


def head_masks(rows):
    lane = lax.broadcasted_iota(jnp.int32, (rows, LANES), 1)
    return (lane < HD, lane >= HD)


def only_head(keep, pair_cols):
    return jnp.where(keep, pair_cols, jnp.zeros_like(pair_cols))


def expand_kernel(buckets_ref, table_ref, bias_ref):
    heads = table_ref.shape[0]
    rows, cols = buckets_ref.shape
    for col in range(0, cols, LANES):
        ids = buckets_ref[:, col : col + LANES]
        for head in range(heads):
            row = jnp.broadcast_to(table_ref[head : head + 1, :], (rows, LANES))
            bias_ref[head, :, col : col + LANES] = jnp.take_along_axis(
                row, ids, axis=1
            ).astype(jnp.bfloat16)


def expand_bias(buckets_t, table_rows):
    length = buckets_t.shape[0]
    heads = table_rows.shape[0]
    block = 64
    return pl.pallas_call(
        expand_kernel,
        grid=(length // block,),
        in_specs=[
            pl.BlockSpec((block, length), lambda i: (i, 0)),
            pl.BlockSpec((heads, LANES), lambda i: (0, 0)),
        ],
        out_specs=pl.BlockSpec((heads, block, length), lambda i: (0, i, 0)),
        out_shape=jax.ShapeDtypeStruct((heads, length, length), jnp.bfloat16),
        cost_estimate=pl.CostEstimate(
            flops=heads * length, bytes_accessed=heads * length, transcendentals=0
        ),
        name="expand_bias",
    )(buckets_t, table_rows)


def forward_kernel(block_cols, qkv_ref, bias_ref, context_ref, lse_ref):
    length = qkv_ref.shape[0]
    keys = qkv_ref[:, LANES : 2 * LANES]
    masks = head_masks(length)
    head_keys = [only_head(keep, keys) for keep in masks]
    values_t = qkv_ref[:, 2 * LANES :].T
    for start in range(0, length, block_cols):
        span = pl.ds(start, block_cols)
        queries = qkv_ref[span, :LANES]
        pieces = []
        for head in range(2):
            scores = nt_dot(head_keys[head], queries) + bias_ref[head, :, span].astype(
                jnp.float32
            )
            top = jnp.max(scores, axis=0, keepdims=True)
            shifted = jnp.exp(scores - top)
            total = jnp.sum(shifted, axis=0, keepdims=True)
            probs = (shifted * (1.0 / total)).astype(jnp.bfloat16)
            pieces.append(nn_dot(values_t[head * HD : (head + 1) * HD], probs))
            lse_ref[0, head : head + 1, span] = top + jnp.log(total)
        context_ref[span, :] = jnp.concatenate(pieces, axis=0).T.astype(jnp.bfloat16)


def attention_forward(qkv, bias_t):
    length = qkv.shape[0]
    pairs = qkv.shape[1] // (3 * LANES)
    heads = 2 * pairs
    return pl.pallas_call(
        functools.partial(forward_kernel, min(256, length)),
        grid=(pairs,),
        in_specs=[
            pl.BlockSpec((length, 3 * LANES), lambda p: (0, p)),
            pl.BlockSpec((2, length, length), lambda p: (p, 0, 0)),
        ],
        out_specs=[
            pl.BlockSpec((length, LANES), lambda p: (0, p)),
            pl.BlockSpec((1, 2, length), lambda p: (p, 0, 0)),
        ],
        out_shape=[
            jax.ShapeDtypeStruct((length, pairs * LANES), jnp.bfloat16),
            jax.ShapeDtypeStruct((pairs, 2, length), jnp.float32),
        ],
        compiler_params=pltpu.CompilerParams(vmem_limit_bytes=VMEM_ROOM),
        cost_estimate=pl.CostEstimate(
            flops=heads * length, bytes_accessed=heads * length, transcendentals=0
        ),
        name="attention_forward",
    )(qkv, bias_t)


def backward_kernel(
    block_cols, qkv_ref, grad_ref, bias_ref, lse_ref, out_ref, grad_scores_ref, dk_acc, dv_acc
):
    length = qkv_ref.shape[0]
    keys = qkv_ref[:, LANES : 2 * LANES]
    values = qkv_ref[:, 2 * LANES :]
    masks = head_masks(length)
    small_masks = head_masks(block_cols)
    head_keys = [only_head(keep, keys) for keep in masks]
    head_values = [only_head(keep, values) for keep in masks]
    keys_t = keys.T
    for start in range(0, length, block_cols):
        span = pl.ds(start, block_cols)
        queries = qkv_ref[span, :LANES]
        grads = grad_ref[span, :]
        pieces = []
        for head in range(2):
            scores = nt_dot(head_keys[head], queries) + bias_ref[head, :, span].astype(
                jnp.float32
            )
            probs = jnp.exp(scores - lse_ref[0, head : head + 1, span])
            grad_probs = nt_dot(head_values[head], grads)
            inner = jnp.sum(probs * grad_probs, axis=0, keepdims=True)
            grad_scores = (probs * (grad_probs - inner)).astype(jnp.bfloat16)
            grad_scores_ref[head, :, span] = grad_scores
            value_part = nn_dot(
                probs.astype(jnp.bfloat16), only_head(small_masks[head], grads)
            )
            key_part = nn_dot(grad_scores, only_head(small_masks[head], queries))
            if start == 0 and head == 0:
                dv_acc[...] = value_part
                dk_acc[...] = key_part
            else:
                dv_acc[...] += value_part
                dk_acc[...] += key_part
            pieces.append(nn_dot(keys_t[head * HD : (head + 1) * HD], grad_scores))
        out_ref[span, :LANES] = jnp.concatenate(pieces, axis=0).T.astype(jnp.bfloat16)
    out_ref[:, LANES : 2 * LANES] = dk_acc[...].astype(jnp.bfloat16)
    out_ref[:, 2 * LANES :] = dv_acc[...].astype(jnp.bfloat16)


def attention_backward(qkv, grad_context, bias_t, lse):
    length = qkv.shape[0]
    pairs = qkv.shape[1] // (3 * LANES)
    heads = 2 * pairs
    return pl.pallas_call(
        functools.partial(backward_kernel, min(256, length)),
        grid=(pairs,),
        in_specs=[
            pl.BlockSpec((length, 3 * LANES), lambda p: (0, p)),
            pl.BlockSpec((length, LANES), lambda p: (0, p)),
            pl.BlockSpec((2, length, length), lambda p: (p, 0, 0)),
            pl.BlockSpec((1, 2, length), lambda p: (p, 0, 0)),
        ],
        out_specs=[
            pl.BlockSpec((length, 3 * LANES), lambda p: (0, p)),
            pl.BlockSpec((2, length, length), lambda p: (p, 0, 0)),
        ],
        out_shape=[
            jax.ShapeDtypeStruct((length, pairs * 3 * LANES), jnp.bfloat16),
            jax.ShapeDtypeStruct((heads, length, length), jnp.bfloat16),
        ],
        scratch_shapes=[
            pltpu.VMEM((length, LANES), jnp.float32),
            pltpu.VMEM((length, LANES), jnp.float32),
        ],
        compiler_params=pltpu.CompilerParams(vmem_limit_bytes=VMEM_ROOM),
        cost_estimate=pl.CostEstimate(
            flops=heads * length, bytes_accessed=heads * length, transcendentals=0
        ),
        name="attention_backward",
    )(qkv, grad_context, bias_t, lse)


def histogram_kernel(bucket_count, group, buckets_ref, *refs):
    grads, (sums_ref, values) = refs[:-2], refs[-2:]
    heads, rows, cols = values.shape

    @pl.when(pl.program_id(0) == 0)
    def _():
        sums_ref[...] = jnp.zeros_like(sums_ref)

    total = grads[0][...].astype(jnp.float32)
    for other in grads[1:]:
        total = total + other[...].astype(jnp.float32)
    values[...] = total

    @pl.loop(0, bucket_count // group)
    def _(step):
        first = step * group
        acc = [[jnp.zeros((8, LANES), jnp.float32) for _ in range(heads)] for _ in range(group)]
        for row in range(0, rows, 8):
            for col in range(0, cols, LANES):
                ids = buckets_ref[row : row + 8, col : col + LANES]
                vals = [values[h, row : row + 8, col : col + LANES] for h in range(heads)]
                for j in range(group):
                    hit = ids == first + j
                    for h in range(heads):
                        acc[j][h] = acc[j][h] + jnp.where(hit, vals[h], 0.0)
        for j in range(group):
            for h in range(heads):
                sums_ref[h, first + j] += acc[j][h]


def bucket_sums(buckets_t, grad_scores, bucket_count):
    heads, length, _ = grad_scores[0].shape
    block = 32
    sums = pl.pallas_call(
        functools.partial(histogram_kernel, bucket_count, 4),
        grid=(length // block,),
        in_specs=[pl.BlockSpec((block, length), lambda i: (i, 0))]
        + [pl.BlockSpec((heads, block, length), lambda i: (0, i, 0))] * len(grad_scores),
        out_specs=pl.BlockSpec((heads, bucket_count, 8, LANES), lambda i: (0, 0, 0, 0)),
        out_shape=jax.ShapeDtypeStruct((heads, bucket_count, 8, LANES), jnp.float32),
        scratch_shapes=[pltpu.VMEM((heads, block, length), jnp.float32)],
        compiler_params=pltpu.CompilerParams(vmem_limit_bytes=VMEM_ROOM),
        cost_estimate=pl.CostEstimate(
            flops=heads * length, bytes_accessed=heads * length, transcendentals=0
        ),
        name="bucket_sums",
    )(buckets_t, *grad_scores)
    return jnp.sum(sums, axis=(2, 3)).T


def xor_pairs(count, mask):
    return [(i, i ^ mask) for i in range(count)]


def reorder(blocks, place):
    blocks = list(blocks)
    bit = 1
    while bit < len(blocks):
        flag = (place & bit) != 0
        blocks = [jnp.where(flag, blocks[i ^ bit], blocks[i]) for i in range(len(blocks))]
        bit *= 2
    return blocks


def rms_parts(seq_rows, gain_vec):
    inv_rms = lax.rsqrt(jnp.mean(seq_rows * seq_rows, axis=-1, keepdims=True) + norm_eps)
    plain_rows = seq_rows * inv_rms
    return (plain_rows, inv_rms, (plain_rows * gain_vec).astype(jnp.bfloat16))


def rms_back(grad_norm, plain_rows, inv_rms, gain_vec):
    scaled_grad = grad_norm * gain_vec
    return inv_rms * (
        scaled_grad - plain_rows * jnp.mean(scaled_grad * plain_rows, axis=-1, keepdims=True)
    )


def gelu_gate(gate_pre, up_pre):
    return jax.nn.gelu(gate_pre, approximate=True) * up_pre


def tn_dot(left, right):
    return lax.dot_general(
        left, right, (((0,), (0,)), ((), ())), preferred_element_type=jnp.float32
    )


def after(x, *needed):
    return lax.optimization_barrier((x, *needed))[0]


def make_body(dp_size, tensor_size):
    zs = tensor_size // 2
    z_groups = [[2 * z + core for z in range(zs)] for core in range(2)]
    core_pairs = xor_pairs(tensor_size, 1)

    def to_core(x):
        return lax.ppermute(x, "tensor", core_pairs)

    def to_dp(x, mask):
        return lax.ppermute(x, "dp", xor_pairs(dp_size, mask))

    def to_z(x, mask):
        return lax.ppermute(x, "tensor", xor_pairs(tensor_size, 2 * mask))

    def dp_relative(x):
        return [x] + [to_dp(x, k) for k in range(1, dp_size)]

    def exchange(send, pick, size):
        return [pick(0)] + [send(pick(k), k) for k in range(1, size)]

    def total_of(send, pick, size):
        own = pick(0).astype(jnp.float32)
        for k in range(1, size):
            own = own + send(pick(k).astype(jnp.bfloat16), k).astype(jnp.float32)
        return own

    def z_gather(x):
        return lax.all_gather(x, "tensor", axis=0, tiled=True, axis_index_groups=z_groups)

    def z_scatter(x):
        return lax.psum_scatter(
            x, "tensor", scatter_dimension=0, tiled=True, axis_index_groups=z_groups
        )

    def all_sum(x, dp_at, z_at, core_at):
        x = sum(reorder([x, to_core(x)], core_at))
        x = sum(reorder(exchange(to_z, lambda k: x, zs), z_at))
        return sum(reorder(dp_relative(x), dp_at))

    def body(
        hidden_in,
        out_grad,
        buckets,
        gain_attn,
        gain_ffn,
        w_query,
        w_key,
        w_value,
        w_out,
        w_gate,
        w_up,
        w_down,
        bias_table,
    ):
        dp_at = lax.axis_index("dp")
        tensor_at = lax.axis_index("tensor")
        core_at = tensor_at % 2
        z_at = tensor_at // 2
        seqs, rows, width = hidden_in.shape
        length = buckets.shape[0]
        feats = w_query.shape[0]
        inner = w_query.shape[1]
        heads = inner // HD
        pairs = inner // LANES
        ff = w_gate.shape[1]
        part = ff // dp_size
        table_rows = bias_table.shape[0]
        bucket_count = table_rows * dp_size
        gain_one = gain_attn.astype(jnp.float32)
        gain_two = gain_ffn.astype(jnp.float32)
        every = range(seqs)

        def feature_block(x, k):
            return lax.dynamic_slice_in_dim(x, (dp_at ^ k) * feats, feats, 1)

        x_rows = [hidden_in[s].astype(jnp.float32) for s in every]
        first_norm = [rms_parts(x, gain_one) for x in x_rows]
        norm_full = [
            lax.all_gather(first_norm[s][2], "tensor", axis=0, tiled=True) for s in every
        ]

        qkv_local = jnp.concatenate(
            [
                w[:, p * LANES : (p + 1) * LANES]
                for p in range(pairs)
                for w in (w_query, w_key, w_value)
            ],
            axis=1,
        )
        table = jnp.concatenate(reorder(dp_relative(bias_table), dp_at), axis=0)
        buckets_t = buckets.T
        bias_t = expand_bias(
            buckets_t,
            jnp.pad(table.astype(jnp.float32).T, ((0, 0), (0, LANES - bucket_count))),
        )
        payload = dp_relative(after(qkv_local, table))
        arrived = payload[1:]
        payload = after(tuple(payload), bias_t)
        w_qkv = jnp.concatenate(reorder(payload, dp_at), axis=0)

        out_z = tuple(exchange(to_z, lambda k: w_out, zs))
        first_qkv = nn_dot(after(norm_full[0], *out_z[1:]), w_qkv).astype(jnp.bfloat16)

        ffn_local = jnp.stack([w_gate.T, w_up.T, w_down]).reshape(3, dp_size, part, feats)
        ffn_local = after(ffn_local, *arrived)
        ffn_parts = exchange(
            to_dp,
            lambda k: lax.dynamic_index_in_dim(ffn_local, dp_at ^ k, 1, keepdims=False),
            dp_size,
        )
        arrived = ffn_parts[1:]
        ffn_parts = reorder(after(tuple(ffn_parts), first_qkv), dp_at)
        pre_rows = jnp.concatenate([p[:2] for p in ffn_parts], axis=2)
        post_rows = jnp.concatenate([p[2] for p in ffn_parts], axis=1)
        pre_rows = pre_rows.reshape(2 * part, width)
        pre_gathered = z_gather(pre_rows)

        out_rows = after(jnp.concatenate(reorder(out_z, z_at), axis=0), *arrived)

        def both_cores(blocks):
            own = jnp.concatenate(blocks, axis=0)
            return jnp.concatenate([own, to_core(own)], axis=0)

        def context_to_tokens(context):
            blocks = context.reshape(zs, 2, rows, inner)
            own = lax.dynamic_index_in_dim(blocks, core_at, 1, keepdims=False)
            got = to_core(lax.dynamic_index_in_dim(blocks, 1 - core_at, 1, keepdims=False))
            both = jnp.concatenate([own, got], axis=-1)
            swapped = got
            moved = exchange(
                to_z,
                lambda k: lax.dynamic_index_in_dim(both, z_at ^ k, 0, keepdims=False),
                zs,
            )
            moved = reorder(moved, z_at)
            return (
                jnp.concatenate([m[:, :inner] for m in moved], axis=1),
                jnp.concatenate([m[:, inner:] for m in moved], axis=1),
                swapped,
            )

        def send_tokens(own, other):
            got = to_core(other)
            pair = jnp.stack(reorder([own, got], core_at))
            moved = exchange(
                to_z,
                lambda k: lax.dynamic_slice_in_dim(pair, (z_at ^ k) * inner, inner, 2),
                zs,
            )
            return tuple(moved), got

        def take_tokens(moved):
            return jnp.stack(reorder(moved, z_at)).reshape(length, inner)

        qkv_all, lse_all, ctx_own, ctx_other, swaps = [], [], [], [], []
        mid_rows, second_norm, norm_two_full = [], [], []

        recent = []
        cot_full = []

        def feed_forward_input(s):
            own, other = ctx_own[s], ctx_other[s]
            if s == 1:
                own = after(own, *recent[-1])
            mid = x_rows[s] + (nn_dot(own, out_own) + nn_dot(other, out_other))
            mid_rows.append(mid)
            second_norm.append(rms_parts(mid, gain_two))
            normed = second_norm[s][2]
            normed = after(normed, *recent[-1])
            riders = [out_grad[t] for t in every if 1 <= s == t - 1]
            parts = dp_relative(jnp.concatenate([normed, *riders], axis=0))
            recent.append(parts[1:])
            norm_two_full.append(both_cores([x[:rows] for x in parts]))
            for i in range(1, len(riders) + 1):
                cot_full.append(both_cores([x[i * rows : (i + 1) * rows] for x in parts]))

        for s in every:
            if s == 0:
                qkv = first_qkv
            else:
                source = after(norm_full[s], swaps[s - 1])
                if s > 1:
                    source = after(source, second_norm[s - 2][2])
                if s == 1:
                    source = after(source, pre_rows)
                qkv = nn_dot(source, w_qkv).astype(jnp.bfloat16)
            context, lse = attention_forward(qkv, bias_t)
            if s == 0:
                post_gathered = z_gather(after(post_rows, context))
                out_parts = dp_relative(out_rows)
                early = dp_relative(
                    after(jnp.concatenate([out_grad[0], out_grad[1]], axis=0), context, *out_parts[1:])
                )
                recent.append(early[1:])
            if s == 1:
                out_parts = after(tuple(out_parts), context)
                out_own = jnp.concatenate(reorder(out_parts, dp_at), axis=1)
                out_other = to_core(out_own)
            if s == 1:
                taken = after(tuple(early), context)
                cot_full.append(both_cores([x[:rows] for x in taken]))
                cot_full.append(both_cores([x[rows:] for x in taken]))
            if s > 0:
                feed_forward_input(s - 1)
                context = after(context, second_norm[s - 1][2])
            own, other, swapped = context_to_tokens(context)
            qkv_all.append(qkv)
            lse_all.append(lse)
            ctx_own.append(own)
            ctx_other.append(other)
            swaps.append(swapped)
        feed_forward_input(seqs - 1)
        pre_gathered = after(pre_gathered, norm_two_full[-1])
        w_pre = jnp.transpose(
            pre_gathered.reshape(zs, 2, part, width), (1, 0, 2, 3)
        ).reshape(2 * ff, width)
        half = dp_size * rows
        first_parts, hidden_all = [], []
        grad_post = None
        for s in every:
            pre = nt_dot(norm_two_full[s], w_pre)
            hidden = gelu_gate(pre[:, :ff], pre[:, ff:]).astype(jnp.bfloat16)
            first_parts.append(pre)
            hidden_all.append(hidden)
            more = tn_dot(hidden, cot_full[s])
            grad_post = more if grad_post is None else grad_post + more
        grad_post = grad_post.astype(jnp.bfloat16)
        w_post = after(post_gathered, grad_post)
        post_z = z_scatter(grad_post)
        pre_all, kept, sums, swaps_in, sent_in = [], [], [], [], []
        ready = grad_post
        for s in every:
            pre = first_parts[s]
            _, pull = jax.vjp(gelu_gate, pre[:, :ff], pre[:, ff:])
            cot = after(cot_full[s], ready)
            if s > 1:
                cot = after(cot, *sums[s - 2])
            grad_gate, grad_up = pull(nt_dot(cot, w_post))
            grad_pre = jnp.concatenate([grad_gate, grad_up], axis=1).astype(jnp.bfloat16)
            ready = nn_dot(grad_pre, w_pre)
            got = to_core(ready[half:].astype(jnp.bfloat16))
            own = ready[:half] + got.astype(jnp.float32)
            blocks = [
                own[k * rows : (k + 1) * rows].astype(jnp.bfloat16) for k in range(1, dp_size)
            ]
            sent = [to_dp(blocks[k - 1], k) for k in range(1, dp_size)]
            kept.append(own[:rows])
            sums.append(blocks)
            swaps_in.append(got)
            sent_in.append(sent)
            pre_all.append(grad_pre)
        grad_mid, grad_mid_low, gain_two_sum = [], [], None
        moves, swapped_in, received = [], [], []
        grad_pre_w = None
        for s in every:
            grad_pre = after(pre_all[s], ready)
            if s == 0:
                grad_pre = after(grad_pre, *sums[1])
            else:
                grad_pre = after(grad_pre, swapped_in[s - 1], *sums[-1])
            if s == seqs - 1:
                grad_pre = after(grad_pre, post_z, *moves[0][1:])
            more = tn_dot(grad_pre, norm_two_full[s])
            grad_pre_w = more if grad_pre_w is None else grad_pre_w + more
            if s == seqs - 1:
                grad_pre_w = grad_pre_w.astype(jnp.bfloat16)
                more = grad_pre_w
            sent = after(tuple(sent_in[s]), more)
            received.append(sent)
            grad_norm = kept[s] + sum(x.astype(jnp.float32) for x in sent)
            plain, inv, _ = second_norm[s]
            more = jnp.sum(grad_norm * plain, axis=0)
            gain_two_sum = more if gain_two_sum is None else gain_two_sum + more
            grad = out_grad[s].astype(jnp.float32) + rms_back(grad_norm, plain, inv, gain_two)
            grad_mid.append(grad)
            grad_mid_low.append(grad.astype(jnp.bfloat16))
            back_own = nt_dot(grad_mid_low[s], out_own).astype(jnp.bfloat16)
            back_other = nt_dot(grad_mid_low[s], out_other).astype(jnp.bfloat16)
            moved, got = send_tokens(back_own, back_other)
            moves.append(moved)
            swapped_in.append(got)
        pre_z = z_scatter(
            jnp.transpose(
                grad_pre_w.reshape(2, zs, part, width), (1, 0, 2, 3)
            ).reshape(zs * 2 * part, width)
        )

        hidden_own = jnp.concatenate([h[:half] for h in hidden_all], axis=0)
        hidden_other = jnp.concatenate([h[half:] for h in hidden_all], axis=0)
        hidden_own, hidden_other = (
            after(hidden_own, grad_pre_w),
            after(hidden_other, grad_pre_w),
        )
        sent = to_core(nn_dot(hidden_other, w_post).astype(jnp.bfloat16))
        own = nn_dot(after(hidden_own, *sent_in[-1]), w_post) + sent.astype(jnp.float32)
        own = own.reshape(seqs, dp_size, rows, width)
        out_blocks = [own[:, k].astype(jnp.bfloat16) for k in range(1, dp_size)]
        out_sent = [to_dp(out_blocks[k - 1], k) for k in range(1, dp_size)]
        ffn_own = own[:, 0]

        def ffn_send(z_rows):
            return tuple(exchange(to_dp, lambda k: feature_block(z_rows, k), dp_size))

        def ffn_take(moved, mats):
            moved = jnp.stack(reorder(moved, dp_at)).reshape(dp_size, mats, part, feats)
            return [moved[:, m].reshape(ff, feats).astype(jnp.float32) for m in range(mats)]

        post_moved = ffn_send(post_z)
        pre_moved = ffn_send(pre_z)
        grad_normed, grad_scores, normed_parts, qkv_grads = [], [], [], []
        grad_qkv = None
        gate = (grad_pre_w,)
        for s in every:
            moved = after(moves[s], *gate)
            if s < seqs - 1:
                moved = after(moved, swapped_in[s + 1])
            if s == 1:
                moved = after(moved, *out_blocks)
            if s == seqs - 1:
                moved = after(moved, *post_moved[1:], *out_give_dp)
            grad_proj, grad_score = attention_backward(
                qkv_all[s], take_tokens(moved), bias_t, lse_all[s]
            )
            grad_scores.append(grad_score)
            qkv_grads.append(grad_proj)
            ordered = grad_proj
            if s == 0:
                ordered = after(ordered, *sent_in[-1])
            if s == 1:
                ordered = after(ordered, *out_sent)
            if s == seqs - 1:
                ordered = after(ordered, *out_moved[1:])
            normed_part = nt_dot(ordered, w_qkv).astype(jnp.bfloat16)
            normed_parts.append(normed_part)
            gate = (normed_part,)
            grad_normed.append(
                lax.psum_scatter(
                    normed_part, "tensor", scatter_dimension=0, tiled=True
                ).astype(jnp.float32)
            )
            if s == 0:
                mid_low = after(jnp.concatenate(grad_mid_low, axis=0), normed_part)
                out_give = tn_dot(jnp.concatenate(ctx_other, axis=0), mid_low).astype(
                    jnp.bfloat16
                )
                out_got = to_core(out_give)
                out_keep = tn_dot(jnp.concatenate(ctx_own, axis=0), mid_low)
                gate = gate + (out_give, out_keep)
            else:
                for t in [0, 1] if s == 1 else [s]:
                    more = tn_dot(norm_full[t], after(qkv_grads[t], normed_part))
                    grad_qkv = more if grad_qkv is None else grad_qkv + more
                gate = gate + (grad_qkv,)
            if s == 1:
                out_sum = out_keep + after(out_got, normed_part).astype(jnp.float32)
                out_give_dp = [
                    feature_block(out_sum, k).astype(jnp.bfloat16) for k in range(1, dp_size)
                ]
                out_moved = (
                    feature_block(out_sum, 0),
                    *[to_dp(out_give_dp[k - 1], k) for k in range(1, dp_size)],
                )
        out_moved = after(out_moved, normed_parts[-1])
        grad_out_z = sum(m.astype(jnp.float32) for m in out_moved)
        grad_out_keep = lax.dynamic_slice_in_dim(grad_out_z, z_at * inner, inner, 0)
        grad_out_blocks = [
            lax.dynamic_slice_in_dim(grad_out_z, (z_at ^ k) * inner, inner, 0).astype(
                jnp.bfloat16
            )
            for k in range(1, zs)
        ]
        grad_out_sent = [to_z(grad_out_blocks[k - 1], k) for k in range(1, zs)]
        qkv_blocks = [
            lax.dynamic_slice_in_dim(grad_qkv, (dp_at ^ k) * feats, feats, 0).astype(
                jnp.bfloat16
            )
            for k in range(1, dp_size)
        ]
        qkv_sent = [to_dp(qkv_blocks[k - 1], k) for k in range(1, dp_size)]
        bucket_gate = after(
            buckets_t, *pre_moved[1:], *grad_out_blocks, *qkv_blocks, grad_normed[0]
        )
        table_grad = bucket_sums(bucket_gate, grad_scores, bucket_count)
        grad_out = grad_out_keep + sum(
            x.astype(jnp.float32) for x in after(tuple(grad_out_sent), table_grad)
        )
        summed = lax.dynamic_slice_in_dim(grad_qkv, dp_at * feats, feats, 0) + sum(
            x.astype(jnp.float32) for x in after(tuple(qkv_sent), table_grad)
        )
        ffn_out = ffn_own + sum(
            m.astype(jnp.float32) for m in after(tuple(out_sent), normed_parts[-1])
        )
        output = jnp.stack(
            [(mid_rows[s] + ffn_out[s]).astype(jnp.bfloat16) for s in every]
        )

        (grad_down,) = ffn_take(post_moved, 1)
        grad_gate_t, grad_up_t = ffn_take(pre_moved, 2)

        def columns(which):
            return jnp.concatenate(
                [
                    summed[:, (3 * p + which) * LANES : (3 * p + which + 1) * LANES]
                    for p in range(pairs)
                ],
                axis=1,
            )

        grad_table = total_of(
            to_dp,
            lambda k: lax.dynamic_slice_in_dim(
                table_grad, (dp_at ^ k) * table_rows, table_rows, 0
            ),
            dp_size,
        )

        grad_in, gain_one_sum = [], None
        for s in every:
            plain, inv, _ = first_norm[s]
            more = jnp.sum(grad_normed[s] * plain, axis=0)
            gain_one_sum = more if gain_one_sum is None else gain_one_sum + more
            grad_in.append(
                (grad_mid[s] + rms_back(grad_normed[s], plain, inv, gain_one)).astype(
                    jnp.bfloat16
                )
            )
        gains = all_sum(jnp.stack([gain_one_sum, gain_two_sum]), dp_at, z_at, core_at)
        return (
            output,
            jnp.stack(grad_in),
            gains[0],
            gains[1],
            columns(0),
            columns(1),
            columns(2),
            grad_out,
            grad_gate_t.T,
            grad_up_t.T,
            grad_down,
            grad_table,
        )

    return body


def solution(mesh):
    in_specs = (
        P("dp", "tensor", None),
        P("dp", "tensor", None),
        P(),
        P(),
        P(),
        P("dp", "tensor"),
        P("dp", "tensor"),
        P("dp", "tensor"),
        P("tensor", "dp"),
        P("dp", "tensor"),
        P("dp", "tensor"),
        P("tensor", "dp"),
        P("dp", "tensor"),
    )
    out_specs = (
        P("dp", "tensor", None),
        P("dp", "tensor", None),
        P(),
        P(),
        P("dp", "tensor"),
        P("dp", "tensor"),
        P("dp", "tensor"),
        P("tensor", "dp"),
        P("dp", "tensor"),
        P("dp", "tensor"),
        P("tensor", "dp"),
        P("dp", "tensor"),
    )
    body = make_body(mesh.shape["dp"], mesh.shape["tensor"])
    return jax.shard_map(body, mesh=mesh, in_specs=in_specs, out_specs=out_specs, check_vma=False)
```
